32 devices in a mesh: tx: 2 (over y), ty: 4 (over z), lev: 4 (over x, core).
Axes of the slice: x: 2, y: 2, z: 4, core: 2. Of those that a mesh axis runs over, the one named last changes fastest.
Arguments:
- members: bfloat16 [8, 128, 64, 128], P('lev', 'tx', 'ty'), may hold values from -6 to 6
- obs_pert: bfloat16 [8192, 128], P(('tx', 'ty', 'lev')), may hold values from -6 to 6
- innovation: bfloat16 [8192], P(('tx', 'ty', 'lev')), may hold values from -6 to 6
- obs_precision: bfloat16 [8192], P(('tx', 'ty', 'lev')), may hold values from 0.25 to 4
- obs_owner: int32 [8, 4, 256], P('tx', 'ty'), may hold values from 0 to 7, as said below
- obs_slot: int32 [8, 4, 256], P('tx', 'ty'), may hold values from 0 to 1023
- obs_count: int32 [8, 4], P('tx', 'ty'), may hold values from 64 to 256
- local_weight: float32 [8, 4, 256], P('tx', 'ty'), may hold values from 0.05 to 1
Outputs:
- analysis: bfloat16 [8, 128, 64, 128], P('lev', 'tx', 'ty')
The draws below stay inside these ranges and needn't reach their ends.
Inputs may be any that keep to these rules, and one draw needn't show every extreme that they name: `obs_owner`: the tile numbered tx index times the number of ty tiles plus ty index; it is the coarse column's own tile or one of the tiles beside it, diagonals included. `obs_count`: slots at and beyond a coarse column's count are padding.
All inputs are finite; a program needn't handle non-finite values.
Results may differ from the reference program's by a relative error of at most 0.0054.
Values may be sent and summed in bfloat16 or wider, within the bound.
No kernel may reach another device: no remote copies, remote signals or barrier semaphores. Data moves between devices by JAX's collectives and lax.ppermute only.
A program may use at most 64 MiB of HBM per device.

```python
import math
import jax
import jax.numpy as jnp
from jax import lax

K = 128
L = 256
SPACING = 16
NS_STEPS = 4
CX = 64
CY = 16
NX = 128
NY = 64
LEVELS = 8
NCX = 8
NCY = 4
OBS_TILE = 1024
NOBS = 8192


def draw_obs_owner(key, part):
    key_x, key_y = jax.random.split(jax.random.fold_in(key, 11))
    grid_shape = (NCX, NCY, L)
    step_x = jax.random.randint(key_x, grid_shape, -1, 2)
    step_y = jax.random.randint(key_y, grid_shape, -1, 2)
    tiles_x = NX // CX
    tiles_y = NY // CY
    home_x = (jnp.arange(NCX) // (CX // SPACING))[:, None, None]
    home_y = (jnp.arange(NCY) // (CY // SPACING))[None, :, None]
    owner_x = jnp.clip(home_x + step_x, 0, tiles_x - 1)
    owner_y = jnp.clip(home_y + step_y, 0, tiles_y - 1)
    return (owner_x * tiles_y + owner_y).astype(jnp.int32)


def with_ends(result, stream_key, smallest, high):
    spot = [jax.random.randint(jax.random.fold_in(stream_key, axis), (), 0, length) for axis, length in enumerate(result.shape)]
    longest = result.shape.index(max(result.shape))
    beside = spot[:longest] + [(spot[longest] + 1) % result.shape[longest]] + spot[longest + 1:]
    return result.at[tuple(spot)].set(smallest).at[tuple(beside)].set(high)


def shard_levels(own_key, dims, cuts, least, top_value):
    def one(position, parts):
        steps = jax.random.uniform(jax.random.fold_in(jax.random.fold_in(own_key, 6), position), (parts,), jnp.float32, least / len(cuts), top_value / len(cuts))
        return jnp.repeat(jnp.exp(steps), dims[position] // parts).reshape((-1,) + (1,) * (len(dims) - position - 1))

    factor_of = one(*cuts[0])
    for cut in cuts[1:]:
        factor_of = factor_of * one(*cut)
    return factor_of


def centred(stream_key, extent, scale, most, shards=(), kind=jnp.bfloat16):
    result = jax.random.normal(stream_key, extent, jnp.float32) * scale
    if len(shards) > 0:
        result = shard_levels(stream_key, extent, shards, -0.22, 0.18) * result
    return jnp.clip(result, min=-most, max=most).astype(kind)


def setup_inputs(seed: int = 0) -> dict:
    keys = jax.random.split(jax.random.key(seed), 9)
    return {
        "members": centred(keys[0], (LEVELS, NX, NY, K), 1.0, 6.0, ((0, 4), (1, 2), (2, 4))),
        "obs_pert": centred(keys[1], (NOBS, K), 1.0, 6.0, ((0, 32),)),
        "innovation": centred(keys[2], (NOBS,), 1.0, 6.0, ((0, 32),)),
        "obs_precision": jnp.clip(jnp.exp(math.log(4.0) - 2.7725887 * jax.random.uniform(keys[3], (NOBS,), jnp.float32) ** shard_levels(keys[3], (NOBS,), ((0, 32),), -0.2, 0.2)), 0.25, 4.0).astype(jnp.bfloat16),
        "obs_owner": draw_obs_owner(jax.random.fold_in(keys[8], 71), 0),
        "obs_slot": with_ends(jax.random.randint(keys[5], (NCX, NCY, L), 0, OBS_TILE), jax.random.fold_in(keys[5], 1), 0, OBS_TILE - 1).astype(jnp.int32),
        "obs_count": with_ends(jax.random.randint(keys[6], (NCX, NCY), L // 4, L + 1), jax.random.fold_in(keys[6], 1), L // 4, L).astype(jnp.int32),
        "local_weight": jnp.clip(0.05 + 0.95 * jax.random.uniform(keys[7], (NCX, NCY, L), jnp.float32) ** shard_levels(keys[7], (NCX, NCY, L), ((0, 2), (1, 4)), -0.2, 0.2), 0.05, 1.0),
    }


def finish_solve(gram_matrix, projected):
    member_count = gram_matrix.shape[1]
    spread = float(member_count - 1)
    identity = jnp.eye(member_count, dtype=jnp.float32)
    scale_norm = spread + jnp.sqrt(lax.optimization_barrier(jnp.sum(gram_matrix * gram_matrix, axis=(1, 2))))
    sqrt_iter = (spread * identity + gram_matrix) / scale_norm[:, None, None]
    inv_iter = jnp.broadcast_to(identity, sqrt_iter.shape)
    for iteration in range(NS_STEPS):
        middle = 1.5 * identity - 0.5 * jnp.einsum('bij,bjk->bik', inv_iter, sqrt_iter, precision=lax.Precision.HIGHEST)
        sqrt_iter = jnp.einsum('bij,bjk->bik', sqrt_iter, middle, precision=lax.Precision.HIGHEST)
        inv_iter = jnp.einsum('bij,bjk->bik', middle, inv_iter, precision=lax.Precision.HIGHEST)
    inner = jnp.einsum('bij,bj->bi', inv_iter, projected, precision=lax.Precision.HIGHEST)
    mean_weights = jnp.einsum('bij,bj->bi', inv_iter, inner, precision=lax.Precision.HIGHEST) / scale_norm[:, None]
    transform = (jnp.sqrt(spread) / jnp.sqrt(scale_norm))[:, None, None] * inv_iter + mean_weights[:, :, None]
    return transform.astype(jnp.bfloat16)

def fractions(count, half_span):
    place = jnp.arange(count)[:, None]
    within = jnp.arange(half_span)[None, :].astype(jnp.float32)
    return jnp.where(place % 2 == 0, (within + half_span + 0.5) / (2 * half_span), (within + 0.5) / (2 * half_span))

def reference(members, obs_pert, innovation, obs_precision, obs_owner, obs_slot, obs_count, local_weight):
    member_count = members.shape[3]
    slots = obs_owner.shape[2]
    lookup = obs_owner * OBS_TILE + obs_slot
    active = jnp.arange(slots)[None, None, :] < obs_count[:, :, None]

    def solve_strip(strip):
        strip_rows, strip_active, strip_local = strip
        pert_rows = obs_pert[strip_rows].astype(jnp.float32)
        precision_w = jnp.where(strip_active, obs_precision[strip_rows].astype(jnp.float32) * strip_local, 0.0)
        departure = innovation[strip_rows].astype(jnp.float32)
        gram_matrix = jnp.einsum('bsk,bsm->bkm', pert_rows * precision_w[:, :, None], pert_rows, precision=lax.Precision.HIGHEST)
        projected = jnp.einsum('bsk,bs->bk', pert_rows, precision_w * departure, precision=lax.Precision.HIGHEST)
        return finish_solve(gram_matrix, projected)
    weights = lax.map(solve_strip, (lookup, active, local_weight))
    padded = jnp.pad(weights, ((1, 1), (1, 1), (0, 0), (0, 0)), mode='edge')
    doubled = jnp.repeat(jnp.repeat(padded, 2, axis=0), 2, axis=1)
    half_span = SPACING // 2
    patch_x = NX // half_span
    patch_y = NY // half_span
    frac_x = fractions(patch_x, half_span)
    frac_y = fractions(patch_y, half_span)

    def one_level(level_states):
        states = level_states.astype(jnp.float32)
        ens_mean = lax.optimization_barrier(jnp.mean(states, axis=2, keepdims=True))
        pert = (states - ens_mean).astype(jnp.bfloat16)
        patched = pert.astype(jnp.float32).reshape(patch_x, half_span, patch_y, half_span, member_count)
        summed = jnp.zeros(patched.shape, jnp.float32)
        for upper_x in range(2):
            for upper_y in range(2):
                corner = doubled[1 + 2 * upper_x:1 + 2 * upper_x + patch_x, 1 + 2 * upper_y:1 + 2 * upper_y + patch_y].astype(jnp.float32)
                product = jnp.einsum('xaybi,xyij->xaybj', patched, corner)
                factor_x = frac_x if upper_x == 1 else 1.0 - frac_x
                factor_y = frac_y if upper_y == 1 else 1.0 - frac_y
                summed = summed + product * factor_x[:, :, None, None, None] * factor_y[None, None, :, :, None]
        return (ens_mean + summed.reshape(states.shape)).astype(jnp.bfloat16)
    return lax.map(one_level, members)
```

```python
import functools

import jax
import jax.numpy as jnp
from jax import lax
from jax.experimental import pallas as pl
from jax.experimental.pallas import tpu as pltpu
from jax.sharding import PartitionSpec as P

SPACING = 16
NS_STEPS = 4


def padded(array, sides, width):
    for axis, dim in sides:
        size, length = (lax.axis_size(axis), array.shape[dim])
        up = [(i, (i + 1) % size) for i in range(size - 1)]
        down = [(j, i) for i, j in up]
        last = lax.slice_in_dim(array, length - width, length, axis=dim)
        initial = lax.slice_in_dim(array, 0, width, axis=dim)
        before = lax.ppermute(last, axis, up)
        after = lax.ppermute(initial, axis, down)
        array = jnp.concatenate([before, array, after], axis=dim)
    return array


def finish_solve(gram_matrix, projected):
    member_count = gram_matrix.shape[1]
    spread = float(member_count - 1)
    identity = jnp.eye(member_count, dtype=jnp.float32)
    scale_norm = spread + jnp.sqrt(jnp.sum(gram_matrix * gram_matrix, axis=(1, 2)))
    sqrt_iter = (spread * identity + gram_matrix) / scale_norm[:, None, None]
    inv_iter = jnp.broadcast_to(identity, sqrt_iter.shape)
    for iteration in range(NS_STEPS):
        middle = 1.5 * identity - 0.5 * jnp.einsum(
            "bij,bjk->bik", inv_iter, sqrt_iter, precision=lax.Precision.HIGHEST
        )
        sqrt_iter = jnp.einsum("bij,bjk->bik", sqrt_iter, middle, precision=lax.Precision.HIGHEST)
        inv_iter = jnp.einsum("bij,bjk->bik", middle, inv_iter, precision=lax.Precision.HIGHEST)
    inner = jnp.einsum("bij,bj->bi", inv_iter, projected, precision=lax.Precision.HIGHEST)
    mean_weights = (
        jnp.einsum("bij,bj->bi", inv_iter, inner, precision=lax.Precision.HIGHEST)
        / scale_norm[:, None]
    )
    transform = (jnp.sqrt(spread) / jnp.sqrt(scale_norm))[:, None, None] * inv_iter + mean_weights[
        :, :, None
    ]
    return transform.astype(jnp.bfloat16)


def fractions(count, half_span):
    place = jnp.arange(count)[:, None]
    within = jnp.arange(half_span)[None, :].astype(jnp.float32)
    return jnp.where(
        place % 2 == 0,
        (within + half_span + 0.5) / (2 * half_span),
        (within + 0.5) / (2 * half_span),
    )


def solve_columns(lookup, counts, local_part, flat_pert, flat_values):
    column_count, slots = lookup.shape
    member_count = flat_pert.shape[1]
    block_len = min(slots, 128)
    live_blocks = (jnp.max(counts) + block_len - 1) // block_len

    def add_block(block_index, carry):
        gram_matrix, projected = carry
        offset = block_index * block_len
        slot_rows = lax.dynamic_slice_in_dim(lookup, offset, block_len, 1)
        slot_local = lax.dynamic_slice_in_dim(local_part, offset, block_len, 1)
        position = offset + jnp.arange(block_len)
        active = position[None, :] < counts[:, None]
        pert_rows = flat_pert[slot_rows].astype(jnp.float32)
        picked = flat_values[:, slot_rows]
        precision_w = jnp.where(active, picked[1].astype(jnp.float32) * slot_local, 0.0)
        departure = picked[0].astype(jnp.float32)
        gram_matrix = gram_matrix + jnp.einsum(
            "bsk,bsm->bkm",
            pert_rows * precision_w[:, :, None],
            pert_rows,
            precision=lax.Precision.HIGHEST,
        )
        projected = projected + jnp.einsum(
            "bsk,bs->bk", pert_rows, precision_w * departure, precision=lax.Precision.HIGHEST
        )
        return (gram_matrix, projected)

    start_gram = jnp.zeros((column_count, member_count, member_count), jnp.float32)
    start_proj = jnp.zeros((column_count, member_count), jnp.float32)
    gram_matrix, projected = lax.fori_loop(0, live_blocks, add_block, (start_gram, start_proj))
    return finish_solve(gram_matrix, projected)


def clamp_edges(rimmed, axis_index, axis_count, dim):
    lower = jnp.where(
        axis_index == 0,
        lax.slice_in_dim(rimmed, 1, 2, axis=dim),
        lax.slice_in_dim(rimmed, 0, 1, axis=dim),
    )
    last = rimmed.shape[dim]
    upper = jnp.where(
        axis_index == axis_count - 1,
        lax.slice_in_dim(rimmed, last - 2, last - 1, axis=dim),
        lax.slice_in_dim(rimmed, last - 1, last, axis=dim),
    )
    return jnp.concatenate(
        [lower, lax.slice_in_dim(rimmed, 1, last - 1, axis=dim), upper], axis=dim
    )


def per_device(
    members, obs_pert, innovation, obs_precision, obs_owner, obs_slot, obs_count, local_weight
):
    scalars = jnp.stack([innovation, obs_precision])
    tile_pert, tile_values = (
        lax.all_gather(obs_pert, "lev", axis=0, tiled=True),
        lax.all_gather(scalars, "lev", axis=1, tiled=True),
    )
    near_pert, near_values = (
        padded(tile_pert[None, None], (("tx", 0), ("ty", 1)), 1),
        padded(tile_values[None, None], (("tx", 0), ("ty", 1)), 1),
    )
    tile_len = near_pert.shape[2]
    member_count = near_pert.shape[3]
    flat_pert = near_pert.reshape(9 * tile_len, member_count)
    flat_values = jnp.transpose(near_values, (2, 0, 1, 3)).reshape(2, 9 * tile_len)
    column_x = lax.axis_index("tx")
    column_y = lax.axis_index("ty")
    tiles_x = lax.axis_size("tx")
    tiles_y = lax.axis_size("ty")
    near_x = obs_owner // tiles_y - column_x + 1
    near_y = obs_owner % tiles_y - column_y + 1
    lookup = (near_x * 3 + near_y) * tile_len + obs_slot
    coarse_x, coarse_y, slots = lookup.shape
    lookup = lookup.reshape(coarse_x * coarse_y, slots)
    counts = obs_count.reshape(coarse_x * coarse_y)
    local_part = local_weight.reshape(coarse_x * coarse_y, slots)
    weights = solve_columns(lookup, counts, local_part, flat_pert, flat_values)
    weights = weights.reshape(coarse_x, coarse_y, member_count, member_count)
    rimmed = padded(weights, (("tx", 0), ("ty", 1)), 1)
    rimmed = clamp_edges(rimmed, column_x, tiles_x, 0)
    rimmed = clamp_edges(rimmed, column_y, tiles_y, 1)
    doubled = jnp.repeat(jnp.repeat(rimmed, 2, axis=0), 2, axis=1)
    level_count, width_x, width_y, _ = members.shape
    half_span = SPACING // 2
    patch_x = width_x // half_span
    patch_y = width_y // half_span
    frac_x = fractions(patch_x, half_span)
    frac_y = fractions(patch_y, half_span)
    ens_mean = jnp.mean(members, axis=3, keepdims=True, dtype=jnp.float32)
    pert = (members.astype(jnp.float32) - ens_mean).astype(jnp.bfloat16)
    patched = pert.reshape(level_count, patch_x, half_span, patch_y, half_span, member_count)
    summed = jnp.zeros(patched.shape, jnp.float32)
    for upper_x in range(2):
        for upper_y in range(2):
            corner = doubled[
                1 + 2 * upper_x : 1 + 2 * upper_x + patch_x,
                1 + 2 * upper_y : 1 + 2 * upper_y + patch_y,
            ]
            product = jnp.einsum(
                "lxaybi,xyij->lxaybj", patched, corner, preferred_element_type=jnp.float32
            )
            factor_x = frac_x if upper_x == 1 else 1.0 - frac_x
            factor_y = frac_y if upper_y == 1 else 1.0 - frac_y
            summed = (
                summed
                + product
                * factor_x[None, :, :, None, None, None]
                * factor_y[None, None, None, :, :, None]
            )
    return (ens_mean + summed.reshape(members.shape)).astype(jnp.bfloat16)


def pair_patterns(mesh_axes):
    tiles_x, tiles_y, parts = (lax.axis_size(a) for a in mesh_axes)

    def flat(x, y, l):
        return (x * tiles_y + y) * parts + l

    def table(move):
        return [
            (flat(x, y, l), flat(*move(x, y, l)))
            for x in range(tiles_x)
            for y in range(tiles_y)
            for l in range(parts)
        ]

    def climb(x, y, l):
        if l % 2 == 0:
            return (x, y + 1, l) if y < tiles_y - 1 else (x, y, l + 1)
        return (x, y - 1, l) if y > 0 else (x, y, l - 1)

    climbing = table(climb)
    return {
        "across": table(lambda x, y, l: (1 - x, y, l)),
        "core": table(lambda x, y, l: (x, y, l ^ 1)),
        "half": table(lambda x, y, l: (x, y, l ^ 2)),
        "climb": climbing,
        "descend": [(b, a) for a, b in climbing],
    }


def vmem_call(kernel, out_shape, scratch=(), flops=0, bytes_accessed=0, name=None):
    single = not isinstance(out_shape, (list, tuple))
    spec = pl.BlockSpec(memory_space=pltpu.VMEM)

    def call(*operands):
        return pl.pallas_call(
            kernel,
            out_shape=out_shape,
            in_specs=[spec] * len(operands),
            out_specs=spec if single else [spec] * len(out_shape),
            scratch_shapes=list(scratch),
            cost_estimate=pl.CostEstimate(
                flops=flops, bytes_accessed=bytes_accessed, transcendentals=0
            ),
            name=name,
        )(*operands)

    return call


def split2(value):
    high = value.astype(jnp.bfloat16)
    return high, (value - high.astype(jnp.float32)).astype(jnp.bfloat16)


def split3(value):
    high, _ = split2(value)
    rest = value - high.astype(jnp.float32)
    middle, low = split2(rest)
    return high, middle, low


def dot(a, b, dims=((1,), (0,))):
    return lax.dot_general(a, b, (dims, ((), ())), preferred_element_type=jnp.float32)


def pack_kernel(rows, pert_ref, inn_ref, prec_ref, owner_ref, slot_ref, count_ref, local_ref, out_ref, tail):
    edge = jnp.where(lax.axis_index("tx") == 0, owner_ref.shape[0] - 1, 0)
    slots = owner_ref.shape[2]
    out_ref[0:rows, :] = pert_ref[...]
    active = lax.broadcasted_iota(jnp.int32, (1, slots), 1) < count_ref[edge, 0]
    local = jnp.where(active, local_ref[edge], 0.0)
    slot = slot_ref[edge]
    lists = [
        prec_ref[...].astype(jnp.float32),
        inn_ref[...].astype(jnp.float32),
        owner_ref[edge].astype(jnp.float32),
        (slot // 128).astype(jnp.float32),
        (slot % 128).astype(jnp.float32),
    ] + [piece.astype(jnp.float32) for piece in split3(local)]
    for k, row in enumerate(lists):
        for part in range(2):
            tail[2 * k + part : 2 * k + part + 1, :] = row[:, 128 * part : 128 * (part + 1)]
    out_ref[rows : rows + 16, :] = tail[...].astype(jnp.bfloat16)


def table_kernel(rows, cols, owner_ref, slot_ref, count_ref, local_ref, other_ref, out_ref):
    tile_x, tile_y, part = (lax.axis_index(a) for a in ("tx", "ty", "lev"))
    tiles_y = lax.axis_size("ty")
    core = lax.rem(part, 2)
    own, slots = owner_ref.shape[0], owner_ref.shape[2]
    received = other_ref[rows : rows + 16, :].astype(jnp.float32)

    def listed(k):
        return jnp.concatenate([received[2 * k : 2 * k + 1, :], received[2 * k + 1 : 2 * k + 2, :]], axis=1)

    far_owner = listed(2).astype(jnp.int32)
    far_slot = (listed(3) * 128.0 + listed(4)).astype(jnp.int32)
    far_local = listed(5) + listed(6) + listed(7)
    position_in = lax.broadcasted_iota(jnp.int32, (1, slots), 1)

    def own_list(k):
        return owner_ref[k], slot_ref[k], jnp.where(position_in < count_ref[k, 0], local_ref[k], 0.0)

    def pick(use_far, k):
        return tuple(jnp.where(use_far, a, b) for a, b in zip((far_owner, far_slot, far_local), own_list(k)))

    lists = [pick(tile_x > 0, 0)] + [own_list(k) for k in range(own)] + [pick(tile_x == 0, own - 1)]
    half = cols // 2
    out_ref[...] = jnp.zeros_like(out_ref)
    for g, (owner, slot, local) in enumerate(lists):
        across = jnp.where(owner // tiles_y == tile_x, 0, 1)
        near = owner % tiles_y - tile_y
        first_way = jnp.where(core == 0, -1, 1)
        block = across * 3 + jnp.where(near == 0, 0, jnp.where(near == first_way, 1, 2))
        mine = slot // rows == part
        within = slot % rows
        high = jnp.where(mine, block * (rows // 128) + within // 128, -1)
        low = within % 128
        picked = jnp.where(lax.broadcasted_iota(jnp.int32, (16, slots), 0) == high, local, 0.0)
        hot = jnp.where(lax.broadcasted_iota(jnp.int32, (128, slots), 0) == low, 1.0, 0.0).astype(jnp.bfloat16)
        parts = split3(picked)
        total = dot(parts[0], hot, ((1,), (1,)))
        for piece in parts[1:]:
            total = total + dot(piece, hot, ((1,), (1,)))
        place = lax.rem(g - core * half + cols, cols)
        out_ref[pl.ds(place, 16, stride=8), :] = total


def gram_kernel(rows, cols, table_ref, b0, b1, b2, b3, b4, b5, mine_ref, rest_ref, turned, scaled):
    blocks = [b0, b1, b2, b3, b4, b5]
    per = rows // 128
    half = cols // 2
    weights = []
    products = []
    for k, ref in enumerate(blocks):
        tail = ref[rows : rows + 16, :].astype(jnp.float32)
        for part in range(per):
            hi = k * per + part
            row = table_ref[8 * hi : 8 * hi + 8, :] * tail[part : part + 1, :]
            weights.append(row)
            products.append(row * tail[per + part : per + part + 1, :])
        turned[:, rows * k : rows * (k + 1)] = ref[0:rows, :].astype(jnp.float32).T.astype(jnp.bfloat16)
    pads = 128 // 8 - len(weights)
    stacked = jnp.concatenate(weights + [jnp.zeros((8 * pads, 128), jnp.float32)], axis=0)
    columns = stacked.T
    projected = jnp.zeros((16, 128), jnp.float32)
    for k, ref in enumerate(blocks):
        wide = jnp.concatenate(products[k * per : (k + 1) * per], axis=1)
        pieces = jnp.concatenate([p.astype(jnp.float32) for p in split2(wide)], axis=0)
        projected = projected + dot(pieces.astype(jnp.bfloat16), ref[0:rows, :])
    projected = projected[0:8] + projected[8:16]
    for position in range(cols):
        for k, ref in enumerate(blocks):
            for part in range(per):
                hi = k * per + part
                values = ref[128 * part : 128 * (part + 1), :].astype(jnp.float32)
                high, low = split2(values * columns[:, 8 * hi + position : 8 * hi + position + 1])
                scaled[128 * hi : 128 * (hi + 1), 0:128] = high
                scaled[128 * hi : 128 * (hi + 1), 128:256] = low
        both = dot(turned[...], scaled[...])
        target = mine_ref if position < half else rest_ref
        at = 128 * (position % half)
        target[at : at + 128, :] = both[:, 0:128] + both[:, 128:256]
    mine_ref[128 * half : 128 * half + 8, :] = projected
    rest_ref[128 * half : 128 * half + 8, :] = jnp.concatenate(
        [projected[half : 2 * half], jnp.zeros((8 - half, 128), jnp.float32)], axis=0
    )


def join_kernel(half, mine_ref, got_ref, sum_ref, send_ref):
    total = mine_ref[...] + got_ref[...]
    sum_ref[...] = total
    edge = 128 * half
    send_ref[0:edge, :] = total[0:edge].astype(jnp.bfloat16)
    high, low = split2(total[edge : edge + 8])
    send_ref[edge : edge + 16, :] = jnp.concatenate(
        [high.astype(jnp.float32), low.astype(jnp.float32)], axis=0
    ).astype(jnp.bfloat16)


def product(a, b):
    (a_high, a_low), (b_high, b_low) = a, b
    return dot(a_high, b_high) + (dot(a_high, b_low) + dot(a_low, b_high))


def solve_kernel(half, sum_ref, got_ref, out_ref):
    size = 128
    spread = float(size - 1)
    eye = jnp.where(
        lax.broadcasted_iota(jnp.int32, (size, size), 0) == lax.broadcasted_iota(jnp.int32, (size, size), 1),
        1.0,
        0.0,
    )
    edge = size * half
    projected = (
        sum_ref[edge : edge + 8, :]
        + got_ref[edge : edge + 16, :].astype(jnp.float32)[0:8]
        + got_ref[edge : edge + 16, :].astype(jnp.float32)[8:16]
    )
    state = []
    for k in range(half):
        gram = sum_ref[size * k : size * (k + 1), :] + got_ref[size * k : size * (k + 1), :].astype(jnp.float32)
        squared = jnp.sum(jnp.sum(gram * gram, axis=0, keepdims=True), axis=1, keepdims=True)
        norm = spread + jnp.sqrt(squared)
        start = (spread * eye + gram) / norm
        state.append((norm, start))
    norms = [n for n, _ in state]
    roots = [s for _, s in state]
    inverses = [None] * half
    for iteration in range(NS_STEPS):
        last = iteration == NS_STEPS - 1
        root_parts = [split2(r) for r in roots]
        if iteration == 0:
            middles = [1.5 * eye - 0.5 * r for r in roots]
        else:
            inverse_parts = [split2(z) for z in inverses]
            middles = [1.5 * eye - 0.5 * product(z, r) for z, r in zip(inverse_parts, root_parts)]
        middle_parts = [split2(m) for m in middles]
        if not last:
            roots = [product(r, m) for r, m in zip(root_parts, middle_parts)]
        if iteration == 0:
            inverses = middles
        else:
            inverses = [product(m, z) for m, z in zip(middle_parts, inverse_parts)]
    for k in range(half):
        inverse, norm = inverses[k], norms[k]
        parts = split2(inverse)
        vector = split3(jnp.broadcast_to(projected[k : k + 1, :], (16, size)))
        inner = jnp.zeros((16, size), jnp.float32)
        for piece in vector[:2]:
            for part in parts:
                inner = inner + dot(piece, part, ((1,), (1,)))
        mean_weights = jnp.sum(inverse * inner[0:1, :], axis=1, keepdims=True) / norm
        transform = (jnp.sqrt(spread) / jnp.sqrt(norm)) * inverse + mean_weights
        out_ref[size * k : size * (k + 1), :] = transform.astype(jnp.bfloat16)


def apply_kernel(cols, members_ref, own, pair, climb, descend, pair_climb, pair_descend, out_ref, table):
    half = cols // 2
    tile_y = lax.axis_index("ty")
    tiles_y = lax.axis_size("ty")
    first = lax.rem(lax.axis_index("lev"), 2) == 0
    at_start, at_end = tile_y == 0, tile_y == tiles_y - 1
    for j in range(half):
        rows = pl.ds(128 * j, 128)
        a, b = own[rows, :], pair[rows, :]
        low, high = jnp.where(first, a, b), jnp.where(first, b, a)
        up, down = climb[rows, :], descend[rows, :]
        pair_up, pair_down = pair_climb[rows, :], pair_descend[rows, :]
        before_low = jnp.where(at_start, low, jnp.where(first, up, pair_up))
        before_high = jnp.where(at_start, high, jnp.where(first, pair_down, down))
        after_low = jnp.where(at_end, low, jnp.where(first, down, pair_down))
        after_high = jnp.where(at_end, high, jnp.where(first, pair_up, up))
        for z, (x, y) in enumerate([(before_low, before_high), (low, high), (after_low, after_high)]):
            table[z, :, 128 * j : 128 * (j + 1)] = x
            table[z, :, 128 * (j + half) : 128 * (j + half + 1)] = y
    levels, width_x, width_y, size = members_ref.shape
    span = SPACING // 2
    shape = (levels, span, span, size)
    step_x = lax.broadcasted_iota(jnp.int32, shape, 1).astype(jnp.float32)
    step_y = lax.broadcasted_iota(jnp.int32, shape, 2).astype(jnp.float32)

    def upper(place, step):
        return (step + (span + 0.5 if place % 2 == 0 else 0.5)) / (2 * span)

    for patch_x in range(width_x // span):
        states = members_ref[:, patch_x * span : (patch_x + 1) * span, :, :].astype(jnp.float32)
        mean = jnp.sum(states, axis=3, keepdims=True) * (1.0 / size)
        moved = states - mean
        column = (patch_x + 1) // 2
        up_x = upper(patch_x, step_x)
        results = []
        for patch_y in range(width_y // span):
            picked = moved[:, :, patch_y * span : (patch_y + 1) * span, :]
            rows = levels * span * span
            left = picked.reshape(rows, size).astype(jnp.bfloat16)
            place = (patch_y + 1) // 2
            near = dot(left, table[place, :, 128 * column : 128 * (column + 2)])
            far = dot(left, table[place + 1, :, 128 * column : 128 * (column + 2)])
            up_y = upper(patch_y, step_y)
            near_mix = (1.0 - up_x) * near[:, 0:128].reshape(shape) + up_x * near[:, 128:256].reshape(shape)
            far_mix = (1.0 - up_x) * far[:, 0:128].reshape(shape) + up_x * far[:, 128:256].reshape(shape)
            results.append((1.0 - up_y) * near_mix + up_y * far_mix)
        whole = mean + jnp.concatenate(results, axis=2)
        out_ref[:, patch_x * span : (patch_x + 1) * span, :, :] = whole.astype(jnp.bfloat16)


def paired_device(
    members, obs_pert, innovation, obs_precision, obs_owner, obs_slot, obs_count, local_weight
):
    axes = ("tx", "ty", "lev")
    ways = pair_patterns(axes)

    def send(value, way):
        return lax.ppermute(value, axes, ways[way])

    bf16, f32 = jnp.bfloat16, jnp.float32
    rows, size = obs_pert.shape
    cols = obs_owner.shape[0] + 2
    half = cols // 2
    shape = jax.ShapeDtypeStruct
    packed = vmem_call(
        functools.partial(pack_kernel, rows),
        shape((rows + 16, size), bf16),
        [pltpu.VMEM((16, size), f32)],
        name="pack",
    )(
        obs_pert,
        innovation.reshape(1, rows),
        obs_precision.reshape(1, rows),
        obs_owner,
        obs_slot,
        obs_count,
        local_weight,
    )
    across = send(packed, "across")
    climb, descend = send(packed, "climb"), send(packed, "descend")
    across_climb, across_descend = send(across, "climb"), send(across, "descend")
    table = vmem_call(
        functools.partial(table_kernel, rows, cols),
        shape((128, 128), f32),
        flops=6 * 2 * 48 * 256 * 128,
        bytes_accessed=1 << 17,
        name="table",
    )(obs_owner, obs_slot, obs_count, local_weight, across)
    mine, rest = vmem_call(
        functools.partial(gram_kernel, rows, cols),
        [shape((128 * half + 8, size), f32)] * 2,
        [pltpu.VMEM((size, 6 * rows), bf16), pltpu.VMEM((6 * rows, 2 * size), bf16)],
        name="gram",
    )(table, packed, climb, descend, across, across_climb, across_descend)
    total, half_sum = vmem_call(
        functools.partial(join_kernel, half),
        [shape((128 * half + 8, size), f32), shape((128 * half + 16, size), bf16)],
        name="join",
    )(mine, send(rest, "core"))
    weights = vmem_call(
        functools.partial(solve_kernel, half), shape((128 * half, size), bf16), name="solve"
    )(total, send(half_sum, "half"))
    pair = send(weights, "core")
    up, down = send(weights, "climb"), send(weights, "descend")
    pair_up, pair_down = send(up, "core"), send(down, "core")
    return vmem_call(
        functools.partial(apply_kernel, cols),
        shape(members.shape, bf16),
        [pltpu.VMEM((3, size, cols * size), bf16)],
        name="apply",
    )(members, weights, pair, up, down, pair_up, pair_down)


def fits_pairs(mesh, members, obs_pert, obs_owner):
    sizes = dict(mesh.shape)
    return (
        sizes["tx"] == 2
        and sizes["lev"] == 4
        and obs_pert == (256, 128)
        and obs_owner == (4, 1, 256)
        and members[1:] == (64, 16, 128)
    )


def solution(mesh):
    placed = (
        P("lev", "tx", "ty", None),
        P(("tx", "ty", "lev"), None),
        P(("tx", "ty", "lev")),
        P(("tx", "ty", "lev")),
        P("tx", "ty", None),
        P("tx", "ty", None),
        P("tx", "ty"),
        P("tx", "ty", None),
    )

    def local(members, obs_pert, innovation, obs_precision, obs_owner, *rest):
        paired = fits_pairs(mesh, members.shape, obs_pert.shape, obs_owner.shape)
        return (paired_device if paired else per_device)(
            members, obs_pert, innovation, obs_precision, obs_owner, *rest
        )

    return jax.shard_map(
        local,
        mesh=mesh,
        in_specs=placed,
        out_specs=P("lev", "tx", "ty", None),
        check_vma=False,
    )
```

```python
import functools

import jax
import jax.numpy as jnp
from jax import lax
from jax.experimental import pallas as pl
from jax.experimental.pallas import tpu as pltpu
from jax.sharding import PartitionSpec as P

SPACING = 16
NS_STEPS = 4
VMEM_LIMIT = 12 << 20


def padded(array, sides, width):
    for axis, dim in sides:
        size, length = (lax.axis_size(axis), array.shape[dim])
        up = [(i, (i + 1) % size) for i in range(size - 1)]
        down = [(j, i) for i, j in up]
        last = lax.slice_in_dim(array, length - width, length, axis=dim)
        initial = lax.slice_in_dim(array, 0, width, axis=dim)
        before = lax.ppermute(last, axis, up)
        after = lax.ppermute(initial, axis, down)
        array = jnp.concatenate([before, array, after], axis=dim)
    return array


def finish_solve(gram_matrix, projected):
    member_count = gram_matrix.shape[1]
    spread = float(member_count - 1)
    identity = jnp.eye(member_count, dtype=jnp.float32)
    scale_norm = spread + jnp.sqrt(jnp.sum(gram_matrix * gram_matrix, axis=(1, 2)))
    sqrt_iter = (spread * identity + gram_matrix) / scale_norm[:, None, None]
    inv_iter = jnp.broadcast_to(identity, sqrt_iter.shape)
    for iteration in range(NS_STEPS):
        middle = 1.5 * identity - 0.5 * jnp.einsum(
            "bij,bjk->bik", inv_iter, sqrt_iter, precision=lax.Precision.HIGHEST
        )
        sqrt_iter = jnp.einsum("bij,bjk->bik", sqrt_iter, middle, precision=lax.Precision.HIGHEST)
        inv_iter = jnp.einsum("bij,bjk->bik", middle, inv_iter, precision=lax.Precision.HIGHEST)
    inner = jnp.einsum("bij,bj->bi", inv_iter, projected, precision=lax.Precision.HIGHEST)
    mean_weights = (
        jnp.einsum("bij,bj->bi", inv_iter, inner, precision=lax.Precision.HIGHEST)
        / scale_norm[:, None]
    )
    transform = (jnp.sqrt(spread) / jnp.sqrt(scale_norm))[:, None, None] * inv_iter + mean_weights[
        :, :, None
    ]
    return transform.astype(jnp.bfloat16)


def fractions(count, half_span):
    place = jnp.arange(count)[:, None]
    within = jnp.arange(half_span)[None, :].astype(jnp.float32)
    return jnp.where(
        place % 2 == 0,
        (within + half_span + 0.5) / (2 * half_span),
        (within + 0.5) / (2 * half_span),
    )


def solve_columns(lookup, counts, local_part, flat_pert, flat_values):
    column_count, slots = lookup.shape
    member_count = flat_pert.shape[1]
    block_len = min(slots, 128)
    live_blocks = (jnp.max(counts) + block_len - 1) // block_len

    def add_block(block_index, carry):
        gram_matrix, projected = carry
        offset = block_index * block_len
        slot_rows = lax.dynamic_slice_in_dim(lookup, offset, block_len, 1)
        slot_local = lax.dynamic_slice_in_dim(local_part, offset, block_len, 1)
        position = offset + jnp.arange(block_len)
        active = position[None, :] < counts[:, None]
        pert_rows = flat_pert[slot_rows].astype(jnp.float32)
        picked = flat_values[:, slot_rows]
        precision_w = jnp.where(active, picked[1].astype(jnp.float32) * slot_local, 0.0)
        departure = picked[0].astype(jnp.float32)
        gram_matrix = gram_matrix + jnp.einsum(
            "bsk,bsm->bkm",
            pert_rows * precision_w[:, :, None],
            pert_rows,
            precision=lax.Precision.HIGHEST,
        )
        projected = projected + jnp.einsum(
            "bsk,bs->bk", pert_rows, precision_w * departure, precision=lax.Precision.HIGHEST
        )
        return (gram_matrix, projected)

    start_gram = jnp.zeros((column_count, member_count, member_count), jnp.float32)
    start_proj = jnp.zeros((column_count, member_count), jnp.float32)
    gram_matrix, projected = lax.fori_loop(0, live_blocks, add_block, (start_gram, start_proj))
    return finish_solve(gram_matrix, projected)


def clamp_edges(rimmed, axis_index, axis_count, dim):
    lower = jnp.where(
        axis_index == 0,
        lax.slice_in_dim(rimmed, 1, 2, axis=dim),
        lax.slice_in_dim(rimmed, 0, 1, axis=dim),
    )
    last = rimmed.shape[dim]
    upper = jnp.where(
        axis_index == axis_count - 1,
        lax.slice_in_dim(rimmed, last - 2, last - 1, axis=dim),
        lax.slice_in_dim(rimmed, last - 1, last, axis=dim),
    )
    return jnp.concatenate(
        [lower, lax.slice_in_dim(rimmed, 1, last - 1, axis=dim), upper], axis=dim
    )


def per_device(
    members, obs_pert, innovation, obs_precision, obs_owner, obs_slot, obs_count, local_weight
):
    scalars = jnp.stack([innovation, obs_precision])
    tile_pert, tile_values = (
        lax.all_gather(obs_pert, "lev", axis=0, tiled=True),
        lax.all_gather(scalars, "lev", axis=1, tiled=True),
    )
    near_pert, near_values = (
        padded(tile_pert[None, None], (("tx", 0), ("ty", 1)), 1),
        padded(tile_values[None, None], (("tx", 0), ("ty", 1)), 1),
    )
    tile_len = near_pert.shape[2]
    member_count = near_pert.shape[3]
    flat_pert = near_pert.reshape(9 * tile_len, member_count)
    flat_values = jnp.transpose(near_values, (2, 0, 1, 3)).reshape(2, 9 * tile_len)
    column_x = lax.axis_index("tx")
    column_y = lax.axis_index("ty")
    tiles_x = lax.axis_size("tx")
    tiles_y = lax.axis_size("ty")
    near_x = obs_owner // tiles_y - column_x + 1
    near_y = obs_owner % tiles_y - column_y + 1
    lookup = (near_x * 3 + near_y) * tile_len + obs_slot
    coarse_x, coarse_y, slots = lookup.shape
    lookup = lookup.reshape(coarse_x * coarse_y, slots)
    counts = obs_count.reshape(coarse_x * coarse_y)
    local_part = local_weight.reshape(coarse_x * coarse_y, slots)
    weights = solve_columns(lookup, counts, local_part, flat_pert, flat_values)
    weights = weights.reshape(coarse_x, coarse_y, member_count, member_count)
    rimmed = padded(weights, (("tx", 0), ("ty", 1)), 1)
    rimmed = clamp_edges(rimmed, column_x, tiles_x, 0)
    rimmed = clamp_edges(rimmed, column_y, tiles_y, 1)
    doubled = jnp.repeat(jnp.repeat(rimmed, 2, axis=0), 2, axis=1)
    level_count, width_x, width_y, _ = members.shape
    half_span = SPACING // 2
    patch_x = width_x // half_span
    patch_y = width_y // half_span
    frac_x = fractions(patch_x, half_span)
    frac_y = fractions(patch_y, half_span)
    ens_mean = jnp.mean(members, axis=3, keepdims=True, dtype=jnp.float32)
    pert = (members.astype(jnp.float32) - ens_mean).astype(jnp.bfloat16)
    patched = pert.reshape(level_count, patch_x, half_span, patch_y, half_span, member_count)
    summed = jnp.zeros(patched.shape, jnp.float32)
    for upper_x in range(2):
        for upper_y in range(2):
            corner = doubled[
                1 + 2 * upper_x : 1 + 2 * upper_x + patch_x,
                1 + 2 * upper_y : 1 + 2 * upper_y + patch_y,
            ]
            product = jnp.einsum(
                "lxaybi,xyij->lxaybj", patched, corner, preferred_element_type=jnp.float32
            )
            factor_x = frac_x if upper_x == 1 else 1.0 - frac_x
            factor_y = frac_y if upper_y == 1 else 1.0 - frac_y
            summed = (
                summed
                + product
                * factor_x[None, :, :, None, None, None]
                * factor_y[None, None, None, :, :, None]
            )
    return (ens_mean + summed.reshape(members.shape)).astype(jnp.bfloat16)


def pair_patterns(mesh_axes):
    tiles_x, tiles_y, parts = (lax.axis_size(a) for a in mesh_axes)

    def flat(x, y, l):
        return (x * tiles_y + y) * parts + l

    def table(move):
        return [
            (flat(x, y, l), flat(*move(x, y, l)))
            for x in range(tiles_x)
            for y in range(tiles_y)
            for l in range(parts)
        ]

    def climb(x, y, l):
        if l % 2 == 0:
            return (x, y + 1, l) if y < tiles_y - 1 else (x, y, l + 1)
        return (x, y - 1, l) if y > 0 else (x, y, l - 1)

    climbing = table(climb)
    return {
        "across": table(lambda x, y, l: (1 - x, y, l)),
        "core": table(lambda x, y, l: (x, y, l ^ 1)),
        "half": table(lambda x, y, l: (x, y, l ^ 2)),
        "climb": climbing,
        "descend": [(b, a) for a, b in climbing],
    }


def vmem_call(kernel, out_shape, scratch=(), flops=0, bytes_accessed=0, name=None):
    single = not isinstance(out_shape, (list, tuple))
    spec = pl.BlockSpec(memory_space=pltpu.VMEM)

    def call(*operands):
        return pl.pallas_call(
            kernel,
            out_shape=out_shape,
            in_specs=[spec] * len(operands),
            out_specs=spec if single else [spec] * len(out_shape),
            scratch_shapes=list(scratch),
            cost_estimate=pl.CostEstimate(
                flops=flops, bytes_accessed=bytes_accessed, transcendentals=0
            ),
            compiler_params=pltpu.CompilerParams(vmem_limit_bytes=VMEM_LIMIT),
            name=name,
        )(*operands)

    return call


def split2(value):
    high = value.astype(jnp.bfloat16)
    return high, (value - high.astype(jnp.float32)).astype(jnp.bfloat16)


def split3(value):
    high, _ = split2(value)
    rest = value - high.astype(jnp.float32)
    middle, low = split2(rest)
    return high, middle, low


def dot(a, b, dims=((1,), (0,))):
    return lax.dot_general(a, b, (dims, ((), ())), preferred_element_type=jnp.float32)


def pack_kernel(rows, pert_ref, inn_ref, prec_ref, owner_ref, slot_ref, count_ref, local_ref, out_ref, tail):
    edge = jnp.where(lax.axis_index("tx") == 0, owner_ref.shape[0] - 1, 0)
    slots = owner_ref.shape[2]
    out_ref[0:rows, :] = pert_ref[...]
    active = lax.broadcasted_iota(jnp.int32, (1, slots), 1) < jnp.where(edge == 0, count_ref[0, 0], count_ref[0, owner_ref.shape[0] - 1])
    local = jnp.where(active, local_ref[edge], 0.0)
    slot = slot_ref[edge]
    for k, ref in enumerate((prec_ref, inn_ref)):
        tail[2 * k : 2 * k + 2, :] = ref[...].astype(jnp.float32)
    lists = [
        owner_ref[edge].astype(jnp.float32),
        (slot // 128).astype(jnp.float32),
        (slot % 128).astype(jnp.float32),
    ] + [piece.astype(jnp.float32) for piece in split3(local)]
    for k, row in enumerate(lists):
        for part in range(2):
            tail[4 + 2 * k + part : 5 + 2 * k + part, :] = row[:, 128 * part : 128 * (part + 1)]
    out_ref[rows : rows + 16, :] = tail[...].astype(jnp.bfloat16)


def table_kernel(rows, cols, owner_ref, slot_ref, count_ref, local_ref, other_ref, out_ref):
    tile_x, tile_y, part = (lax.axis_index(a) for a in ("tx", "ty", "lev"))
    tiles_y = lax.axis_size("ty")
    core = lax.rem(part, 2)
    own, slots = owner_ref.shape[0], owner_ref.shape[2]
    received = other_ref[rows : rows + 16, :].astype(jnp.float32)

    def listed(k):
        return jnp.concatenate([received[2 * k : 2 * k + 1, :], received[2 * k + 1 : 2 * k + 2, :]], axis=1)

    far_owner = listed(2).astype(jnp.int32)
    far_slot = (listed(3) * 128.0 + listed(4)).astype(jnp.int32)
    far_local = listed(5) + listed(6) + listed(7)
    position_in = lax.broadcasted_iota(jnp.int32, (1, slots), 1)

    def own_list(k):
        return owner_ref[k], slot_ref[k], jnp.where(position_in < count_ref[0, k], local_ref[k], 0.0)

    def pick(use_far, k):
        return tuple(jnp.where(use_far, a, b) for a, b in zip((far_owner, far_slot, far_local), own_list(k)))

    lists = [pick(tile_x > 0, 0)] + [own_list(k) for k in range(own)] + [pick(tile_x == 0, own - 1)]
    half = cols // 2
    out_ref[...] = jnp.zeros_like(out_ref)
    for g, (owner, slot, local) in enumerate(lists):
        across = jnp.where(owner // tiles_y == tile_x, 0, 1)
        near = owner % tiles_y - tile_y
        first_way = jnp.where(core == 0, -1, 1)
        block = across * 3 + jnp.where(near == 0, 0, jnp.where(near == first_way, 1, 2))
        mine = slot // rows == part
        within = slot % rows
        high = jnp.where(mine, block * (rows // 128) + within // 128, -1)
        low = within % 128
        picked = jnp.where(lax.broadcasted_iota(jnp.int32, (16, slots), 0) == high, local, 0.0)
        hot = jnp.where(lax.broadcasted_iota(jnp.int32, (128, slots), 0) == low, 1.0, 0.0).astype(jnp.bfloat16)
        parts = split3(picked)
        total = dot(parts[0], hot, ((1,), (1,)))
        for piece in parts[1:]:
            total = total + dot(piece, hot, ((1,), (1,)))
        place = lax.rem(g - core * half + cols, cols)
        out_ref[pl.ds(place, 16, stride=8), :] = total


def gram_kernel(rows, cols, table_ref, b0, b1, b2, b3, b4, b5, mine_ref, rest_ref, turned, scaled):
    blocks = [b0, b1, b2, b3, b4, b5]
    per = rows // 128
    half = cols // 2
    weights = []
    products = []
    for k, ref in enumerate(blocks):
        tail = ref[rows : rows + 16, :].astype(jnp.float32)
        for part in range(per):
            hi = k * per + part
            row = table_ref[8 * hi : 8 * hi + 8, :] * tail[part : part + 1, :]
            weights.append(row)
            products.append(row * tail[per + part : per + part + 1, :])
        turned[:, rows * k : rows * (k + 1)] = ref[0:rows, :].astype(jnp.float32).T.astype(jnp.bfloat16)
    pads = 128 // 8 - len(weights)
    stacked = jnp.concatenate(weights + [jnp.zeros((8 * pads, 128), jnp.float32)], axis=0)
    columns = stacked.T
    projected = jnp.zeros((16, 128), jnp.float32)
    for k, ref in enumerate(blocks):
        wide = jnp.concatenate(products[k * per : (k + 1) * per], axis=1)
        pieces = jnp.concatenate([p.astype(jnp.float32) for p in split2(wide)], axis=0)
        projected = projected + dot(pieces.astype(jnp.bfloat16), ref[0:rows, :])
    projected = projected[0:8] + projected[8:16]
    for position in range(cols):
        for k, ref in enumerate(blocks):
            for part in range(per):
                hi = k * per + part
                values = ref[128 * part : 128 * (part + 1), :].astype(jnp.float32)
                high, low = split2(values * columns[:, 8 * hi + position : 8 * hi + position + 1])
                scaled[128 * hi : 128 * (hi + 1), 0:128] = high
                scaled[128 * hi : 128 * (hi + 1), 128:256] = low
        both = dot(turned[...], scaled[...])
        target = mine_ref if position < half else rest_ref
        at = 128 * (position % half)
        target[at : at + 128, :] = both[:, 0:128] + both[:, 128:256]
    mine_ref[128 * half : 128 * half + 8, :] = projected
    rest_ref[128 * half : 128 * half + 8, :] = jnp.concatenate(
        [projected[half : 2 * half], jnp.zeros((8 - half, 128), jnp.float32)], axis=0
    )


def join_kernel(half, mine_ref, got_ref, sum_ref, send_ref):
    total = mine_ref[...] + got_ref[...]
    sum_ref[...] = total
    edge = 128 * half
    send_ref[0:edge, :] = total[0:edge].astype(jnp.bfloat16)
    high, low = split2(total[edge : edge + 8])
    send_ref[edge : edge + 16, :] = jnp.concatenate(
        [high.astype(jnp.float32), low.astype(jnp.float32)], axis=0
    ).astype(jnp.bfloat16)


def product(a, b):
    (a_high, a_low), (b_high, b_low) = a, b
    return dot(a_high, b_high) + (dot(a_high, b_low) + dot(a_low, b_high))


def solve_kernel(half, sum_ref, got_ref, out_ref):
    size = 128
    spread = float(size - 1)
    eye = jnp.where(
        lax.broadcasted_iota(jnp.int32, (size, size), 0) == lax.broadcasted_iota(jnp.int32, (size, size), 1),
        1.0,
        0.0,
    )
    edge = size * half
    projected = (
        sum_ref[edge : edge + 8, :]
        + got_ref[edge : edge + 16, :].astype(jnp.float32)[0:8]
        + got_ref[edge : edge + 16, :].astype(jnp.float32)[8:16]
    )
    state = []
    for k in range(half):
        gram = sum_ref[size * k : size * (k + 1), :] + got_ref[size * k : size * (k + 1), :].astype(jnp.float32)
        squared = jnp.sum(jnp.sum(gram * gram, axis=0, keepdims=True), axis=1, keepdims=True)
        norm = spread + jnp.sqrt(squared)
        start = (spread * eye + gram) / norm
        state.append((norm, start))
    norms = [n for n, _ in state]
    roots = [s for _, s in state]
    inverses = [None] * half
    for iteration in range(NS_STEPS):
        last = iteration == NS_STEPS - 1
        root_parts = [split2(r) for r in roots]
        if iteration == 0:
            middles = [1.5 * eye - 0.5 * r for r in roots]
        else:
            inverse_parts = [split2(z) for z in inverses]
            middles = [1.5 * eye - 0.5 * product(z, r) for z, r in zip(inverse_parts, root_parts)]
        middle_parts = [split2(m) for m in middles]
        if not last:
            roots = [product(r, m) for r, m in zip(root_parts, middle_parts)]
        if iteration == 0:
            inverses = middles
        else:
            inverses = [product(m, z) for m, z in zip(middle_parts, inverse_parts)]
    for k in range(half):
        inverse, norm = inverses[k], norms[k]
        parts = split2(inverse)
        vector = split3(jnp.broadcast_to(projected[k : k + 1, :], (16, size)))
        inner = jnp.zeros((16, size), jnp.float32)
        for piece in vector[:2]:
            for part in parts:
                inner = inner + dot(piece, part, ((1,), (1,)))
        mean_weights = jnp.sum(inverse * inner[0:1, :], axis=1, keepdims=True) / norm
        transform = (jnp.sqrt(spread) / jnp.sqrt(norm)) * inverse + mean_weights
        out_ref[size * k : size * (k + 1), :] = transform.astype(jnp.bfloat16)


def apply_kernel(cols, members_ref, own, pair, climb, descend, pair_climb, pair_descend, out_ref, table):
    half = cols // 2
    tile_y = lax.axis_index("ty")
    tiles_y = lax.axis_size("ty")
    first = lax.rem(lax.axis_index("lev"), 2) == 0
    at_start, at_end = tile_y == 0, tile_y == tiles_y - 1
    for j in range(half):
        rows = pl.ds(128 * j, 128)
        a, b = own[rows, :], pair[rows, :]
        low, high = jnp.where(first, a, b), jnp.where(first, b, a)
        up, down = climb[rows, :], descend[rows, :]
        pair_up, pair_down = pair_climb[rows, :], pair_descend[rows, :]
        before_low = jnp.where(at_start, low, jnp.where(first, up, pair_up))
        before_high = jnp.where(at_start, high, jnp.where(first, pair_down, down))
        after_low = jnp.where(at_end, low, jnp.where(first, down, pair_down))
        after_high = jnp.where(at_end, high, jnp.where(first, pair_up, up))
        for z, (x, y) in enumerate([(before_low, before_high), (low, high), (after_low, after_high)]):
            table[z, :, 128 * j : 128 * (j + 1)] = x
            table[z, :, 128 * (j + half) : 128 * (j + half + 1)] = y
    levels, width_x, width_y, size = members_ref.shape
    span = SPACING // 2
    shape = (levels, span, span, size)
    step_x = lax.broadcasted_iota(jnp.int32, shape, 1).astype(jnp.float32)
    step_y = lax.broadcasted_iota(jnp.int32, shape, 2).astype(jnp.float32)

    def upper(place, step):
        return (step + (span + 0.5 if place % 2 == 0 else 0.5)) / (2 * span)

    for patch_x in range(width_x // span):
        states = members_ref[:, patch_x * span : (patch_x + 1) * span, :, :].astype(jnp.float32)
        mean = jnp.sum(states, axis=3, keepdims=True) * (1.0 / size)
        moved = states - mean
        column = (patch_x + 1) // 2
        up_x = upper(patch_x, step_x)
        results = []
        for patch_y in range(width_y // span):
            picked = moved[:, :, patch_y * span : (patch_y + 1) * span, :]
            rows = levels * span * span
            left = picked.reshape(rows, size).astype(jnp.bfloat16)
            place = (patch_y + 1) // 2
            near = dot(left, table[place, :, 128 * column : 128 * (column + 2)])
            far = dot(left, table[place + 1, :, 128 * column : 128 * (column + 2)])
            up_y = upper(patch_y, step_y)
            near_mix = (1.0 - up_x) * near[:, 0:128].reshape(shape) + up_x * near[:, 128:256].reshape(shape)
            far_mix = (1.0 - up_x) * far[:, 0:128].reshape(shape) + up_x * far[:, 128:256].reshape(shape)
            results.append((1.0 - up_y) * near_mix + up_y * far_mix)
        whole = mean + jnp.concatenate(results, axis=2)
        out_ref[:, patch_x * span : (patch_x + 1) * span, :, :] = whole.astype(jnp.bfloat16)


def paired_device(
    members, obs_pert, innovation, obs_precision, obs_owner, obs_slot, obs_count, local_weight
):
    axes = ("tx", "ty", "lev")
    ways = pair_patterns(axes)

    def send(value, way):
        return lax.ppermute(value, axes, ways[way])

    bf16, f32 = jnp.bfloat16, jnp.float32
    rows, size = obs_pert.shape
    cols = obs_owner.shape[0] + 2
    half = cols // 2
    shape = jax.ShapeDtypeStruct
    counts = obs_count.reshape(1, -1)
    packed = vmem_call(
        functools.partial(pack_kernel, rows),
        shape((rows + 16, size), bf16),
        [pltpu.VMEM((16, size), f32)],
        name="pack",
    )(
        obs_pert,
        innovation.reshape(rows // size, size),
        obs_precision.reshape(rows // size, size),
        obs_owner,
        obs_slot,
        counts,
        local_weight,
    )
    across = send(packed, "across")
    climb, descend = send(packed, "climb"), send(packed, "descend")
    across_climb, across_descend = send(across, "climb"), send(across, "descend")
    table = vmem_call(
        functools.partial(table_kernel, rows, cols),
        shape((128, 128), f32),
        flops=6 * 2 * 48 * 256 * 128,
        bytes_accessed=1 << 17,
        name="table",
    )(obs_owner, obs_slot, counts, local_weight, across)
    mine, rest = vmem_call(
        functools.partial(gram_kernel, rows, cols),
        [shape((128 * half + 8, size), f32)] * 2,
        [pltpu.VMEM((size, 6 * rows), bf16), pltpu.VMEM((6 * rows, 2 * size), bf16)],
        name="gram",
    )(table, packed, climb, descend, across, across_climb, across_descend)
    total, half_sum = vmem_call(
        functools.partial(join_kernel, half),
        [shape((128 * half + 8, size), f32), shape((128 * half + 16, size), bf16)],
        name="join",
    )(mine, send(rest, "core"))
    weights = vmem_call(
        functools.partial(solve_kernel, half), shape((128 * half, size), bf16), name="solve"
    )(total, send(half_sum, "half"))
    pair = send(weights, "core")
    up, down = send(weights, "climb"), send(weights, "descend")
    pair_up, pair_down = send(up, "core"), send(down, "core")
    return vmem_call(
        functools.partial(apply_kernel, cols),
        shape(members.shape, bf16),
        [pltpu.VMEM((3, size, cols * size), bf16)],
        name="apply",
    )(members, weights, pair, up, down, pair_up, pair_down)


def fits_pairs(mesh, members, obs_pert, obs_owner):
    sizes = dict(mesh.shape)
    return (
        sizes["tx"] == 2
        and sizes["lev"] == 4
        and obs_pert == (256, 128)
        and obs_owner == (4, 1, 256)
        and members[1:] == (64, 16, 128)
    )


def solution(mesh):
    placed = (
        P("lev", "tx", "ty", None),
        P(("tx", "ty", "lev"), None),
        P(("tx", "ty", "lev")),
        P(("tx", "ty", "lev")),
        P("tx", "ty", None),
        P("tx", "ty", None),
        P("tx", "ty"),
        P("tx", "ty", None),
    )

    def local(members, obs_pert, innovation, obs_precision, obs_owner, *rest):
        paired = fits_pairs(mesh, members.shape, obs_pert.shape, obs_owner.shape)
        return (paired_device if paired else per_device)(
            members, obs_pert, innovation, obs_precision, obs_owner, *rest
        )

    return jax.shard_map(
        local,
        mesh=mesh,
        in_specs=placed,
        out_specs=P("lev", "tx", "ty", None),
        check_vma=False,
    )
```

```python
import functools

import jax
import jax.numpy as jnp
from jax import lax
from jax.experimental import pallas as pl
from jax.experimental.pallas import tpu as pltpu
from jax.sharding import PartitionSpec as P

SPACING = 16
NS_STEPS = 4
VMEM_LIMIT = 12 << 20
WHOLE_VMEM = 67043328


def padded(array, sides, width):
    for axis, dim in sides:
        size, length = (lax.axis_size(axis), array.shape[dim])
        up = [(i, (i + 1) % size) for i in range(size - 1)]
        down = [(j, i) for i, j in up]
        last = lax.slice_in_dim(array, length - width, length, axis=dim)
        initial = lax.slice_in_dim(array, 0, width, axis=dim)
        before = lax.ppermute(last, axis, up)
        after = lax.ppermute(initial, axis, down)
        array = jnp.concatenate([before, array, after], axis=dim)
    return array


def finish_solve(gram_matrix, projected):
    member_count = gram_matrix.shape[1]
    spread = float(member_count - 1)
    identity = jnp.eye(member_count, dtype=jnp.float32)
    scale_norm = spread + jnp.sqrt(jnp.sum(gram_matrix * gram_matrix, axis=(1, 2)))
    sqrt_iter = (spread * identity + gram_matrix) / scale_norm[:, None, None]
    inv_iter = jnp.broadcast_to(identity, sqrt_iter.shape)
    for iteration in range(NS_STEPS):
        middle = 1.5 * identity - 0.5 * jnp.einsum(
            "bij,bjk->bik", inv_iter, sqrt_iter, precision=lax.Precision.HIGHEST
        )
        sqrt_iter = jnp.einsum("bij,bjk->bik", sqrt_iter, middle, precision=lax.Precision.HIGHEST)
        inv_iter = jnp.einsum("bij,bjk->bik", middle, inv_iter, precision=lax.Precision.HIGHEST)
    inner = jnp.einsum("bij,bj->bi", inv_iter, projected, precision=lax.Precision.HIGHEST)
    mean_weights = (
        jnp.einsum("bij,bj->bi", inv_iter, inner, precision=lax.Precision.HIGHEST)
        / scale_norm[:, None]
    )
    transform = (jnp.sqrt(spread) / jnp.sqrt(scale_norm))[:, None, None] * inv_iter + mean_weights[
        :, :, None
    ]
    return transform.astype(jnp.bfloat16)


def fractions(count, half_span):
    place = jnp.arange(count)[:, None]
    within = jnp.arange(half_span)[None, :].astype(jnp.float32)
    return jnp.where(
        place % 2 == 0,
        (within + half_span + 0.5) / (2 * half_span),
        (within + 0.5) / (2 * half_span),
    )


def solve_columns(lookup, counts, local_part, flat_pert, flat_values):
    column_count, slots = lookup.shape
    member_count = flat_pert.shape[1]
    block_len = min(slots, 128)
    live_blocks = (jnp.max(counts) + block_len - 1) // block_len

    def add_block(block_index, carry):
        gram_matrix, projected = carry
        offset = block_index * block_len
        slot_rows = lax.dynamic_slice_in_dim(lookup, offset, block_len, 1)
        slot_local = lax.dynamic_slice_in_dim(local_part, offset, block_len, 1)
        position = offset + jnp.arange(block_len)
        active = position[None, :] < counts[:, None]
        pert_rows = flat_pert[slot_rows].astype(jnp.float32)
        picked = flat_values[:, slot_rows]
        precision_w = jnp.where(active, picked[1].astype(jnp.float32) * slot_local, 0.0)
        departure = picked[0].astype(jnp.float32)
        gram_matrix = gram_matrix + jnp.einsum(
            "bsk,bsm->bkm",
            pert_rows * precision_w[:, :, None],
            pert_rows,
            precision=lax.Precision.HIGHEST,
        )
        projected = projected + jnp.einsum(
            "bsk,bs->bk", pert_rows, precision_w * departure, precision=lax.Precision.HIGHEST
        )
        return (gram_matrix, projected)

    start_gram = jnp.zeros((column_count, member_count, member_count), jnp.float32)
    start_proj = jnp.zeros((column_count, member_count), jnp.float32)
    gram_matrix, projected = lax.fori_loop(0, live_blocks, add_block, (start_gram, start_proj))
    return finish_solve(gram_matrix, projected)


def clamp_edges(rimmed, axis_index, axis_count, dim):
    lower = jnp.where(
        axis_index == 0,
        lax.slice_in_dim(rimmed, 1, 2, axis=dim),
        lax.slice_in_dim(rimmed, 0, 1, axis=dim),
    )
    last = rimmed.shape[dim]
    upper = jnp.where(
        axis_index == axis_count - 1,
        lax.slice_in_dim(rimmed, last - 2, last - 1, axis=dim),
        lax.slice_in_dim(rimmed, last - 1, last, axis=dim),
    )
    return jnp.concatenate(
        [lower, lax.slice_in_dim(rimmed, 1, last - 1, axis=dim), upper], axis=dim
    )


def per_device(
    members, obs_pert, innovation, obs_precision, obs_owner, obs_slot, obs_count, local_weight
):
    scalars = jnp.stack([innovation, obs_precision])
    tile_pert, tile_values = (
        lax.all_gather(obs_pert, "lev", axis=0, tiled=True),
        lax.all_gather(scalars, "lev", axis=1, tiled=True),
    )
    near_pert, near_values = (
        padded(tile_pert[None, None], (("tx", 0), ("ty", 1)), 1),
        padded(tile_values[None, None], (("tx", 0), ("ty", 1)), 1),
    )
    tile_len = near_pert.shape[2]
    member_count = near_pert.shape[3]
    flat_pert = near_pert.reshape(9 * tile_len, member_count)
    flat_values = jnp.transpose(near_values, (2, 0, 1, 3)).reshape(2, 9 * tile_len)
    column_x = lax.axis_index("tx")
    column_y = lax.axis_index("ty")
    tiles_x = lax.axis_size("tx")
    tiles_y = lax.axis_size("ty")
    near_x = obs_owner // tiles_y - column_x + 1
    near_y = obs_owner % tiles_y - column_y + 1
    lookup = (near_x * 3 + near_y) * tile_len + obs_slot
    coarse_x, coarse_y, slots = lookup.shape
    lookup = lookup.reshape(coarse_x * coarse_y, slots)
    counts = obs_count.reshape(coarse_x * coarse_y)
    local_part = local_weight.reshape(coarse_x * coarse_y, slots)
    weights = solve_columns(lookup, counts, local_part, flat_pert, flat_values)
    weights = weights.reshape(coarse_x, coarse_y, member_count, member_count)
    rimmed = padded(weights, (("tx", 0), ("ty", 1)), 1)
    rimmed = clamp_edges(rimmed, column_x, tiles_x, 0)
    rimmed = clamp_edges(rimmed, column_y, tiles_y, 1)
    doubled = jnp.repeat(jnp.repeat(rimmed, 2, axis=0), 2, axis=1)
    level_count, width_x, width_y, _ = members.shape
    half_span = SPACING // 2
    patch_x = width_x // half_span
    patch_y = width_y // half_span
    frac_x = fractions(patch_x, half_span)
    frac_y = fractions(patch_y, half_span)
    ens_mean = jnp.mean(members, axis=3, keepdims=True, dtype=jnp.float32)
    pert = (members.astype(jnp.float32) - ens_mean).astype(jnp.bfloat16)
    patched = pert.reshape(level_count, patch_x, half_span, patch_y, half_span, member_count)
    summed = jnp.zeros(patched.shape, jnp.float32)
    for upper_x in range(2):
        for upper_y in range(2):
            corner = doubled[
                1 + 2 * upper_x : 1 + 2 * upper_x + patch_x,
                1 + 2 * upper_y : 1 + 2 * upper_y + patch_y,
            ]
            product = jnp.einsum(
                "lxaybi,xyij->lxaybj", patched, corner, preferred_element_type=jnp.float32
            )
            factor_x = frac_x if upper_x == 1 else 1.0 - frac_x
            factor_y = frac_y if upper_y == 1 else 1.0 - frac_y
            summed = (
                summed
                + product
                * factor_x[None, :, :, None, None, None]
                * factor_y[None, None, None, :, :, None]
            )
    return (ens_mean + summed.reshape(members.shape)).astype(jnp.bfloat16)


def pair_patterns(mesh_axes):
    tiles_x, tiles_y, parts = (lax.axis_size(a) for a in mesh_axes)

    def flat(x, y, l):
        return (x * tiles_y + y) * parts + l

    def table(move):
        return [
            (flat(x, y, l), flat(*move(x, y, l)))
            for x in range(tiles_x)
            for y in range(tiles_y)
            for l in range(parts)
        ]

    def climb(x, y, l):
        if l % 2 == 0:
            return (x, y + 1, l) if y < tiles_y - 1 else (x, y, l + 1)
        return (x, y - 1, l) if y > 0 else (x, y, l - 1)

    climbing = table(climb)
    return {
        "across": table(lambda x, y, l: (1 - x, y, l)),
        "core": table(lambda x, y, l: (x, y, l ^ 1)),
        "half": table(lambda x, y, l: (x, y, l ^ 2)),
        "climb": climbing,
        "descend": [(b, a) for a, b in climbing],
    }


def device_call(kernel, operands, out_shape, scratch=(), flops=0, name=None, in_hbm=False, out_hbm=False, limit=VMEM_LIMIT):
    single = not isinstance(out_shape, (list, tuple))
    spec = pl.BlockSpec(memory_space=pltpu.VMEM)
    hbm = pl.BlockSpec(memory_space=pltpu.HBM)
    out_spec = hbm if out_hbm else spec
    return pl.pallas_call(
        kernel,
        out_shape=out_shape,
        in_specs=[hbm if in_hbm else spec] * len(operands),
        out_specs=out_spec if single else [out_spec] * len(out_shape),
        scratch_shapes=list(scratch),
        cost_estimate=pl.CostEstimate(flops=flops, bytes_accessed=1 << 18, transcendentals=0),
        compiler_params=pltpu.CompilerParams(vmem_limit_bytes=limit),
        name=name,
    )(*operands)


def split2(value):
    high = value.astype(jnp.bfloat16)
    return high, (value - high.astype(jnp.float32)).astype(jnp.bfloat16)


def split3(value):
    high, _ = split2(value)
    rest = value - high.astype(jnp.float32)
    middle, low = split2(rest)
    return high, middle, low


def dot(a, b, dims=((1,), (0,))):
    return lax.dot_general(a, b, (dims, ((), ())), preferred_element_type=jnp.float32)


def pack_kernel(
    rows, pert, inn, prec, owner, slot, count, local, out_ref, inn_ref, prec_ref, owner_ref, slot_ref, count_ref, local_ref, tail, sems
):
    sources = (owner, slot, count, local, inn, prec, pert)
    targets = (owner_ref, slot_ref, count_ref, local_ref, inn_ref, prec_ref, out_ref.at[0:rows, :])
    copies = [pltpu.make_async_copy(x, y, sems.at[k]) for k, (x, y) in enumerate(zip(sources, targets))]
    for copy in copies:
        copy.start()
    for copy in copies[:-1]:
        copy.wait()
    edge = jnp.where(lax.axis_index("tx") == 0, owner_ref.shape[0] - 1, 0)
    slots = owner_ref.shape[2]
    limit = jnp.where(edge == 0, count_ref[0, 0], count_ref[0, owner_ref.shape[0] - 1])
    active = lax.broadcasted_iota(jnp.int32, (1, slots), 1) < limit
    local_part = jnp.where(active, local_ref[edge], 0.0)
    slot_part = slot_ref[edge]
    for k, ref in enumerate((prec_ref, inn_ref)):
        tail[2 * k : 2 * k + 2, :] = ref[...].astype(jnp.float32)
    lists = [
        owner_ref[edge].astype(jnp.float32),
        (slot_part // 128).astype(jnp.float32),
        (slot_part % 128).astype(jnp.float32),
    ] + [piece.astype(jnp.float32) for piece in split3(local_part)]
    for k, row in enumerate(lists):
        for part in range(2):
            tail[4 + 2 * k + part : 5 + 2 * k + part, :] = row[:, 128 * part : 128 * (part + 1)]
    out_ref[rows : rows + 16, :] = tail[...].astype(jnp.bfloat16)
    copies[-1].wait()


def table_kernel(rows, cols, owner_ref, slot_ref, count_ref, local_ref, other_ref, out_ref):
    tile_x, tile_y, part = (lax.axis_index(a) for a in ("tx", "ty", "lev"))
    tiles_y = lax.axis_size("ty")
    core = lax.rem(part, 2)
    own, slots = owner_ref.shape[0], owner_ref.shape[2]
    received = other_ref[rows : rows + 16, :].astype(jnp.float32)

    def listed(k):
        return jnp.concatenate([received[2 * k : 2 * k + 1, :], received[2 * k + 1 : 2 * k + 2, :]], axis=1)

    far_owner = listed(2).astype(jnp.int32)
    far_slot = (listed(3) * 128.0 + listed(4)).astype(jnp.int32)
    far_local = listed(5) + listed(6) + listed(7)
    position_in = lax.broadcasted_iota(jnp.int32, (1, slots), 1)

    def own_list(k):
        return owner_ref[k], slot_ref[k], jnp.where(position_in < count_ref[0, k], local_ref[k], 0.0)

    def pick(use_far, k):
        return tuple(jnp.where(use_far, a, b) for a, b in zip((far_owner, far_slot, far_local), own_list(k)))

    lists = [pick(tile_x > 0, 0)] + [own_list(k) for k in range(own)] + [pick(tile_x == 0, own - 1)]
    half = cols // 2
    out_ref[...] = jnp.zeros_like(out_ref)
    for g, (owner, slot, local) in enumerate(lists):
        across = jnp.where(owner // tiles_y == tile_x, 0, 1)
        near = owner % tiles_y - tile_y
        first_way = jnp.where(core == 0, -1, 1)
        block = across * 3 + jnp.where(near == 0, 0, jnp.where(near == first_way, 1, 2))
        mine = slot // rows == part
        within = slot % rows
        high = jnp.where(mine, block * (rows // 128) + within // 128, -1)
        low = within % 128
        picked = jnp.where(lax.broadcasted_iota(jnp.int32, (16, slots), 0) == high, local, 0.0)
        hot = jnp.where(lax.broadcasted_iota(jnp.int32, (128, slots), 0) == low, 1.0, 0.0).astype(jnp.bfloat16)
        parts = split3(picked)
        total = dot(parts[0], hot, ((1,), (1,)))
        for piece in parts[1:]:
            total = total + dot(piece, hot, ((1,), (1,)))
        place = lax.rem(g - core * half + cols, cols)
        out_ref[pl.ds(place, 16, stride=8), :] = total


def gram_blocks(rows, cols, first, blocks, table_ref, turned, plain, scaled):
    per = rows // 128
    products, weights = [], []
    for k, ref in enumerate(blocks):
        tail = ref[rows : rows + 16, :].astype(jnp.float32)
        for part in range(per):
            hi = (first + k) * per + part
            row = table_ref[8 * hi : 8 * hi + 8, :] * tail[part : part + 1, :]
            weights.append(row)
            products.append(row * tail[per + part : per + part + 1, :])
        block = ref[0:rows, :]
        plain[rows * k : rows * (k + 1), :] = block
        turned[:, rows * k : rows * (k + 1)] = block.astype(jnp.float32).T
    weight = jnp.concatenate(weights, axis=1)
    high, low = split2(jnp.concatenate(products, axis=1))
    for position in range(cols):
        at = 128 * position
        scaled[at : at + 128, :] = (turned[...] * weight[position : position + 1, :]).astype(jnp.bfloat16)
    at = 128 * cols
    scaled[at : at + 16, :] = jnp.concatenate(
        [high.astype(jnp.float32), low.astype(jnp.float32)], axis=0
    ).astype(jnp.bfloat16)
    return dot(scaled[...], plain[...])


def gram_near_kernel(rows, cols, table_ref, b0, b1, b2, b3, out_ref, turned, plain, scaled):
    out_ref[...] = gram_blocks(rows, cols, 0, [b0, b1, b2, b3], table_ref, turned, plain, scaled)


def gram_far_kernel(rows, cols, table_ref, near_ref, b4, b5, mine_ref, rest_ref, turned, plain, scaled):
    half = cols // 2
    total = near_ref[...] + gram_blocks(rows, cols, 4, [b4, b5], table_ref, turned, plain, scaled)
    edge = 128 * half
    projected = total[2 * edge : 2 * edge + 8] + total[2 * edge + 8 : 2 * edge + 16]
    mine_ref[0:edge, :] = total[0:edge]
    rest_ref[0:edge, :] = total[edge : 2 * edge]
    mine_ref[edge : edge + 8, :] = projected
    rest_ref[edge : edge + 8, :] = jnp.concatenate(
        [projected[half : 2 * half], jnp.zeros((8 - half, 128), jnp.float32)], axis=0
    )


def join_kernel(half, mine_ref, got_ref, sum_ref, send_ref):
    total = mine_ref[...] + got_ref[...]
    sum_ref[...] = total
    edge = 128 * half
    send_ref[0:edge, :] = total[0:edge].astype(jnp.bfloat16)
    high, low = split2(total[edge : edge + 8])
    send_ref[edge : edge + 16, :] = jnp.concatenate(
        [high.astype(jnp.float32), low.astype(jnp.float32)], axis=0
    ).astype(jnp.bfloat16)


def product(a, b):
    (a_high, a_low), (b_high, b_low) = a, b
    left = jnp.concatenate([a_high, a_high, a_low], axis=1)
    return dot(left, jnp.concatenate([b_high, b_low, b_high], axis=0))


def solve_kernel(half, sum_ref, got_ref, out_ref):
    size = 128
    spread = float(size - 1)
    eye = jnp.where(
        lax.broadcasted_iota(jnp.int32, (size, size), 0) == lax.broadcasted_iota(jnp.int32, (size, size), 1),
        1.0,
        0.0,
    )
    edge = size * half
    projected = (
        sum_ref[edge : edge + 8, :]
        + got_ref[edge : edge + 16, :].astype(jnp.float32)[0:8]
        + got_ref[edge : edge + 16, :].astype(jnp.float32)[8:16]
    )
    state = []
    for k in range(half):
        gram = sum_ref[size * k : size * (k + 1), :] + got_ref[size * k : size * (k + 1), :].astype(jnp.float32)
        squared = jnp.sum(jnp.sum(gram * gram, axis=0, keepdims=True), axis=1, keepdims=True)
        norm = spread + jnp.sqrt(squared)
        start = (spread * eye + gram) / norm
        state.append((norm, start))
    norms = [n for n, _ in state]
    roots = [s for _, s in state]
    inverses = [None] * half
    for iteration in range(NS_STEPS):
        last = iteration == NS_STEPS - 1
        root_parts = [split2(r) for r in roots]
        if iteration == 0:
            middles = [1.5 * eye - 0.5 * r for r in roots]
        else:
            inverse_parts = [split2(z) for z in inverses]
            middles = [1.5 * eye - 0.5 * product(z, r) for z, r in zip(inverse_parts, root_parts)]
        middle_parts = [split2(m) for m in middles]
        if not last:
            roots = [product(r, m) for r, m in zip(root_parts, middle_parts)]
        if iteration == 0:
            inverses = middles
        else:
            inverses = [product(m, z) for m, z in zip(middle_parts, inverse_parts)]
    for k in range(half):
        inverse, norm = inverses[k], norms[k]
        parts = split2(inverse)
        vector = split3(jnp.broadcast_to(projected[k : k + 1, :], (16, size)))
        inner = jnp.zeros((16, size), jnp.float32)
        for piece in vector[:2]:
            for part in parts:
                inner = inner + dot(piece, part, ((1,), (1,)))
        mean_weights = jnp.sum(inverse * inner[0:1, :], axis=1, keepdims=True) / norm
        transform = (jnp.sqrt(spread) / jnp.sqrt(norm)) * inverse + mean_weights
        out_ref[size * k : size * (k + 1), :] = transform.astype(jnp.bfloat16)


def upper(place, step):
    span = SPACING // 2
    return (step + (span + 0.5 if place % 2 == 0 else 0.5)) / (2 * span)


def near_kernel(cols, members_ref, own, pair, part_ref, pert_ref, table):
    half = cols // 2
    first = lax.rem(lax.axis_index("lev"), 2) == 0
    for j in range(half):
        rows = pl.ds(128 * j, 128)
        a, b = own[rows, :], pair[rows, :]
        table[:, 128 * j : 128 * (j + 1)] = jnp.where(first, a, b)
        table[:, 128 * (j + half) : 128 * (j + half + 1)] = jnp.where(first, b, a)
    levels, width_x, width_y, size = members_ref.shape
    span = SPACING // 2
    shape = (levels, span, span, size)
    rows = levels * span * span
    step_x = lax.broadcasted_iota(jnp.int32, shape, 1).astype(jnp.float32)
    step_y = lax.broadcasted_iota(jnp.int32, shape, 2).astype(jnp.float32)
    for patch_x in range(width_x // span):
        states = members_ref[:, patch_x * span : (patch_x + 1) * span, :, :].astype(jnp.float32)
        mean = jnp.sum(states, axis=3, keepdims=True) * (1.0 / size)
        moved = states - mean
        column = (patch_x + 1) // 2
        up_x = upper(patch_x, step_x)
        for patch_y in range(2):
            inside = slice(patch_y * span, (patch_y + 1) * span)
            left = moved[:, :, inside, :].reshape(rows, size).astype(jnp.bfloat16)
            pert_ref[patch_x, patch_y] = left
            both = dot(left, table[:, 128 * column : 128 * (column + 2)])
            mix = (1.0 - up_x) * both[:, 0:128].reshape(shape) + up_x * both[:, 128:256].reshape(shape)
            up_y = upper(patch_y, step_y)
            share = up_y if patch_y == 0 else 1.0 - up_y
            part_ref[patch_x, patch_y] = (mean[:, :, inside, :] + share * mix).reshape(rows, size)


def far_kernel(cols, part_ref, pert_ref, own, pair, climb, descend, pair_climb, pair_descend, out_hbm, table, staged, sems):
    half = cols // 2
    tile_y = lax.axis_index("ty")
    first = lax.rem(lax.axis_index("lev"), 2) == 0
    at_start, at_end = tile_y == 0, tile_y == lax.axis_size("ty") - 1
    for j in range(half):
        rows = pl.ds(128 * j, 128)
        a, b = own[rows, :], pair[rows, :]
        low, high = jnp.where(first, a, b), jnp.where(first, b, a)
        up, down = climb[rows, :], descend[rows, :]
        pair_up, pair_down = pair_climb[rows, :], pair_descend[rows, :]
        before = (
            jnp.where(at_start, low, jnp.where(first, up, pair_up)),
            jnp.where(at_start, high, jnp.where(first, pair_down, down)),
        )
        after = (
            jnp.where(at_end, low, jnp.where(first, down, pair_down)),
            jnp.where(at_end, high, jnp.where(first, pair_up, up)),
        )
        for z, (x, y) in enumerate((before, after)):
            table[z, :, 128 * j : 128 * (j + 1)] = x
            table[z, :, 128 * (j + half) : 128 * (j + half + 1)] = y
    levels, width_x, width_y, size = staged.shape
    span = SPACING // 2
    shape = (levels, span, span, size)
    step_x = lax.broadcasted_iota(jnp.int32, shape, 1).astype(jnp.float32)
    step_y = lax.broadcasted_iota(jnp.int32, shape, 2).astype(jnp.float32)
    copies = []
    for patch_x in range(width_x // span):
        column = (patch_x + 1) // 2
        up_x = upper(patch_x, step_x)
        results = []
        for patch_y in range(2):
            both = dot(pert_ref[patch_x, patch_y], table[patch_y, :, 128 * column : 128 * (column + 2)])
            mix = (1.0 - up_x) * both[:, 0:128].reshape(shape) + up_x * both[:, 128:256].reshape(shape)
            up_y = upper(patch_y, step_y)
            share = 1.0 - up_y if patch_y == 0 else up_y
            results.append(part_ref[patch_x, patch_y].reshape(shape) + share * mix)
        inside = pl.ds(patch_x * span, span)
        staged[:, inside, :, :] = jnp.concatenate(results, axis=2).astype(jnp.bfloat16)
        copy = pltpu.make_async_copy(staged.at[:, inside], out_hbm.at[:, inside], sems.at[patch_x])
        copy.start()
        copies.append(copy)
    for copy in copies:
        copy.wait()


def paired_device(
    members, obs_pert, innovation, obs_precision, obs_owner, obs_slot, obs_count, local_weight
):
    axes = ("tx", "ty", "lev")
    ways = pair_patterns(axes)

    def send(value, way):
        return lax.ppermute(value, axes, ways[way])

    bf16, f32 = jnp.bfloat16, jnp.float32
    rows, size = obs_pert.shape
    cols = obs_owner.shape[0] + 2
    half = cols // 2
    shape = jax.ShapeDtypeStruct
    counts = obs_count.reshape(1, -1)
    lists = (obs_owner, obs_slot, counts, local_weight)
    scalars = [v.reshape(rows // size, size) for v in (innovation, obs_precision)]
    packed = device_call(
        functools.partial(pack_kernel, rows),
        (obs_pert, *scalars, *lists),
        shape((rows + 16, size), bf16),
        [pltpu.VMEM(v.shape, v.dtype) for v in scalars]
        + [
            pltpu.VMEM(obs_owner.shape, jnp.int32),
            pltpu.VMEM(obs_slot.shape, jnp.int32),
            pltpu.SMEM(counts.shape, jnp.int32),
            pltpu.VMEM(local_weight.shape, f32),
            pltpu.VMEM((16, size), f32),
            pltpu.SemaphoreType.DMA((7,)),
        ],
        name="pack",
        in_hbm=True,
        limit=WHOLE_VMEM - 2 * (rows + 16) * size * 2,
    )
    across = send(packed, "across")
    climb, descend = send(packed, "climb"), send(packed, "descend")
    across_climb, across_descend = send(across, "climb"), send(across, "descend")
    table = device_call(
        functools.partial(table_kernel, rows, cols),
        (*lists, across),
        shape((128, 128), f32),
        flops=6 * 2 * 48 * 256 * 128,
        name="table",
    )
    tall = size * cols + 16
    near = device_call(
        functools.partial(gram_near_kernel, rows, cols),
        (table, packed, climb, descend, across),
        shape((tall, size), f32),
        [
            pltpu.VMEM((size, 4 * rows), f32),
            pltpu.VMEM((4 * rows, size), bf16),
            pltpu.VMEM((tall, 4 * rows), bf16),
        ],
        flops=2 * tall * size * 4 * rows,
        name="gram_near",
    )
    mine, rest = device_call(
        functools.partial(gram_far_kernel, rows, cols),
        (table, near, across_climb, across_descend),
        [shape((size * half + 8, size), f32)] * 2,
        [
            pltpu.VMEM((size, 2 * rows), f32),
            pltpu.VMEM((2 * rows, size), bf16),
            pltpu.VMEM((tall, 2 * rows), bf16),
        ],
        flops=2 * tall * size * 2 * rows,
        name="gram_far",
    )
    total, half_sum = device_call(
        functools.partial(join_kernel, half),
        (mine, send(rest, "core")),
        [shape((size * half + 8, size), f32), shape((size * half + 16, size), bf16)],
        name="join",
    )
    weights = device_call(
        functools.partial(solve_kernel, half),
        (total, send(half_sum, "half")),
        shape((size * half, size), bf16),
        flops=2 * 27 * half * size**3,
        name="solve",
    )
    pair = send(weights, "core")
    up, down = send(weights, "climb"), send(weights, "descend")
    levels, width_x, width_y, _ = members.shape
    patches = (width_x * 2 // SPACING, 2, levels * SPACING**2 // 4, size)
    part, pert = device_call(
        functools.partial(near_kernel, cols),
        (members, weights, pair),
        [shape(patches, f32), shape(patches, bf16)],
        [pltpu.VMEM((size, cols * size), bf16)],
        flops=2 * levels * width_x * width_y * size * 2 * size,
        name="apply_near",
    )
    up, down, part = lax.optimization_barrier((up, down, part))
    pair_up, pair_down = send(up, "core"), send(down, "core")
    return device_call(
        functools.partial(far_kernel, cols),
        (part, pert, weights, pair, up, down, pair_up, pair_down),
        shape(members.shape, bf16),
        [
            pltpu.VMEM((2, size, cols * size), bf16),
            pltpu.VMEM(members.shape, bf16),
            pltpu.SemaphoreType.DMA((patches[0],)),
        ],
        flops=2 * levels * width_x * width_y * size * 2 * size,
        name="apply_far",
        out_hbm=True,
    )


def fits_pairs(mesh, members, obs_pert, obs_owner):
    sizes = dict(mesh.shape)
    return (
        sizes["tx"] == 2
        and sizes["lev"] == 4
        and obs_pert == (256, 128)
        and obs_owner == (4, 1, 256)
        and members[1:] == (64, 16, 128)
    )


def solution(mesh):
    placed = (
        P("lev", "tx", "ty", None),
        P(("tx", "ty", "lev"), None),
        P(("tx", "ty", "lev")),
        P(("tx", "ty", "lev")),
        P("tx", "ty", None),
        P("tx", "ty", None),
        P("tx", "ty"),
        P("tx", "ty", None),
    )

    def local(members, obs_pert, innovation, obs_precision, obs_owner, *rest):
        paired = fits_pairs(mesh, members.shape, obs_pert.shape, obs_owner.shape)
        return (paired_device if paired else per_device)(
            members, obs_pert, innovation, obs_precision, obs_owner, *rest
        )

    return jax.shard_map(
        local,
        mesh=mesh,
        in_specs=placed,
        out_specs=P("lev", "tx", "ty", None),
        check_vma=False,
    )
```

```python
import functools

import jax
import jax.numpy as jnp
from jax import lax
from jax.experimental import pallas as pl
from jax.experimental.pallas import tpu as pltpu
from jax.sharding import PartitionSpec as P

SPACING = 16
NS_STEPS = 4
VMEM_LIMIT = 12 << 20
WHOLE_VMEM = 67043328


def padded(array, sides, width):
    for axis, dim in sides:
        size, length = (lax.axis_size(axis), array.shape[dim])
        up = [(i, (i + 1) % size) for i in range(size - 1)]
        down = [(j, i) for i, j in up]
        last = lax.slice_in_dim(array, length - width, length, axis=dim)
        initial = lax.slice_in_dim(array, 0, width, axis=dim)
        before = lax.ppermute(last, axis, up)
        after = lax.ppermute(initial, axis, down)
        array = jnp.concatenate([before, array, after], axis=dim)
    return array


def finish_solve(gram_matrix, projected):
    member_count = gram_matrix.shape[1]
    spread = float(member_count - 1)
    identity = jnp.eye(member_count, dtype=jnp.float32)
    scale_norm = spread + jnp.sqrt(jnp.sum(gram_matrix * gram_matrix, axis=(1, 2)))
    sqrt_iter = (spread * identity + gram_matrix) / scale_norm[:, None, None]
    inv_iter = jnp.broadcast_to(identity, sqrt_iter.shape)
    for iteration in range(NS_STEPS):
        middle = 1.5 * identity - 0.5 * jnp.einsum(
            "bij,bjk->bik", inv_iter, sqrt_iter, precision=lax.Precision.HIGHEST
        )
        sqrt_iter = jnp.einsum("bij,bjk->bik", sqrt_iter, middle, precision=lax.Precision.HIGHEST)
        inv_iter = jnp.einsum("bij,bjk->bik", middle, inv_iter, precision=lax.Precision.HIGHEST)
    inner = jnp.einsum("bij,bj->bi", inv_iter, projected, precision=lax.Precision.HIGHEST)
    mean_weights = (
        jnp.einsum("bij,bj->bi", inv_iter, inner, precision=lax.Precision.HIGHEST)
        / scale_norm[:, None]
    )
    transform = (jnp.sqrt(spread) / jnp.sqrt(scale_norm))[:, None, None] * inv_iter + mean_weights[
        :, :, None
    ]
    return transform.astype(jnp.bfloat16)


def fractions(count, half_span):
    place = jnp.arange(count)[:, None]
    within = jnp.arange(half_span)[None, :].astype(jnp.float32)
    return jnp.where(
        place % 2 == 0,
        (within + half_span + 0.5) / (2 * half_span),
        (within + 0.5) / (2 * half_span),
    )


def solve_columns(lookup, counts, local_part, flat_pert, flat_values):
    column_count, slots = lookup.shape
    member_count = flat_pert.shape[1]
    block_len = min(slots, 128)
    live_blocks = (jnp.max(counts) + block_len - 1) // block_len

    def add_block(block_index, carry):
        gram_matrix, projected = carry
        offset = block_index * block_len
        slot_rows = lax.dynamic_slice_in_dim(lookup, offset, block_len, 1)
        slot_local = lax.dynamic_slice_in_dim(local_part, offset, block_len, 1)
        position = offset + jnp.arange(block_len)
        active = position[None, :] < counts[:, None]
        pert_rows = flat_pert[slot_rows].astype(jnp.float32)
        picked = flat_values[:, slot_rows]
        precision_w = jnp.where(active, picked[1].astype(jnp.float32) * slot_local, 0.0)
        departure = picked[0].astype(jnp.float32)
        gram_matrix = gram_matrix + jnp.einsum(
            "bsk,bsm->bkm",
            pert_rows * precision_w[:, :, None],
            pert_rows,
            precision=lax.Precision.HIGHEST,
        )
        projected = projected + jnp.einsum(
            "bsk,bs->bk", pert_rows, precision_w * departure, precision=lax.Precision.HIGHEST
        )
        return (gram_matrix, projected)

    start_gram = jnp.zeros((column_count, member_count, member_count), jnp.float32)
    start_proj = jnp.zeros((column_count, member_count), jnp.float32)
    gram_matrix, projected = lax.fori_loop(0, live_blocks, add_block, (start_gram, start_proj))
    return finish_solve(gram_matrix, projected)


def clamp_edges(rimmed, axis_index, axis_count, dim):
    lower = jnp.where(
        axis_index == 0,
        lax.slice_in_dim(rimmed, 1, 2, axis=dim),
        lax.slice_in_dim(rimmed, 0, 1, axis=dim),
    )
    last = rimmed.shape[dim]
    upper = jnp.where(
        axis_index == axis_count - 1,
        lax.slice_in_dim(rimmed, last - 2, last - 1, axis=dim),
        lax.slice_in_dim(rimmed, last - 1, last, axis=dim),
    )
    return jnp.concatenate(
        [lower, lax.slice_in_dim(rimmed, 1, last - 1, axis=dim), upper], axis=dim
    )


def per_device(
    members, obs_pert, innovation, obs_precision, obs_owner, obs_slot, obs_count, local_weight
):
    scalars = jnp.stack([innovation, obs_precision])
    tile_pert, tile_values = (
        lax.all_gather(obs_pert, "lev", axis=0, tiled=True),
        lax.all_gather(scalars, "lev", axis=1, tiled=True),
    )
    near_pert, near_values = (
        padded(tile_pert[None, None], (("tx", 0), ("ty", 1)), 1),
        padded(tile_values[None, None], (("tx", 0), ("ty", 1)), 1),
    )
    tile_len = near_pert.shape[2]
    member_count = near_pert.shape[3]
    flat_pert = near_pert.reshape(9 * tile_len, member_count)
    flat_values = jnp.transpose(near_values, (2, 0, 1, 3)).reshape(2, 9 * tile_len)
    column_x = lax.axis_index("tx")
    column_y = lax.axis_index("ty")
    tiles_x = lax.axis_size("tx")
    tiles_y = lax.axis_size("ty")
    near_x = obs_owner // tiles_y - column_x + 1
    near_y = obs_owner % tiles_y - column_y + 1
    lookup = (near_x * 3 + near_y) * tile_len + obs_slot
    coarse_x, coarse_y, slots = lookup.shape
    lookup = lookup.reshape(coarse_x * coarse_y, slots)
    counts = obs_count.reshape(coarse_x * coarse_y)
    local_part = local_weight.reshape(coarse_x * coarse_y, slots)
    weights = solve_columns(lookup, counts, local_part, flat_pert, flat_values)
    weights = weights.reshape(coarse_x, coarse_y, member_count, member_count)
    rimmed = padded(weights, (("tx", 0), ("ty", 1)), 1)
    rimmed = clamp_edges(rimmed, column_x, tiles_x, 0)
    rimmed = clamp_edges(rimmed, column_y, tiles_y, 1)
    doubled = jnp.repeat(jnp.repeat(rimmed, 2, axis=0), 2, axis=1)
    level_count, width_x, width_y, _ = members.shape
    half_span = SPACING // 2
    patch_x = width_x // half_span
    patch_y = width_y // half_span
    frac_x = fractions(patch_x, half_span)
    frac_y = fractions(patch_y, half_span)
    ens_mean = jnp.mean(members, axis=3, keepdims=True, dtype=jnp.float32)
    pert = (members.astype(jnp.float32) - ens_mean).astype(jnp.bfloat16)
    patched = pert.reshape(level_count, patch_x, half_span, patch_y, half_span, member_count)
    summed = jnp.zeros(patched.shape, jnp.float32)
    for upper_x in range(2):
        for upper_y in range(2):
            corner = doubled[
                1 + 2 * upper_x : 1 + 2 * upper_x + patch_x,
                1 + 2 * upper_y : 1 + 2 * upper_y + patch_y,
            ]
            product = jnp.einsum(
                "lxaybi,xyij->lxaybj", patched, corner, preferred_element_type=jnp.float32
            )
            factor_x = frac_x if upper_x == 1 else 1.0 - frac_x
            factor_y = frac_y if upper_y == 1 else 1.0 - frac_y
            summed = (
                summed
                + product
                * factor_x[None, :, :, None, None, None]
                * factor_y[None, None, None, :, :, None]
            )
    return (ens_mean + summed.reshape(members.shape)).astype(jnp.bfloat16)


def pair_patterns(mesh_axes):
    tiles_x, tiles_y, parts = (lax.axis_size(a) for a in mesh_axes)

    def flat(x, y, l):
        return (x * tiles_y + y) * parts + l

    def table(move):
        return [
            (flat(x, y, l), flat(*move(x, y, l)))
            for x in range(tiles_x)
            for y in range(tiles_y)
            for l in range(parts)
        ]

    def climb(x, y, l):
        if l % 2 == 0:
            return (x, y + 1, l) if y < tiles_y - 1 else (x, y, l + 1)
        return (x, y - 1, l) if y > 0 else (x, y, l - 1)

    climbing = table(climb)
    return {
        "across": table(lambda x, y, l: (1 - x, y, l)),
        "core": table(lambda x, y, l: (x, y, l ^ 1)),
        "half": table(lambda x, y, l: (x, y, l ^ 2)),
        "climb": climbing,
        "descend": [(b, a) for a, b in climbing],
    }


def device_call(kernel, operands, out_shape, scratch=(), flops=0, name=None, in_hbm=False, out_hbm=False, limit=VMEM_LIMIT):
    single = not isinstance(out_shape, (list, tuple))
    spec = pl.BlockSpec(memory_space=pltpu.VMEM)
    hbm = pl.BlockSpec(memory_space=pltpu.HBM)
    out_spec = hbm if out_hbm else spec
    return pl.pallas_call(
        kernel,
        out_shape=out_shape,
        in_specs=[hbm if in_hbm else spec] * len(operands),
        out_specs=out_spec if single else [out_spec] * len(out_shape),
        scratch_shapes=list(scratch),
        cost_estimate=pl.CostEstimate(flops=flops, bytes_accessed=1 << 18, transcendentals=0),
        compiler_params=pltpu.CompilerParams(vmem_limit_bytes=limit),
        name=name,
    )(*operands)


def split2(value):
    high = value.astype(jnp.bfloat16)
    return high, (value - high.astype(jnp.float32)).astype(jnp.bfloat16)


def split3(value):
    high, _ = split2(value)
    rest = value - high.astype(jnp.float32)
    middle, low = split2(rest)
    return high, middle, low


def dot(a, b, dims=((1,), (0,))):
    return lax.dot_general(a, b, (dims, ((), ())), preferred_element_type=jnp.float32)


def pack_kernel(
    rows, pert, inn, prec, owner, slot, count, local, out_ref, inn_ref, prec_ref, owner_ref, slot_ref, count_ref, local_ref, tail, sems
):
    sources = (owner, slot, count, local, inn, prec, pert)
    targets = (owner_ref, slot_ref, count_ref, local_ref, inn_ref, prec_ref, out_ref.at[0:rows, :])
    copies = [pltpu.make_async_copy(x, y, sems.at[k]) for k, (x, y) in enumerate(zip(sources, targets))]
    for copy in copies:
        copy.start()
    for copy in copies[:-1]:
        copy.wait()
    edge = jnp.where(lax.axis_index("tx") == 0, owner_ref.shape[0] - 1, 0)
    slots = owner_ref.shape[2]
    limit = jnp.where(edge == 0, count_ref[0, 0], count_ref[0, owner_ref.shape[0] - 1])
    active = lax.broadcasted_iota(jnp.int32, (1, slots), 1) < limit
    local_part = jnp.where(active, local_ref[edge], 0.0)
    slot_part = slot_ref[edge]
    for k, ref in enumerate((prec_ref, inn_ref)):
        tail[2 * k : 2 * k + 2, :] = ref[...].astype(jnp.float32)
    lists = [
        owner_ref[edge].astype(jnp.float32),
        (slot_part // 128).astype(jnp.float32),
        (slot_part % 128).astype(jnp.float32),
    ] + [piece.astype(jnp.float32) for piece in split3(local_part)]
    for k, row in enumerate(lists):
        for part in range(2):
            tail[4 + 2 * k + part : 5 + 2 * k + part, :] = row[:, 128 * part : 128 * (part + 1)]
    out_ref[rows : rows + 16, :] = tail[...].astype(jnp.bfloat16)
    copies[-1].wait()


def table_kernel(rows, cols, owner_ref, slot_ref, count_ref, local_ref, other_ref, out_ref):
    tile_x, tile_y, part = (lax.axis_index(a) for a in ("tx", "ty", "lev"))
    tiles_y = lax.axis_size("ty")
    core = lax.rem(part, 2)
    own, slots = owner_ref.shape[0], owner_ref.shape[2]
    received = other_ref[rows : rows + 16, :].astype(jnp.float32)

    def listed(k):
        return jnp.concatenate([received[2 * k : 2 * k + 1, :], received[2 * k + 1 : 2 * k + 2, :]], axis=1)

    far_owner = listed(2).astype(jnp.int32)
    far_slot = (listed(3) * 128.0 + listed(4)).astype(jnp.int32)
    far_local = listed(5) + listed(6) + listed(7)
    position_in = lax.broadcasted_iota(jnp.int32, (1, slots), 1)

    def own_list(k):
        return owner_ref[k], slot_ref[k], jnp.where(position_in < count_ref[0, k], local_ref[k], 0.0)

    def pick(use_far, k):
        return tuple(jnp.where(use_far, a, b) for a, b in zip((far_owner, far_slot, far_local), own_list(k)))

    lists = [pick(tile_x > 0, 0)] + [own_list(k) for k in range(own)] + [pick(tile_x == 0, own - 1)]
    half = cols // 2
    out_ref[...] = jnp.zeros_like(out_ref)
    for g, (owner, slot, local) in enumerate(lists):
        across = jnp.where(owner // tiles_y == tile_x, 0, 1)
        near = owner % tiles_y - tile_y
        first_way = jnp.where(core == 0, -1, 1)
        block = across * 3 + jnp.where(near == 0, 0, jnp.where(near == first_way, 1, 2))
        mine = slot // rows == part
        within = slot % rows
        high = jnp.where(mine, block * (rows // 128) + within // 128, -1)
        low = within % 128
        picked = jnp.where(lax.broadcasted_iota(jnp.int32, (16, slots), 0) == high, local, 0.0)
        hot = jnp.where(lax.broadcasted_iota(jnp.int32, (128, slots), 0) == low, 1.0, 0.0).astype(jnp.bfloat16)
        parts = split3(picked)
        total = dot(parts[0], hot, ((1,), (1,)))
        for piece in parts[1:]:
            total = total + dot(piece, hot, ((1,), (1,)))
        place = lax.rem(g - core * half + cols, cols)
        out_ref[pl.ds(place, 16, stride=8), :] = total


def gram_blocks(rows, cols, first, blocks, table_ref, turned, plain, scaled):
    per = rows // 128
    products, weights = [], []
    for k, ref in enumerate(blocks):
        tail = ref[rows : rows + 16, :].astype(jnp.float32)
        for part in range(per):
            hi = (first + k) * per + part
            row = table_ref[8 * hi : 8 * hi + 8, :] * tail[part : part + 1, :]
            weights.append(row)
            products.append(row * tail[per + part : per + part + 1, :])
        block = ref[0:rows, :]
        plain[rows * k : rows * (k + 1), :] = block
        turned[:, rows * k : rows * (k + 1)] = block.astype(jnp.float32).T
    weight = jnp.concatenate(weights, axis=1)
    high, low = split2(jnp.concatenate(products, axis=1))
    for position in range(cols):
        at = 128 * position
        scaled[at : at + 128, :] = (turned[...] * weight[position : position + 1, :]).astype(jnp.bfloat16)
    at = 128 * cols
    scaled[at : at + 16, :] = jnp.concatenate(
        [high.astype(jnp.float32), low.astype(jnp.float32)], axis=0
    ).astype(jnp.bfloat16)
    return dot(scaled[...], plain[...])


def gram_near_kernel(rows, cols, table_ref, b0, b1, b2, b3, out_ref, turned, plain, scaled):
    out_ref[...] = gram_blocks(rows, cols, 0, [b0, b1, b2, b3], table_ref, turned, plain, scaled)


def gram_far_kernel(rows, cols, table_ref, near_ref, b4, b5, mine_ref, rest_ref, turned, plain, scaled):
    half = cols // 2
    total = near_ref[...] + gram_blocks(rows, cols, 4, [b4, b5], table_ref, turned, plain, scaled)
    edge = 128 * half
    projected = total[2 * edge : 2 * edge + 8] + total[2 * edge + 8 : 2 * edge + 16]
    mine_ref[0:edge, :] = total[0:edge]
    rest_ref[0:edge, :] = total[edge : 2 * edge]
    mine_ref[edge : edge + 8, :] = projected
    rest_ref[edge : edge + 8, :] = jnp.concatenate(
        [projected[half : 2 * half], jnp.zeros((8 - half, 128), jnp.float32)], axis=0
    )


def join_kernel(half, mine_ref, got_ref, sum_ref, send_ref):
    total = mine_ref[...] + got_ref[...]
    sum_ref[...] = total
    edge = 128 * half
    send_ref[0:edge, :] = total[0:edge].astype(jnp.bfloat16)
    high, low = split2(total[edge : edge + 8])
    send_ref[edge : edge + 16, :] = jnp.concatenate(
        [high.astype(jnp.float32), low.astype(jnp.float32)], axis=0
    ).astype(jnp.bfloat16)


def product(a, b):
    (a_high, a_low), (b_high, b_low) = a, b
    left = jnp.concatenate([a_high, a_high, a_low], axis=1)
    return dot(left, jnp.concatenate([b_high, b_low, b_high], axis=0))


def solve_kernel(half, sum_ref, got_ref, out_ref):
    size = 128
    spread = float(size - 1)
    eye = jnp.where(
        lax.broadcasted_iota(jnp.int32, (size, size), 0) == lax.broadcasted_iota(jnp.int32, (size, size), 1),
        1.0,
        0.0,
    )
    edge = size * half
    projected = (
        sum_ref[edge : edge + 8, :]
        + got_ref[edge : edge + 16, :].astype(jnp.float32)[0:8]
        + got_ref[edge : edge + 16, :].astype(jnp.float32)[8:16]
    )
    state = []
    for k in range(half):
        gram = sum_ref[size * k : size * (k + 1), :] + got_ref[size * k : size * (k + 1), :].astype(jnp.float32)
        squared = jnp.sum(jnp.sum(gram * gram, axis=0, keepdims=True), axis=1, keepdims=True)
        norm = spread + jnp.sqrt(squared)
        start = (spread * eye + gram) / norm
        state.append((norm, start))
    norms = [n for n, _ in state]
    roots = [s for _, s in state]
    inverses = [None] * half
    for iteration in range(NS_STEPS):
        last = iteration == NS_STEPS - 1
        root_parts = [split2(r) for r in roots]
        if iteration == 0:
            middles = [1.5 * eye - 0.5 * r for r in roots]
        else:
            inverse_parts = [split2(z) for z in inverses]
            middles = [1.5 * eye - 0.5 * product(z, r) for z, r in zip(inverse_parts, root_parts)]
        middle_parts = [split2(m) for m in middles]
        if not last:
            roots = [product(r, m) for r, m in zip(root_parts, middle_parts)]
        if iteration == 0:
            inverses = middles
        else:
            inverses = [product(m, z) for m, z in zip(middle_parts, inverse_parts)]
    for k in range(half):
        inverse, norm = inverses[k], norms[k]
        parts = split2(inverse)
        vector = split3(jnp.broadcast_to(projected[k : k + 1, :], (16, size)))
        inner = jnp.zeros((16, size), jnp.float32)
        for piece in vector[:2]:
            for part in parts:
                inner = inner + dot(piece, part, ((1,), (1,)))
        mean_weights = jnp.sum(inverse * inner[0:1, :], axis=1, keepdims=True) / norm
        transform = (jnp.sqrt(spread) / jnp.sqrt(norm)) * inverse + mean_weights
        out_ref[size * k : size * (k + 1), :] = transform.astype(jnp.bfloat16)


def upper(place, step):
    span = SPACING // 2
    return (step + (span + 0.5 if place % 2 == 0 else 0.5)) / (2 * span)


def near_kernel(cols, members_ref, own, pair, part_ref, pert_ref, table):
    half = cols // 2
    first = lax.rem(lax.axis_index("lev"), 2) == 0
    for j in range(half):
        rows = pl.ds(128 * j, 128)
        a, b = own[rows, :], pair[rows, :]
        table[:, 128 * j : 128 * (j + 1)] = jnp.where(first, a, b)
        table[:, 128 * (j + half) : 128 * (j + half + 1)] = jnp.where(first, b, a)
    levels, width_x, width_y, size = members_ref.shape
    span = SPACING // 2
    shape = (levels, span, span, size)
    rows = levels * span * span
    step_x = lax.broadcasted_iota(jnp.int32, shape, 1).astype(jnp.float32)
    step_y = lax.broadcasted_iota(jnp.int32, shape, 2).astype(jnp.float32)
    for patch_x in range(width_x // span):
        states = members_ref[:, patch_x * span : (patch_x + 1) * span, :, :].astype(jnp.float32)
        mean = jnp.sum(states, axis=3, keepdims=True) * (1.0 / size)
        moved = states - mean
        column = (patch_x + 1) // 2
        up_x = upper(patch_x, step_x)
        for patch_y in range(2):
            inside = slice(patch_y * span, (patch_y + 1) * span)
            left = moved[:, :, inside, :].reshape(rows, size).astype(jnp.bfloat16)
            pert_ref[patch_x, patch_y] = left
            both = dot(left, table[:, 128 * column : 128 * (column + 2)])
            mix = (1.0 - up_x) * both[:, 0:128].reshape(shape) + up_x * both[:, 128:256].reshape(shape)
            up_y = upper(patch_y, step_y)
            share = up_y if patch_y == 0 else 1.0 - up_y
            part_ref[patch_x, patch_y] = (mean[:, :, inside, :] + share * mix).reshape(rows, size)


def far_kernel(cols, part_ref, pert_ref, own, pair, climb, descend, pair_climb, pair_descend, out_hbm, table, staged, sems):
    half = cols // 2
    tile_y = lax.axis_index("ty")
    first = lax.rem(lax.axis_index("lev"), 2) == 0
    at_start, at_end = tile_y == 0, tile_y == lax.axis_size("ty") - 1
    for j in range(half):
        rows = pl.ds(128 * j, 128)
        a, b = own[rows, :], pair[rows, :]
        low, high = jnp.where(first, a, b), jnp.where(first, b, a)
        up, down = climb[rows, :], descend[rows, :]
        pair_up, pair_down = pair_climb[rows, :], pair_descend[rows, :]
        before = (
            jnp.where(at_start, low, jnp.where(first, up, pair_up)),
            jnp.where(at_start, high, jnp.where(first, pair_down, down)),
        )
        after = (
            jnp.where(at_end, low, jnp.where(first, down, pair_down)),
            jnp.where(at_end, high, jnp.where(first, pair_up, up)),
        )
        for z, (x, y) in enumerate((before, after)):
            table[z, :, 128 * j : 128 * (j + 1)] = x
            table[z, :, 128 * (j + half) : 128 * (j + half + 1)] = y
    levels, width_x, width_y, size = staged.shape
    span = SPACING // 2
    shape = (levels, span, span, size)
    step_x = lax.broadcasted_iota(jnp.int32, shape, 1).astype(jnp.float32)
    step_y = lax.broadcasted_iota(jnp.int32, shape, 2).astype(jnp.float32)
    copies = []
    for patch_x in range(width_x // span):
        column = (patch_x + 1) // 2
        up_x = upper(patch_x, step_x)
        results = []
        for patch_y in range(2):
            both = dot(pert_ref[patch_x, patch_y], table[patch_y, :, 128 * column : 128 * (column + 2)])
            mix = (1.0 - up_x) * both[:, 0:128].reshape(shape) + up_x * both[:, 128:256].reshape(shape)
            up_y = upper(patch_y, step_y)
            share = 1.0 - up_y if patch_y == 0 else up_y
            results.append(part_ref[patch_x, patch_y].reshape(shape) + share * mix)
        inside = pl.ds(patch_x * span, span)
        staged[:, inside, :, :] = jnp.concatenate(results, axis=2).astype(jnp.bfloat16)
        copy = pltpu.make_async_copy(staged.at[:, inside], out_hbm.at[:, inside], sems.at[patch_x])
        copy.start()
        copies.append(copy)
    for copy in copies:
        copy.wait()


def paired_device(
    members, obs_pert, innovation, obs_precision, obs_owner, obs_slot, obs_count, local_weight
):
    axes = ("tx", "ty", "lev")
    ways = pair_patterns(axes)

    def send(value, way):
        return lax.ppermute(value, axes, ways[way])

    bf16, f32 = jnp.bfloat16, jnp.float32
    rows, size = obs_pert.shape
    cols = obs_owner.shape[0] + 2
    half = cols // 2
    shape = jax.ShapeDtypeStruct
    counts = obs_count.reshape(1, -1)
    lists = (obs_owner, obs_slot, counts, local_weight)
    scalars = [v.reshape(rows // size, size) for v in (innovation, obs_precision)]
    packed = device_call(
        functools.partial(pack_kernel, rows),
        tuple(pltpu.with_memory_space_constraint(v, pltpu.HBM) for v in (obs_pert, *scalars, *lists)),
        shape((rows + 16, size), bf16),
        [pltpu.VMEM(v.shape, v.dtype) for v in scalars]
        + [
            pltpu.VMEM(obs_owner.shape, jnp.int32),
            pltpu.VMEM(obs_slot.shape, jnp.int32),
            pltpu.SMEM(counts.shape, jnp.int32),
            pltpu.VMEM(local_weight.shape, f32),
            pltpu.VMEM((16, size), f32),
            pltpu.SemaphoreType.DMA((7,)),
        ],
        name="pack",
        in_hbm=True,
    )
    across = send(packed, "across")
    climb, descend = send(packed, "climb"), send(packed, "descend")
    across_climb, across_descend = send(across, "climb"), send(across, "descend")
    table = device_call(
        functools.partial(table_kernel, rows, cols),
        (*lists, across),
        shape((128, 128), f32),
        flops=6 * 2 * 48 * 256 * 128,
        name="table",
    )
    tall = size * cols + 16
    near = device_call(
        functools.partial(gram_near_kernel, rows, cols),
        (table, packed, climb, descend, across),
        shape((tall, size), f32),
        [
            pltpu.VMEM((size, 4 * rows), f32),
            pltpu.VMEM((4 * rows, size), bf16),
            pltpu.VMEM((tall, 4 * rows), bf16),
        ],
        flops=2 * tall * size * 4 * rows,
        name="gram_near",
    )
    mine, rest = device_call(
        functools.partial(gram_far_kernel, rows, cols),
        (table, near, across_climb, across_descend),
        [shape((size * half + 8, size), f32)] * 2,
        [
            pltpu.VMEM((size, 2 * rows), f32),
            pltpu.VMEM((2 * rows, size), bf16),
            pltpu.VMEM((tall, 2 * rows), bf16),
        ],
        flops=2 * tall * size * 2 * rows,
        name="gram_far",
    )
    total, half_sum = device_call(
        functools.partial(join_kernel, half),
        (mine, send(rest, "core")),
        [shape((size * half + 8, size), f32), shape((size * half + 16, size), bf16)],
        name="join",
    )
    weights = device_call(
        functools.partial(solve_kernel, half),
        (total, send(half_sum, "half")),
        shape((size * half, size), bf16),
        flops=2 * 27 * half * size**3,
        name="solve",
    )
    pair = send(weights, "core")
    up, down = send(weights, "climb"), send(weights, "descend")
    levels, width_x, width_y, _ = members.shape
    patches = (width_x * 2 // SPACING, 2, levels * SPACING**2 // 4, size)
    part, pert = device_call(
        functools.partial(near_kernel, cols),
        (members, weights, pair),
        [shape(patches, f32), shape(patches, bf16)],
        [pltpu.VMEM((size, cols * size), bf16)],
        flops=2 * levels * width_x * width_y * size * 2 * size,
        name="apply_near",
    )
    up, down, part = lax.optimization_barrier((up, down, part))
    pair_up, pair_down = send(up, "core"), send(down, "core")
    return device_call(
        functools.partial(far_kernel, cols),
        (part, pert, weights, pair, up, down, pair_up, pair_down),
        shape(members.shape, bf16),
        [
            pltpu.VMEM((2, size, cols * size), bf16),
            pltpu.VMEM(members.shape, bf16),
            pltpu.SemaphoreType.DMA((patches[0],)),
        ],
        flops=2 * levels * width_x * width_y * size * 2 * size,
        name="apply_far",
        out_hbm=True,
    )


def fits_pairs(mesh, members, obs_pert, obs_owner):
    sizes = dict(mesh.shape)
    return (
        sizes["tx"] == 2
        and sizes["lev"] == 4
        and obs_pert == (256, 128)
        and obs_owner == (4, 1, 256)
        and members[1:] == (64, 16, 128)
    )


def solution(mesh):
    placed = (
        P("lev", "tx", "ty", None),
        P(("tx", "ty", "lev"), None),
        P(("tx", "ty", "lev")),
        P(("tx", "ty", "lev")),
        P("tx", "ty", None),
        P("tx", "ty", None),
        P("tx", "ty"),
        P("tx", "ty", None),
    )

    def local(members, obs_pert, innovation, obs_precision, obs_owner, *rest):
        paired = fits_pairs(mesh, members.shape, obs_pert.shape, obs_owner.shape)
        return (paired_device if paired else per_device)(
            members, obs_pert, innovation, obs_precision, obs_owner, *rest
        )

    return jax.shard_map(
        local,
        mesh=mesh,
        in_specs=placed,
        out_specs=P("lev", "tx", "ty", None),
        check_vma=False,
    )
```

```python
import functools

import jax
import jax.numpy as jnp
from jax import lax
from jax.experimental import pallas as pl
from jax.experimental.pallas import tpu as pltpu
from jax.sharding import PartitionSpec as P

SPACING = 16
NS_STEPS = 4
VMEM_LIMIT = 12 << 20


def padded(array, sides, width):
    for axis, dim in sides:
        size, length = (lax.axis_size(axis), array.shape[dim])
        up = [(i, (i + 1) % size) for i in range(size - 1)]
        down = [(j, i) for i, j in up]
        last = lax.slice_in_dim(array, length - width, length, axis=dim)
        initial = lax.slice_in_dim(array, 0, width, axis=dim)
        before = lax.ppermute(last, axis, up)
        after = lax.ppermute(initial, axis, down)
        array = jnp.concatenate([before, array, after], axis=dim)
    return array


def finish_solve(gram_matrix, projected):
    member_count = gram_matrix.shape[1]
    spread = float(member_count - 1)
    identity = jnp.eye(member_count, dtype=jnp.float32)
    scale_norm = spread + jnp.sqrt(jnp.sum(gram_matrix * gram_matrix, axis=(1, 2)))
    sqrt_iter = (spread * identity + gram_matrix) / scale_norm[:, None, None]
    inv_iter = jnp.broadcast_to(identity, sqrt_iter.shape)
    for iteration in range(NS_STEPS):
        middle = 1.5 * identity - 0.5 * jnp.einsum(
            "bij,bjk->bik", inv_iter, sqrt_iter, precision=lax.Precision.HIGHEST
        )
        sqrt_iter = jnp.einsum("bij,bjk->bik", sqrt_iter, middle, precision=lax.Precision.HIGHEST)
        inv_iter = jnp.einsum("bij,bjk->bik", middle, inv_iter, precision=lax.Precision.HIGHEST)
    inner = jnp.einsum("bij,bj->bi", inv_iter, projected, precision=lax.Precision.HIGHEST)
    mean_weights = (
        jnp.einsum("bij,bj->bi", inv_iter, inner, precision=lax.Precision.HIGHEST)
        / scale_norm[:, None]
    )
    transform = (jnp.sqrt(spread) / jnp.sqrt(scale_norm))[:, None, None] * inv_iter + mean_weights[
        :, :, None
    ]
    return transform.astype(jnp.bfloat16)


def fractions(count, half_span):
    place = jnp.arange(count)[:, None]
    within = jnp.arange(half_span)[None, :].astype(jnp.float32)
    return jnp.where(
        place % 2 == 0,
        (within + half_span + 0.5) / (2 * half_span),
        (within + 0.5) / (2 * half_span),
    )


def solve_columns(lookup, counts, local_part, flat_pert, flat_values):
    column_count, slots = lookup.shape
    member_count = flat_pert.shape[1]
    block_len = min(slots, 128)
    live_blocks = (jnp.max(counts) + block_len - 1) // block_len

    def add_block(block_index, carry):
        gram_matrix, projected = carry
        offset = block_index * block_len
        slot_rows = lax.dynamic_slice_in_dim(lookup, offset, block_len, 1)
        slot_local = lax.dynamic_slice_in_dim(local_part, offset, block_len, 1)
        position = offset + jnp.arange(block_len)
        active = position[None, :] < counts[:, None]
        pert_rows = flat_pert[slot_rows].astype(jnp.float32)
        picked = flat_values[:, slot_rows]
        precision_w = jnp.where(active, picked[1].astype(jnp.float32) * slot_local, 0.0)
        departure = picked[0].astype(jnp.float32)
        gram_matrix = gram_matrix + jnp.einsum(
            "bsk,bsm->bkm",
            pert_rows * precision_w[:, :, None],
            pert_rows,
            precision=lax.Precision.HIGHEST,
        )
        projected = projected + jnp.einsum(
            "bsk,bs->bk", pert_rows, precision_w * departure, precision=lax.Precision.HIGHEST
        )
        return (gram_matrix, projected)

    start_gram = jnp.zeros((column_count, member_count, member_count), jnp.float32)
    start_proj = jnp.zeros((column_count, member_count), jnp.float32)
    gram_matrix, projected = lax.fori_loop(0, live_blocks, add_block, (start_gram, start_proj))
    return finish_solve(gram_matrix, projected)


def clamp_edges(rimmed, axis_index, axis_count, dim):
    lower = jnp.where(
        axis_index == 0,
        lax.slice_in_dim(rimmed, 1, 2, axis=dim),
        lax.slice_in_dim(rimmed, 0, 1, axis=dim),
    )
    last = rimmed.shape[dim]
    upper = jnp.where(
        axis_index == axis_count - 1,
        lax.slice_in_dim(rimmed, last - 2, last - 1, axis=dim),
        lax.slice_in_dim(rimmed, last - 1, last, axis=dim),
    )
    return jnp.concatenate(
        [lower, lax.slice_in_dim(rimmed, 1, last - 1, axis=dim), upper], axis=dim
    )


def per_device(
    members, obs_pert, innovation, obs_precision, obs_owner, obs_slot, obs_count, local_weight
):
    scalars = jnp.stack([innovation, obs_precision])
    tile_pert, tile_values = (
        lax.all_gather(obs_pert, "lev", axis=0, tiled=True),
        lax.all_gather(scalars, "lev", axis=1, tiled=True),
    )
    near_pert, near_values = (
        padded(tile_pert[None, None], (("tx", 0), ("ty", 1)), 1),
        padded(tile_values[None, None], (("tx", 0), ("ty", 1)), 1),
    )
    tile_len = near_pert.shape[2]
    member_count = near_pert.shape[3]
    flat_pert = near_pert.reshape(9 * tile_len, member_count)
    flat_values = jnp.transpose(near_values, (2, 0, 1, 3)).reshape(2, 9 * tile_len)
    column_x = lax.axis_index("tx")
    column_y = lax.axis_index("ty")
    tiles_x = lax.axis_size("tx")
    tiles_y = lax.axis_size("ty")
    near_x = obs_owner // tiles_y - column_x + 1
    near_y = obs_owner % tiles_y - column_y + 1
    lookup = (near_x * 3 + near_y) * tile_len + obs_slot
    coarse_x, coarse_y, slots = lookup.shape
    lookup = lookup.reshape(coarse_x * coarse_y, slots)
    counts = obs_count.reshape(coarse_x * coarse_y)
    local_part = local_weight.reshape(coarse_x * coarse_y, slots)
    weights = solve_columns(lookup, counts, local_part, flat_pert, flat_values)
    weights = weights.reshape(coarse_x, coarse_y, member_count, member_count)
    rimmed = padded(weights, (("tx", 0), ("ty", 1)), 1)
    rimmed = clamp_edges(rimmed, column_x, tiles_x, 0)
    rimmed = clamp_edges(rimmed, column_y, tiles_y, 1)
    doubled = jnp.repeat(jnp.repeat(rimmed, 2, axis=0), 2, axis=1)
    level_count, width_x, width_y, _ = members.shape
    half_span = SPACING // 2
    patch_x = width_x // half_span
    patch_y = width_y // half_span
    frac_x = fractions(patch_x, half_span)
    frac_y = fractions(patch_y, half_span)
    ens_mean = jnp.mean(members, axis=3, keepdims=True, dtype=jnp.float32)
    pert = (members.astype(jnp.float32) - ens_mean).astype(jnp.bfloat16)
    patched = pert.reshape(level_count, patch_x, half_span, patch_y, half_span, member_count)
    summed = jnp.zeros(patched.shape, jnp.float32)
    for upper_x in range(2):
        for upper_y in range(2):
            corner = doubled[
                1 + 2 * upper_x : 1 + 2 * upper_x + patch_x,
                1 + 2 * upper_y : 1 + 2 * upper_y + patch_y,
            ]
            product = jnp.einsum(
                "lxaybi,xyij->lxaybj", patched, corner, preferred_element_type=jnp.float32
            )
            factor_x = frac_x if upper_x == 1 else 1.0 - frac_x
            factor_y = frac_y if upper_y == 1 else 1.0 - frac_y
            summed = (
                summed
                + product
                * factor_x[None, :, :, None, None, None]
                * factor_y[None, None, None, :, :, None]
            )
    return (ens_mean + summed.reshape(members.shape)).astype(jnp.bfloat16)


def pair_patterns(mesh_axes):
    tiles_x, tiles_y, parts = (lax.axis_size(a) for a in mesh_axes)

    def flat(x, y, l):
        return (x * tiles_y + y) * parts + l

    def table(move):
        return [
            (flat(x, y, l), flat(*move(x, y, l)))
            for x in range(tiles_x)
            for y in range(tiles_y)
            for l in range(parts)
        ]

    def climb(x, y, l):
        if l % 2 == 0:
            return (x, y + 1, l) if y < tiles_y - 1 else (x, y, l + 1)
        return (x, y - 1, l) if y > 0 else (x, y, l - 1)

    climbing = table(climb)
    return {
        "across": table(lambda x, y, l: (1 - x, y, l)),
        "core": table(lambda x, y, l: (x, y, l ^ 1)),
        "half": table(lambda x, y, l: (x, y, l ^ 2)),
        "climb": climbing,
        "descend": [(b, a) for a, b in climbing],
    }


def device_call(kernel, operands, out_shape, scratch=(), flops=0, name=None, in_hbm=False, out_hbm=False, alias=False):
    single = not isinstance(out_shape, (list, tuple))
    spec = pl.BlockSpec(memory_space=pltpu.VMEM)
    hbm = pl.BlockSpec(memory_space=pltpu.HBM)
    out_spec = hbm if out_hbm else spec
    in_specs = [hbm if in_hbm else spec] * len(operands)
    if alias:
        in_specs[-1] = hbm
    return pl.pallas_call(
        kernel,
        out_shape=out_shape,
        in_specs=in_specs,
        out_specs=out_spec if single else [out_spec] * len(out_shape),
        scratch_shapes=list(scratch),
        cost_estimate=pl.CostEstimate(flops=flops, bytes_accessed=1 << 18, transcendentals=0),
        compiler_params=pltpu.CompilerParams(vmem_limit_bytes=VMEM_LIMIT),
        input_output_aliases={len(operands) - 1: 0} if alias else {},
        name=name,
    )(*operands)


def split2(value):
    high = value.astype(jnp.bfloat16)
    return high, (value - high.astype(jnp.float32)).astype(jnp.bfloat16)


def split3(value):
    high, _ = split2(value)
    rest = value - high.astype(jnp.float32)
    middle, low = split2(rest)
    return high, middle, low


def dot(a, b, dims=((1,), (0,))):
    return lax.dot_general(a, b, (dims, ((), ())), preferred_element_type=jnp.float32)


def pack_kernel(
    rows, pert, inn, prec, owner, slot, count, local, out_ref, inn_ref, prec_ref, owner_ref, slot_ref, count_ref, local_ref, tail, sems
):
    sources = (owner, slot, count, local, inn, prec, pert)
    targets = (owner_ref, slot_ref, count_ref, local_ref, inn_ref, prec_ref, out_ref.at[0:rows, :])
    copies = [pltpu.make_async_copy(x, y, sems.at[k]) for k, (x, y) in enumerate(zip(sources, targets))]
    for copy in copies:
        copy.start()
    for copy in copies[:-1]:
        copy.wait()
    edge = jnp.where(lax.axis_index("tx") == 0, owner_ref.shape[0] - 1, 0)
    slots = owner_ref.shape[2]
    limit = jnp.where(edge == 0, count_ref[0, 0], count_ref[0, owner_ref.shape[0] - 1])
    active = lax.broadcasted_iota(jnp.int32, (1, slots), 1) < limit
    local_part = jnp.where(active, local_ref[edge], 0.0)
    slot_part = slot_ref[edge]
    for k, ref in enumerate((prec_ref, inn_ref)):
        tail[2 * k : 2 * k + 2, :] = ref[...].astype(jnp.float32)
    lists = [
        owner_ref[edge].astype(jnp.float32),
        (slot_part // 128).astype(jnp.float32),
        (slot_part % 128).astype(jnp.float32),
    ] + [piece.astype(jnp.float32) for piece in split3(local_part)]
    for k, row in enumerate(lists):
        for part in range(2):
            tail[4 + 2 * k + part : 5 + 2 * k + part, :] = row[:, 128 * part : 128 * (part + 1)]
    out_ref[rows : rows + 16, :] = tail[...].astype(jnp.bfloat16)
    copies[-1].wait()


def table_kernel(rows, cols, owner_ref, slot_ref, count_ref, local_ref, other_ref, out_ref):
    tile_x, tile_y, part = (lax.axis_index(a) for a in ("tx", "ty", "lev"))
    tiles_y = lax.axis_size("ty")
    core = lax.rem(part, 2)
    own, slots = owner_ref.shape[0], owner_ref.shape[2]
    received = other_ref[rows : rows + 16, :].astype(jnp.float32)

    def listed(k):
        return jnp.concatenate([received[2 * k : 2 * k + 1, :], received[2 * k + 1 : 2 * k + 2, :]], axis=1)

    far_owner = listed(2).astype(jnp.int32)
    far_slot = (listed(3) * 128.0 + listed(4)).astype(jnp.int32)
    far_local = listed(5) + listed(6) + listed(7)
    position_in = lax.broadcasted_iota(jnp.int32, (1, slots), 1)

    def own_list(k):
        return owner_ref[k], slot_ref[k], jnp.where(position_in < count_ref[0, k], local_ref[k], 0.0)

    def pick(use_far, k):
        return tuple(jnp.where(use_far, a, b) for a, b in zip((far_owner, far_slot, far_local), own_list(k)))

    lists = [pick(tile_x > 0, 0)] + [own_list(k) for k in range(own)] + [pick(tile_x == 0, own - 1)]
    half = cols // 2
    out_ref[...] = jnp.zeros_like(out_ref)
    for g, (owner, slot, local) in enumerate(lists):
        across = jnp.where(owner // tiles_y == tile_x, 0, 1)
        near = owner % tiles_y - tile_y
        first_way = jnp.where(core == 0, -1, 1)
        block = across * 3 + jnp.where(near == 0, 0, jnp.where(near == first_way, 1, 2))
        mine = slot // rows == part
        within = slot % rows
        high = jnp.where(mine, block * (rows // 128) + within // 128, -1)
        low = within % 128
        picked = jnp.where(lax.broadcasted_iota(jnp.int32, (16, slots), 0) == high, local, 0.0)
        hot = jnp.where(lax.broadcasted_iota(jnp.int32, (128, slots), 0) == low, 1.0, 0.0).astype(jnp.bfloat16)
        parts = split3(picked)
        total = dot(parts[0], hot, ((1,), (1,)))
        for piece in parts[1:]:
            total = total + dot(piece, hot, ((1,), (1,)))
        place = lax.rem(g - core * half + cols, cols)
        out_ref[pl.ds(place, 16, stride=8), :] = total


def gram_blocks(rows, cols, first, blocks, table_ref, turned, plain, scaled):
    per = rows // 128
    products, weights = [], []
    for k, ref in enumerate(blocks):
        tail = ref[rows : rows + 16, :].astype(jnp.float32)
        for part in range(per):
            hi = (first + k) * per + part
            row = table_ref[8 * hi : 8 * hi + 8, :] * tail[part : part + 1, :]
            weights.append(row)
            products.append(row * tail[per + part : per + part + 1, :])
        block = ref[0:rows, :]
        plain[rows * k : rows * (k + 1), :] = block
        turned[:, rows * k : rows * (k + 1)] = block.astype(jnp.float32).T
    weight = jnp.concatenate(weights, axis=1)
    high, low = split2(jnp.concatenate(products, axis=1))
    for position in range(cols):
        at = 128 * position
        scaled[at : at + 128, :] = (turned[...] * weight[position : position + 1, :]).astype(jnp.bfloat16)
    at = 128 * cols
    scaled[at : at + 16, :] = jnp.concatenate(
        [high.astype(jnp.float32), low.astype(jnp.float32)], axis=0
    ).astype(jnp.bfloat16)
    return dot(scaled[...], plain[...])


def gram_near_kernel(rows, cols, table_ref, b0, b1, b2, b3, out_ref, turned, plain, scaled):
    out_ref[...] = gram_blocks(rows, cols, 0, [b0, b1, b2, b3], table_ref, turned, plain, scaled)


def gram_far_kernel(rows, cols, table_ref, near_ref, b4, b5, mine_ref, rest_ref, turned, plain, scaled):
    half = cols // 2
    total = near_ref[...] + gram_blocks(rows, cols, 4, [b4, b5], table_ref, turned, plain, scaled)
    edge = 128 * half
    projected = total[2 * edge : 2 * edge + 8] + total[2 * edge + 8 : 2 * edge + 16]
    mine_ref[0:edge, :] = total[0:edge]
    rest_ref[0:edge, :] = total[edge : 2 * edge]
    mine_ref[edge : edge + 8, :] = projected
    rest_ref[edge : edge + 8, :] = jnp.concatenate(
        [projected[half : 2 * half], jnp.zeros((8 - half, 128), jnp.float32)], axis=0
    )


def join_kernel(half, mine_ref, got_ref, sum_ref, send_ref):
    total = mine_ref[...] + got_ref[...]
    sum_ref[...] = total
    edge = 128 * half
    send_ref[0:edge, :] = total[0:edge].astype(jnp.bfloat16)
    high, low = split2(total[edge : edge + 8])
    send_ref[edge : edge + 16, :] = jnp.concatenate(
        [high.astype(jnp.float32), low.astype(jnp.float32)], axis=0
    ).astype(jnp.bfloat16)


def beside(*pieces):
    return jnp.concatenate(pieces, axis=1)


def above(*pieces):
    return jnp.concatenate(pieces, axis=0)


def product(a, b):
    (a_high, a_low), (b_high, b_low) = a, b
    return dot(beside(a_high, a_low), above(b_high, b_high)) + dot(a_high, b_low)


def solve_kernel(half, sum_ref, got_ref, out_ref):
    size = 128
    spread = float(size - 1)
    eye = jnp.where(
        lax.broadcasted_iota(jnp.int32, (size, size), 0) == lax.broadcasted_iota(jnp.int32, (size, size), 1),
        1.0,
        0.0,
    )
    edge = size * half
    projected = (
        sum_ref[edge : edge + 8, :]
        + got_ref[edge : edge + 16, :].astype(jnp.float32)[0:8]
        + got_ref[edge : edge + 16, :].astype(jnp.float32)[8:16]
    )
    state = []
    for k in range(half):
        gram = sum_ref[size * k : size * (k + 1), :] + got_ref[size * k : size * (k + 1), :].astype(jnp.float32)
        squared = jnp.sum(jnp.sum(gram * gram, axis=0, keepdims=True), axis=1, keepdims=True)
        norm = spread + jnp.sqrt(squared)
        start = (spread * eye + gram) / norm
        state.append((norm, start))
    norms = [n for n, _ in state]
    roots = [s for _, s in state]
    inverses = [None] * half
    for iteration in range(NS_STEPS):
        last = iteration == NS_STEPS - 1
        root_parts = [split2(r) for r in roots]
        if iteration == 0:
            middles = [1.5 * eye - 0.5 * r for r in roots]
            roots = [product(split2(m), r) for m, r in zip(middles, root_parts)]
            inverses = middles
            continue
        inverse_parts = [split2(z) for z in inverses]
        middles = [1.5 * eye - 0.5 * product(z, r) for z, r in zip(inverse_parts, root_parts)]
        middle_parts = [split2(m) for m in middles]
        if last:
            inverses = [product(m, z) for m, z in zip(middle_parts, inverse_parts)]
            continue
        both = [
            product(m, (beside(r[0], z[0]), beside(r[1], z[1])))
            for m, r, z in zip(middle_parts, root_parts, inverse_parts)
        ]
        roots = [x[:, 0:size] for x in both]
        inverses = [x[:, size : 2 * size] for x in both]
    for k in range(half):
        inverse, norm = inverses[k], norms[k]
        parts = split2(inverse)
        vector = split3(jnp.broadcast_to(projected[k : k + 1, :], (16, size)))
        inner = jnp.zeros((16, size), jnp.float32)
        for piece in vector[:2]:
            for part in parts:
                inner = inner + dot(piece, part, ((1,), (1,)))
        mean_weights = jnp.sum(inverse * inner[0:1, :], axis=1, keepdims=True) / norm
        transform = (jnp.sqrt(spread) / jnp.sqrt(norm)) * inverse + mean_weights
        out_ref[size * k : size * (k + 1), :] = transform.astype(jnp.bfloat16)


def upper(place, step):
    span = SPACING // 2
    return (step + (span + 0.5 if place % 2 == 0 else 0.5)) / (2 * span)


def near_kernel(cols, members_ref, own, pair, part_ref, pert_ref, table):
    half = cols // 2
    first = lax.rem(lax.axis_index("lev"), 2) == 0
    for j in range(half):
        rows = pl.ds(128 * j, 128)
        a, b = own[rows, :], pair[rows, :]
        table[:, 128 * j : 128 * (j + 1)] = jnp.where(first, a, b)
        table[:, 128 * (j + half) : 128 * (j + half + 1)] = jnp.where(first, b, a)
    levels, width_x, width_y, size = members_ref.shape
    span = SPACING // 2
    shape = (levels, span, span, size)
    rows = levels * span * span
    step_x = lax.broadcasted_iota(jnp.int32, shape, 1).astype(jnp.float32)
    step_y = lax.broadcasted_iota(jnp.int32, shape, 2).astype(jnp.float32)
    for patch_x in range(width_x // span):
        states = members_ref[:, patch_x * span : (patch_x + 1) * span, :, :].astype(jnp.float32)
        mean = jnp.sum(states, axis=3, keepdims=True) * (1.0 / size)
        moved = states - mean
        column = (patch_x + 1) // 2
        up_x = upper(patch_x, step_x)
        for patch_y in range(2):
            inside = slice(patch_y * span, (patch_y + 1) * span)
            left = moved[:, :, inside, :].reshape(rows, size).astype(jnp.bfloat16)
            pert_ref[patch_x, patch_y] = left
            both = dot(left, table[:, 128 * column : 128 * (column + 2)])
            mix = (1.0 - up_x) * both[:, 0:128].reshape(shape) + up_x * both[:, 128:256].reshape(shape)
            up_y = upper(patch_y, step_y)
            share = up_y if patch_y == 0 else 1.0 - up_y
            part_ref[patch_x, patch_y] = (mean[:, :, inside, :] + share * mix).reshape(rows, size)


def add_far(first_patch, count, first_column, table, part_ref, pert_ref, staged, out_hbm, sems):
    levels, _, _, size = staged.shape
    span = SPACING // 2
    shape = (levels, span, span, size)
    step_x = lax.broadcasted_iota(jnp.int32, shape, 1).astype(jnp.float32)
    step_y = lax.broadcasted_iota(jnp.int32, shape, 2).astype(jnp.float32)
    copies = []
    for k in range(count):
        patch_x = first_patch + k
        column = lax.div(patch_x + 1, 2) - first_column
        lanes = pl.ds(pl.multiple_of(128 * column, 128), 256)
        up_x = (step_x + jnp.where(lax.rem(patch_x, 2) == 0, span + 0.5, 0.5)) / (2 * span)
        results = []
        for patch_y in range(2):
            both = dot(pert_ref[patch_x, patch_y], table[patch_y, :, lanes])
            mix = (1.0 - up_x) * both[:, 0:128].reshape(shape) + up_x * both[:, 128:256].reshape(shape)
            up_y = upper(patch_y, step_y)
            share = 1.0 - up_y if patch_y == 0 else up_y
            results.append(part_ref[patch_x, patch_y].reshape(shape) + share * mix)
        inside = pl.ds(patch_x * span, span)
        staged[:, inside, :, :] = jnp.concatenate(results, axis=2).astype(jnp.bfloat16)
        copy = pltpu.make_async_copy(staged.at[:, inside], out_hbm.at[:, inside], sems.at[k])
        copy.start()
        copies.append(copy)
    for copy in copies:
        copy.wait()


def neighbours(climb, descend, own, first, rows):
    tile_y = lax.axis_index("ty")
    up, down, mine = climb[rows, :], descend[rows, :], own[rows, :]
    before = jnp.where(tile_y == 0, mine, jnp.where(first, up, down))
    after = jnp.where(tile_y == lax.axis_size("ty") - 1, mine, jnp.where(first, down, up))
    return before, after


def far_first_kernel(cols, part_ref, pert_ref, own, climb, descend, out_hbm, table, staged, sems):
    half = cols // 2
    core = lax.rem(lax.axis_index("lev"), 2)
    for j in range(half):
        for z, value in enumerate(neighbours(climb, descend, own, core == 0, pl.ds(128 * j, 128))):
            table[z, :, 128 * j : 128 * (j + 1)] = value
    count, total = sems.shape[0], part_ref.shape[0]
    add_far(core * (total - count), count, core * half, table, part_ref, pert_ref, staged, out_hbm, sems)


def far_rest_kernel(
    cols, part_ref, pert_ref, own, pair, climb, descend, pair_climb, pair_descend, begun_hbm, out_hbm, table, staged, sems
):
    half = cols // 2
    core = lax.rem(lax.axis_index("lev"), 2)
    first = core == 0
    for j in range(half):
        rows = pl.ds(128 * j, 128)
        mine = neighbours(climb, descend, own, first, rows)
        theirs = neighbours(pair_climb, pair_descend, pair, jnp.logical_not(first), rows)
        for z, (x, y) in enumerate(zip(mine, theirs)):
            table[z, :, 128 * j : 128 * (j + 1)] = jnp.where(first, x, y)
            table[z, :, 128 * (j + half) : 128 * (j + half + 1)] = jnp.where(first, y, x)
    count, total = sems.shape[0], part_ref.shape[0]
    add_far((1 - core) * (total - count), count, 0, table, part_ref, pert_ref, staged, out_hbm, sems)


def paired_device(
    members, obs_pert, innovation, obs_precision, obs_owner, obs_slot, obs_count, local_weight
):
    axes = ("tx", "ty", "lev")
    ways = pair_patterns(axes)

    def send(value, way):
        return lax.ppermute(value, axes, ways[way])

    bf16, f32 = jnp.bfloat16, jnp.float32
    rows, size = obs_pert.shape
    cols = obs_owner.shape[0] + 2
    half = cols // 2
    shape = jax.ShapeDtypeStruct
    counts = obs_count.reshape(1, -1)
    lists = (obs_owner, obs_slot, counts, local_weight)
    scalars = [v.reshape(rows // size, size) for v in (innovation, obs_precision)]
    packed = device_call(
        functools.partial(pack_kernel, rows),
        tuple(pltpu.with_memory_space_constraint(v, pltpu.HBM) for v in (obs_pert, *scalars, *lists)),
        shape((rows + 16, size), bf16),
        [pltpu.VMEM(v.shape, v.dtype) for v in scalars]
        + [
            pltpu.VMEM(obs_owner.shape, jnp.int32),
            pltpu.VMEM(obs_slot.shape, jnp.int32),
            pltpu.SMEM(counts.shape, jnp.int32),
            pltpu.VMEM(local_weight.shape, f32),
            pltpu.VMEM((16, size), f32),
            pltpu.SemaphoreType.DMA((7,)),
        ],
        name="pack",
        in_hbm=True,
    )
    across = send(packed, "across")
    climb, descend = send(packed, "climb"), send(packed, "descend")
    across_climb, across_descend = send(across, "climb"), send(across, "descend")
    table = device_call(
        functools.partial(table_kernel, rows, cols),
        (*lists, across),
        shape((128, 128), f32),
        flops=6 * 2 * 48 * 256 * 128,
        name="table",
    )
    tall = size * cols + 16
    near = device_call(
        functools.partial(gram_near_kernel, rows, cols),
        (table, packed, climb, descend, across),
        shape((tall, size), f32),
        [
            pltpu.VMEM((size, 4 * rows), f32),
            pltpu.VMEM((4 * rows, size), bf16),
            pltpu.VMEM((tall, 4 * rows), bf16),
        ],
        flops=2 * tall * size * 4 * rows,
        name="gram_near",
    )
    mine, rest = device_call(
        functools.partial(gram_far_kernel, rows, cols),
        (table, near, across_climb, across_descend),
        [shape((size * half + 8, size), f32)] * 2,
        [
            pltpu.VMEM((size, 2 * rows), f32),
            pltpu.VMEM((2 * rows, size), bf16),
            pltpu.VMEM((tall, 2 * rows), bf16),
        ],
        flops=2 * tall * size * 2 * rows,
        name="gram_far",
    )
    total, half_sum = device_call(
        functools.partial(join_kernel, half),
        (mine, send(rest, "core")),
        [shape((size * half + 8, size), f32), shape((size * half + 16, size), bf16)],
        name="join",
    )
    weights = device_call(
        functools.partial(solve_kernel, half),
        (total, send(half_sum, "half")),
        shape((size * half, size), bf16),
        flops=2 * 27 * half * size**3,
        name="solve",
    )
    pair = send(weights, "core")
    up, down = send(weights, "climb"), send(weights, "descend")
    levels, width_x, width_y, _ = members.shape
    patches = (width_x * 2 // SPACING, 2, levels * SPACING**2 // 4, size)
    part, pert = device_call(
        functools.partial(near_kernel, cols),
        (members, weights, pair),
        [shape(patches, f32), shape(patches, bf16)],
        [pltpu.VMEM((size, cols * size), bf16)],
        flops=2 * levels * width_x * width_y * size * 2 * size,
        name="apply_near",
    )
    up, down, part = lax.optimization_barrier((up, down, part))
    pair_up, pair_down = send(up, "core"), send(down, "core")
    early = cols - 3

    def finish(kernel, name, operands, count, wide, alias):
        return device_call(
            functools.partial(kernel, cols),
            operands,
            shape(members.shape, bf16),
            [
                pltpu.VMEM((2, size, wide * size), bf16),
                pltpu.VMEM(members.shape, bf16),
                pltpu.SemaphoreType.DMA((count,)),
            ],
            flops=2 * levels * 8 * count * width_y * size * 2 * size,
            name=name,
            out_hbm=True,
            alias=alias,
        )

    begun = finish(far_first_kernel, "far_first", (part, pert, weights, up, down), early, half, False)
    return finish(
        far_rest_kernel,
        "far_rest",
        (part, pert, weights, pair, up, down, pair_up, pair_down, begun),
        patches[0] - early,
        cols,
        True,
    )


def fits_pairs(mesh, members, obs_pert, obs_owner):
    sizes = dict(mesh.shape)
    return (
        sizes["tx"] == 2
        and sizes["lev"] == 4
        and obs_pert == (256, 128)
        and obs_owner == (4, 1, 256)
        and members[1:] == (64, 16, 128)
    )


def solution(mesh):
    placed = (
        P("lev", "tx", "ty", None),
        P(("tx", "ty", "lev"), None),
        P(("tx", "ty", "lev")),
        P(("tx", "ty", "lev")),
        P("tx", "ty", None),
        P("tx", "ty", None),
        P("tx", "ty"),
        P("tx", "ty", None),
    )

    def local(members, obs_pert, innovation, obs_precision, obs_owner, *rest):
        paired = fits_pairs(mesh, members.shape, obs_pert.shape, obs_owner.shape)
        return (paired_device if paired else per_device)(
            members, obs_pert, innovation, obs_precision, obs_owner, *rest
        )

    return jax.shard_map(
        local,
        mesh=mesh,
        in_specs=placed,
        out_specs=P("lev", "tx", "ty", None),
        check_vma=False,
    )
```

```python
import functools

import jax
import jax.numpy as jnp
from jax import lax
from jax.experimental import pallas as pl
from jax.experimental.pallas import tpu as pltpu
from jax.sharding import PartitionSpec as P

SPACING = 16
NS_STEPS = 4
VMEM_LIMIT = 12 << 20


def padded(array, sides, width):
    for axis, dim in sides:
        size, length = (lax.axis_size(axis), array.shape[dim])
        up = [(i, (i + 1) % size) for i in range(size - 1)]
        down = [(j, i) for i, j in up]
        last = lax.slice_in_dim(array, length - width, length, axis=dim)
        initial = lax.slice_in_dim(array, 0, width, axis=dim)
        before = lax.ppermute(last, axis, up)
        after = lax.ppermute(initial, axis, down)
        array = jnp.concatenate([before, array, after], axis=dim)
    return array


def finish_solve(gram_matrix, projected):
    member_count = gram_matrix.shape[1]
    spread = float(member_count - 1)
    identity = jnp.eye(member_count, dtype=jnp.float32)
    scale_norm = spread + jnp.sqrt(jnp.sum(gram_matrix * gram_matrix, axis=(1, 2)))
    sqrt_iter = (spread * identity + gram_matrix) / scale_norm[:, None, None]
    inv_iter = jnp.broadcast_to(identity, sqrt_iter.shape)
    for iteration in range(NS_STEPS):
        middle = 1.5 * identity - 0.5 * jnp.einsum(
            "bij,bjk->bik", inv_iter, sqrt_iter, precision=lax.Precision.HIGHEST
        )
        sqrt_iter = jnp.einsum("bij,bjk->bik", sqrt_iter, middle, precision=lax.Precision.HIGHEST)
        inv_iter = jnp.einsum("bij,bjk->bik", middle, inv_iter, precision=lax.Precision.HIGHEST)
    inner = jnp.einsum("bij,bj->bi", inv_iter, projected, precision=lax.Precision.HIGHEST)
    mean_weights = (
        jnp.einsum("bij,bj->bi", inv_iter, inner, precision=lax.Precision.HIGHEST)
        / scale_norm[:, None]
    )
    transform = (jnp.sqrt(spread) / jnp.sqrt(scale_norm))[:, None, None] * inv_iter + mean_weights[
        :, :, None
    ]
    return transform.astype(jnp.bfloat16)


def fractions(count, half_span):
    place = jnp.arange(count)[:, None]
    within = jnp.arange(half_span)[None, :].astype(jnp.float32)
    return jnp.where(
        place % 2 == 0,
        (within + half_span + 0.5) / (2 * half_span),
        (within + 0.5) / (2 * half_span),
    )


def solve_columns(lookup, counts, local_part, flat_pert, flat_values):
    column_count, slots = lookup.shape
    member_count = flat_pert.shape[1]
    block_len = min(slots, 128)
    live_blocks = (jnp.max(counts) + block_len - 1) // block_len

    def add_block(block_index, carry):
        gram_matrix, projected = carry
        offset = block_index * block_len
        slot_rows = lax.dynamic_slice_in_dim(lookup, offset, block_len, 1)
        slot_local = lax.dynamic_slice_in_dim(local_part, offset, block_len, 1)
        position = offset + jnp.arange(block_len)
        active = position[None, :] < counts[:, None]
        pert_rows = flat_pert[slot_rows].astype(jnp.float32)
        picked = flat_values[:, slot_rows]
        precision_w = jnp.where(active, picked[1].astype(jnp.float32) * slot_local, 0.0)
        departure = picked[0].astype(jnp.float32)
        gram_matrix = gram_matrix + jnp.einsum(
            "bsk,bsm->bkm",
            pert_rows * precision_w[:, :, None],
            pert_rows,
            precision=lax.Precision.HIGHEST,
        )
        projected = projected + jnp.einsum(
            "bsk,bs->bk", pert_rows, precision_w * departure, precision=lax.Precision.HIGHEST
        )
        return (gram_matrix, projected)

    start_gram = jnp.zeros((column_count, member_count, member_count), jnp.float32)
    start_proj = jnp.zeros((column_count, member_count), jnp.float32)
    gram_matrix, projected = lax.fori_loop(0, live_blocks, add_block, (start_gram, start_proj))
    return finish_solve(gram_matrix, projected)


def clamp_edges(rimmed, axis_index, axis_count, dim):
    lower = jnp.where(
        axis_index == 0,
        lax.slice_in_dim(rimmed, 1, 2, axis=dim),
        lax.slice_in_dim(rimmed, 0, 1, axis=dim),
    )
    last = rimmed.shape[dim]
    upper = jnp.where(
        axis_index == axis_count - 1,
        lax.slice_in_dim(rimmed, last - 2, last - 1, axis=dim),
        lax.slice_in_dim(rimmed, last - 1, last, axis=dim),
    )
    return jnp.concatenate(
        [lower, lax.slice_in_dim(rimmed, 1, last - 1, axis=dim), upper], axis=dim
    )


def per_device(
    members, obs_pert, innovation, obs_precision, obs_owner, obs_slot, obs_count, local_weight
):
    scalars = jnp.stack([innovation, obs_precision])
    tile_pert, tile_values = (
        lax.all_gather(obs_pert, "lev", axis=0, tiled=True),
        lax.all_gather(scalars, "lev", axis=1, tiled=True),
    )
    near_pert, near_values = (
        padded(tile_pert[None, None], (("tx", 0), ("ty", 1)), 1),
        padded(tile_values[None, None], (("tx", 0), ("ty", 1)), 1),
    )
    tile_len = near_pert.shape[2]
    member_count = near_pert.shape[3]
    flat_pert = near_pert.reshape(9 * tile_len, member_count)
    flat_values = jnp.transpose(near_values, (2, 0, 1, 3)).reshape(2, 9 * tile_len)
    column_x = lax.axis_index("tx")
    column_y = lax.axis_index("ty")
    tiles_x = lax.axis_size("tx")
    tiles_y = lax.axis_size("ty")
    near_x = obs_owner // tiles_y - column_x + 1
    near_y = obs_owner % tiles_y - column_y + 1
    lookup = (near_x * 3 + near_y) * tile_len + obs_slot
    coarse_x, coarse_y, slots = lookup.shape
    lookup = lookup.reshape(coarse_x * coarse_y, slots)
    counts = obs_count.reshape(coarse_x * coarse_y)
    local_part = local_weight.reshape(coarse_x * coarse_y, slots)
    weights = solve_columns(lookup, counts, local_part, flat_pert, flat_values)
    weights = weights.reshape(coarse_x, coarse_y, member_count, member_count)
    rimmed = padded(weights, (("tx", 0), ("ty", 1)), 1)
    rimmed = clamp_edges(rimmed, column_x, tiles_x, 0)
    rimmed = clamp_edges(rimmed, column_y, tiles_y, 1)
    doubled = jnp.repeat(jnp.repeat(rimmed, 2, axis=0), 2, axis=1)
    level_count, width_x, width_y, _ = members.shape
    half_span = SPACING // 2
    patch_x = width_x // half_span
    patch_y = width_y // half_span
    frac_x = fractions(patch_x, half_span)
    frac_y = fractions(patch_y, half_span)
    ens_mean = jnp.mean(members, axis=3, keepdims=True, dtype=jnp.float32)
    pert = (members.astype(jnp.float32) - ens_mean).astype(jnp.bfloat16)
    patched = pert.reshape(level_count, patch_x, half_span, patch_y, half_span, member_count)
    summed = jnp.zeros(patched.shape, jnp.float32)
    for upper_x in range(2):
        for upper_y in range(2):
            corner = doubled[
                1 + 2 * upper_x : 1 + 2 * upper_x + patch_x,
                1 + 2 * upper_y : 1 + 2 * upper_y + patch_y,
            ]
            product = jnp.einsum(
                "lxaybi,xyij->lxaybj", patched, corner, preferred_element_type=jnp.float32
            )
            factor_x = frac_x if upper_x == 1 else 1.0 - frac_x
            factor_y = frac_y if upper_y == 1 else 1.0 - frac_y
            summed = (
                summed
                + product
                * factor_x[None, :, :, None, None, None]
                * factor_y[None, None, None, :, :, None]
            )
    return (ens_mean + summed.reshape(members.shape)).astype(jnp.bfloat16)


def pair_patterns(mesh_axes):
    tiles_x, tiles_y, parts = (lax.axis_size(a) for a in mesh_axes)

    def flat(x, y, l):
        return (x * tiles_y + y) * parts + l

    def table(move):
        return [
            (flat(x, y, l), flat(*move(x, y, l)))
            for x in range(tiles_x)
            for y in range(tiles_y)
            for l in range(parts)
        ]

    def climb(x, y, l):
        if l % 2 == 0:
            return (x, y + 1, l) if y < tiles_y - 1 else (x, y, l + 1)
        return (x, y - 1, l) if y > 0 else (x, y, l - 1)

    climbing = table(climb)
    return {
        "across": table(lambda x, y, l: (1 - x, y, l)),
        "core": table(lambda x, y, l: (x, y, l ^ 1)),
        "half": table(lambda x, y, l: (x, y, l ^ 2)),
        "climb": climbing,
        "descend": [(b, a) for a, b in climbing],
    }


def device_call(kernel, operands, out_shape, scratch=(), flops=0, name=None, in_hbm=False, out_hbm=False):
    single = not isinstance(out_shape, (list, tuple))
    spec = pl.BlockSpec(memory_space=pltpu.VMEM)
    hbm = pl.BlockSpec(memory_space=pltpu.HBM)
    out_spec = hbm if out_hbm else spec
    return pl.pallas_call(
        kernel,
        out_shape=out_shape,
        in_specs=[hbm if in_hbm else spec] * len(operands),
        out_specs=out_spec if single else [out_spec] * len(out_shape),
        scratch_shapes=list(scratch),
        cost_estimate=pl.CostEstimate(flops=flops, bytes_accessed=1 << 18, transcendentals=0),
        compiler_params=pltpu.CompilerParams(vmem_limit_bytes=VMEM_LIMIT),
        name=name,
    )(*operands)


def split2(value):
    high = value.astype(jnp.bfloat16)
    return high, (value - high.astype(jnp.float32)).astype(jnp.bfloat16)


def split3(value):
    high, _ = split2(value)
    rest = value - high.astype(jnp.float32)
    middle, low = split2(rest)
    return high, middle, low


def dot(a, b, dims=((1,), (0,))):
    return lax.dot_general(a, b, (dims, ((), ())), preferred_element_type=jnp.float32)


def pack_kernel(
    rows, pert, inn, prec, owner, slot, count, local, out_ref, inn_ref, prec_ref, owner_ref, slot_ref, count_ref, local_ref, tail, sems
):
    sources = (owner, slot, count, local, inn, prec, pert)
    targets = (owner_ref, slot_ref, count_ref, local_ref, inn_ref, prec_ref, out_ref.at[0:rows, :])
    copies = [pltpu.make_async_copy(x, y, sems.at[k]) for k, (x, y) in enumerate(zip(sources, targets))]
    for copy in copies:
        copy.start()
    for copy in copies[:-1]:
        copy.wait()
    edge = jnp.where(lax.axis_index("tx") == 0, owner_ref.shape[0] - 1, 0)
    slots = owner_ref.shape[2]
    limit = jnp.where(edge == 0, count_ref[0, 0], count_ref[0, owner_ref.shape[0] - 1])
    active = lax.broadcasted_iota(jnp.int32, (1, slots), 1) < limit
    local_part = jnp.where(active, local_ref[edge], 0.0)
    slot_part = slot_ref[edge]
    for k, ref in enumerate((prec_ref, inn_ref)):
        tail[2 * k : 2 * k + 2, :] = ref[...].astype(jnp.float32)
    lists = [
        owner_ref[edge].astype(jnp.float32),
        (slot_part // 128).astype(jnp.float32),
        (slot_part % 128).astype(jnp.float32),
    ] + [piece.astype(jnp.float32) for piece in split3(local_part)]
    for k, row in enumerate(lists):
        for part in range(2):
            tail[4 + 2 * k + part : 5 + 2 * k + part, :] = row[:, 128 * part : 128 * (part + 1)]
    out_ref[rows : rows + 16, :] = tail[...].astype(jnp.bfloat16)
    copies[-1].wait()


def table_kernel(rows, cols, owner_ref, slot_ref, count_ref, local_ref, other_ref, out_ref):
    tile_x, tile_y, part = (lax.axis_index(a) for a in ("tx", "ty", "lev"))
    tiles_y = lax.axis_size("ty")
    core = lax.rem(part, 2)
    own, slots = owner_ref.shape[0], owner_ref.shape[2]
    received = other_ref[rows : rows + 16, :].astype(jnp.float32)

    def listed(k):
        return jnp.concatenate([received[2 * k : 2 * k + 1, :], received[2 * k + 1 : 2 * k + 2, :]], axis=1)

    far_owner = listed(2).astype(jnp.int32)
    far_slot = (listed(3) * 128.0 + listed(4)).astype(jnp.int32)
    far_local = listed(5) + listed(6) + listed(7)
    position_in = lax.broadcasted_iota(jnp.int32, (1, slots), 1)

    def own_list(k):
        return owner_ref[k], slot_ref[k], jnp.where(position_in < count_ref[0, k], local_ref[k], 0.0)

    def pick(use_far, k):
        return tuple(jnp.where(use_far, a, b) for a, b in zip((far_owner, far_slot, far_local), own_list(k)))

    lists = [pick(tile_x > 0, 0)] + [own_list(k) for k in range(own)] + [pick(tile_x == 0, own - 1)]
    half = cols // 2
    out_ref[...] = jnp.zeros_like(out_ref)
    for g, (owner, slot, local) in enumerate(lists):
        across = jnp.where(owner // tiles_y == tile_x, 0, 1)
        near = owner % tiles_y - tile_y
        first_way = jnp.where(core == 0, -1, 1)
        block = across * 3 + jnp.where(near == 0, 0, jnp.where(near == first_way, 1, 2))
        mine = slot // rows == part
        within = slot % rows
        high = jnp.where(mine, block * (rows // 128) + within // 128, -1)
        low = within % 128
        picked = jnp.where(lax.broadcasted_iota(jnp.int32, (16, slots), 0) == high, local, 0.0)
        hot = jnp.where(lax.broadcasted_iota(jnp.int32, (128, slots), 0) == low, 1.0, 0.0).astype(jnp.bfloat16)
        parts = split3(picked)
        total = dot(parts[0], hot, ((1,), (1,)))
        for piece in parts[1:]:
            total = total + dot(piece, hot, ((1,), (1,)))
        place = lax.rem(g - core * half + cols, cols)
        out_ref[pl.ds(place, 16, stride=8), :] = total


def gram_blocks(rows, cols, first, blocks, table_ref, turned, plain, scaled):
    per = rows // 128
    products, weights = [], []
    for k, ref in enumerate(blocks):
        tail = ref[rows : rows + 16, :].astype(jnp.float32)
        for part in range(per):
            hi = (first + k) * per + part
            row = table_ref[8 * hi : 8 * hi + 8, :] * tail[part : part + 1, :]
            weights.append(row)
            products.append(row * tail[per + part : per + part + 1, :])
        block = ref[0:rows, :]
        plain[rows * k : rows * (k + 1), :] = block
        turned[:, rows * k : rows * (k + 1)] = block.astype(jnp.float32).T
    weight = jnp.concatenate(weights, axis=1)
    high, low = split2(jnp.concatenate(products, axis=1))
    for position in range(cols):
        at = 128 * position
        scaled[at : at + 128, :] = (turned[...] * weight[position : position + 1, :]).astype(jnp.bfloat16)
    at = 128 * cols
    scaled[at : at + 16, :] = jnp.concatenate(
        [high.astype(jnp.float32), low.astype(jnp.float32)], axis=0
    ).astype(jnp.bfloat16)
    return dot(scaled[...], plain[...])


def gram_near_kernel(rows, cols, table_ref, b0, b1, b2, b3, out_ref, turned, plain, scaled):
    out_ref[...] = gram_blocks(rows, cols, 0, [b0, b1, b2, b3], table_ref, turned, plain, scaled)


def gram_next_kernel(rows, cols, first, table_ref, so_far_ref, block, out_ref, turned, plain, scaled):
    out_ref[...] = so_far_ref[...] + gram_blocks(rows, cols, first, [block], table_ref, turned, plain, scaled)


def gram_last_kernel(rows, cols, first, table_ref, so_far_ref, block, mine_ref, rest_ref, turned, plain, scaled):
    half = cols // 2
    total = so_far_ref[...] + gram_blocks(rows, cols, first, [block], table_ref, turned, plain, scaled)
    edge = 128 * half
    projected = total[2 * edge : 2 * edge + 8] + total[2 * edge + 8 : 2 * edge + 16]
    mine_ref[0:edge, :] = total[0:edge]
    rest_ref[0:edge, :] = total[edge : 2 * edge]
    mine_ref[edge : edge + 8, :] = projected
    rest_ref[edge : edge + 8, :] = jnp.concatenate(
        [projected[half : 2 * half], jnp.zeros((8 - half, 128), jnp.float32)], axis=0
    )


def lanes_from(lane, values, others=0.0):
    return jnp.where(lax.broadcasted_iota(jnp.int32, values.shape, 1) >= lane, values, others)


def fold(grams):
    top = [g[0:32] for g in grams]
    sides = [lanes_from(32, g[32:64], pltpu.roll(g[96:128], 32, 1)) for g in grams]
    third = [g[64:96] for g in grams]
    return above(*top, *sides, lanes_from(64, third[0], pltpu.roll(third[1], 64, 1)), third[2])


def unfold(folded, k, eye):
    side = folded[96 + 32 * k : 128 + 32 * k]
    third = folded[192:224] if k < 2 else folded[224:256]
    third = pltpu.roll(third, 64, 1) if k == 1 else third
    upper_part = above(
        folded[32 * k : 32 * k + 32],
        lanes_from(32, side),
        lanes_from(64, third),
        lanes_from(96, pltpu.roll(side, 96, 1)),
    )
    turned = dot(eye.astype(jnp.bfloat16), upper_part.astype(jnp.bfloat16), ((1,), (1,)))
    below = lax.broadcasted_iota(jnp.int32, eye.shape, 0) // 32 > lax.broadcasted_iota(jnp.int32, eye.shape, 1) // 32
    return jnp.where(below, turned, upper_part)


def join_kernel(half, mine_ref, got_ref, sum_ref, send_ref):
    total = mine_ref[...] + got_ref[...]
    sum_ref[...] = total
    edge = 128 * half
    folded = fold([total[128 * k : 128 * (k + 1)] for k in range(half)])
    high, low = split2(total[edge : edge + 8])
    send_ref[...] = above(folded, high.astype(jnp.float32), low.astype(jnp.float32)).astype(jnp.bfloat16)


def beside(*pieces):
    return jnp.concatenate(pieces, axis=1)


def above(*pieces):
    return jnp.concatenate(pieces, axis=0)


def product(a, b):
    (a_high, a_low), (b_high, b_low) = a, b
    return dot(beside(a_high, a_low), above(b_high, b_high)) + dot(a_high, b_low)


def solve_kernel(half, sum_ref, got_ref, out_ref):
    size = 128
    spread = float(size - 1)
    eye = jnp.where(
        lax.broadcasted_iota(jnp.int32, (size, size), 0) == lax.broadcasted_iota(jnp.int32, (size, size), 1),
        1.0,
        0.0,
    )
    edge = size * half
    got = got_ref[...].astype(jnp.float32)
    projected = sum_ref[edge : edge + 8, :] + got[256:264] + got[264:272]
    norms, bases = [], []
    for k in range(half):
        gram = sum_ref[size * k : size * (k + 1), :] + unfold(got, k, eye)
        squared = jnp.sum(jnp.sum(gram * gram, axis=0, keepdims=True), axis=1, keepdims=True)
        norm = spread + jnp.sqrt(squared)
        norms.append(norm)
        bases.append((spread * eye + gram) / norm)
    base_parts = [split2(base) for base in bases]
    squares = [dot(high, high) for high, _ in base_parts]
    inverses = [
        1.5 * (1.5 * eye - 0.5 * base)
        - 0.5
        * dot(
            (1.5 * base - 0.5 * square).astype(jnp.bfloat16),
            (2.25 * eye - 1.5 * base + 0.25 * square).astype(jnp.bfloat16),
        )
        for base, square in zip(bases, squares)
    ]
    for _ in range(NS_STEPS - 2):
        inverse_parts = [split2(z) for z in inverses]
        both = [
            product(z, (beside(b[0], z[0]), beside(b[1], z[1]))) for b, z in zip(base_parts, inverse_parts)
        ]
        inverses = [
            1.5 * z - 0.5 * product(split2(x[:, 0:size]), split2(x[:, size : 2 * size])) for z, x in zip(inverses, both)
        ]
    for k in range(half):
        inverse, norm = inverses[k], norms[k]
        parts = split2(inverse)
        vector = split3(jnp.broadcast_to(projected[k : k + 1, :], (16, size)))
        inner = jnp.zeros((16, size), jnp.float32)
        for piece in vector[:2]:
            for part in parts:
                inner = inner + dot(piece, part, ((1,), (1,)))
        mean_weights = jnp.sum(inverse * inner[0:1, :], axis=1, keepdims=True) / norm
        transform = (jnp.sqrt(spread) / jnp.sqrt(norm)) * inverse + mean_weights
        out_ref[size * k : size * (k + 1), :] = transform.astype(jnp.bfloat16)


def shares(levels, size):
    span = SPACING // 2
    shape = (1, span, span, size)
    along_x = lax.broadcasted_iota(jnp.int32, shape, 1).astype(jnp.float32) / (2 * span)
    along_y = lax.broadcasted_iota(jnp.int32, shape, 2).astype(jnp.float32) / (2 * span)
    upper_y = [along_y + (span + 0.5) / (2 * span), along_y + 0.5 / (2 * span)]
    return along_x, upper_y


def mixed(both, share, upper_x, shape):
    high = share * upper_x
    return (share - high) * both[:, 0:128].reshape(shape) + high * both[:, 128:256].reshape(shape)


def near_kernel(cols, members_ref, own, pair, part_ref, pert_ref, table):
    half = cols // 2
    first = lax.rem(lax.axis_index("lev"), 2) == 0
    for j in range(half):
        rows = pl.ds(128 * j, 128)
        a, b = own[rows, :], pair[rows, :]
        table[:, 128 * j : 128 * (j + 1)] = jnp.where(first, a, b)
        table[:, 128 * (j + half) : 128 * (j + half + 1)] = jnp.where(first, b, a)
    levels, width_x, width_y, size = members_ref.shape
    span = SPACING // 2
    shape = (levels, span, span, size)
    rows = levels * span * span
    along_x, upper_y = shares(levels, size)
    for patch_x in range(width_x // span):
        states = members_ref[:, patch_x * span : (patch_x + 1) * span, :, :].astype(jnp.float32)
        mean = jnp.sum(states, axis=3, keepdims=True) * (1.0 / size)
        moved = states - mean
        column = (patch_x + 1) // 2
        upper_x = along_x + (span + 0.5 if patch_x % 2 == 0 else 0.5) / (2 * span)
        for patch_y in range(2):
            inside = slice(patch_y * span, (patch_y + 1) * span)
            left = moved[:, :, inside, :].reshape(rows, size).astype(jnp.bfloat16)
            pert_ref[patch_x, patch_y] = left
            both = dot(left, table[:, 128 * column : 128 * (column + 2)])
            share = upper_y[0] if patch_y == 0 else 1.0 - upper_y[1]
            part_ref[patch_x, patch_y] = (mean[:, :, inside, :] + mixed(both, share, upper_x, shape)).reshape(rows, size)


def add_far(first_patch, count, first_column, table, part_ref, pert_ref, keep):
    levels, size = part_ref.shape[2] // (SPACING // 2) ** 2, part_ref.shape[3]
    span = SPACING // 2
    shape = (levels, span, span, size)
    along_x, upper_y = shares(levels, size)
    for k in range(count):
        patch_x = first_patch + k
        column = lax.div(patch_x + 1, 2) - first_column
        lanes = pl.ds(pl.multiple_of(128 * column, 128), 256)
        upper_x = along_x + jnp.where(lax.rem(patch_x, 2) == 0, span + 0.5, 0.5) / (2 * span)
        results = []
        for patch_y in range(2):
            both = dot(pert_ref[patch_x, patch_y], table[patch_y, :, lanes])
            share = 1.0 - upper_y[0] if patch_y == 0 else upper_y[1]
            results.append(part_ref[patch_x, patch_y].reshape(shape) + mixed(both, share, upper_x, shape))
        keep(k, patch_x, jnp.concatenate(results, axis=2).astype(jnp.bfloat16))


def neighbours(climb, descend, own, first, rows):
    tile_y = lax.axis_index("ty")
    up, down, mine = climb[rows, :], descend[rows, :], own[rows, :]
    before = jnp.where(tile_y == 0, mine, jnp.where(first, up, down))
    after = jnp.where(tile_y == lax.axis_size("ty") - 1, mine, jnp.where(first, down, up))
    return before, after


def far_first_kernel(cols, count, part_ref, pert_ref, own, climb, descend, out_ref, table):
    half, span = cols // 2, SPACING // 2
    core = lax.rem(lax.axis_index("lev"), 2)
    for j in range(half):
        for z, value in enumerate(neighbours(climb, descend, own, core == 0, pl.ds(128 * j, 128))):
            table[z, :, 128 * j : 128 * (j + 1)] = value

    def keep(k, _, value):
        out_ref[:, k * span : (k + 1) * span] = value

    add_far(core * (part_ref.shape[0] - count), count, core * half, table, part_ref, pert_ref, keep)


def far_rest_kernel(
    cols, count, part_ref, pert_ref, own, pair, climb, descend, pair_climb, pair_descend, begun, out_hbm, table, staged, sems
):
    half, span = cols // 2, SPACING // 2
    core = lax.rem(lax.axis_index("lev"), 2)
    first = core == 0
    total = part_ref.shape[0]
    early = total - count
    start = core * (total - early) * span
    copies = [pltpu.make_async_copy(begun, out_hbm.at[:, pl.ds(start, early * span)], sems.at[count])]
    copies[0].start()
    for j in range(half):
        at = pl.multiple_of(128 * j + jnp.where(first, 128, 0), 128)
        values = neighbours(pair_climb, pair_descend, pair, jnp.logical_not(first), pl.ds(128 * j, 128))
        for z, value in enumerate(values):
            table[z, :, pl.ds(at, 128)] = value
    border = pl.ds(pl.multiple_of(jnp.where(first, 128 * (half - 1), 0), 128), 128)
    at = pl.multiple_of(jnp.where(first, 0, 128 * half), 128)
    for z, value in enumerate(neighbours(climb, descend, own, first, border)):
        table[z, :, pl.ds(at, 128)] = value

    def keep(k, patch_x, value):
        inside = pl.ds(patch_x * span, span)
        staged[:, inside] = value
        copies.append(pltpu.make_async_copy(staged.at[:, inside], out_hbm.at[:, inside], sems.at[k]))
        copies[-1].start()

    first_column = jnp.where(first, half - 1, 0)
    add_far((1 - core) * early, count, first_column, table, part_ref, pert_ref, keep)
    for copy in copies:
        copy.wait()


def paired_device(
    members, obs_pert, innovation, obs_precision, obs_owner, obs_slot, obs_count, local_weight
):
    axes = ("tx", "ty", "lev")
    ways = pair_patterns(axes)

    def send(value, way):
        return lax.ppermute(value, axes, ways[way])

    bf16, f32 = jnp.bfloat16, jnp.float32
    rows, size = obs_pert.shape
    cols = obs_owner.shape[0] + 2
    half = cols // 2
    shape = jax.ShapeDtypeStruct
    counts = obs_count.reshape(1, -1)
    lists = (obs_owner, obs_slot, counts, local_weight)
    scalars = [v.reshape(rows // size, size) for v in (innovation, obs_precision)]
    packed = device_call(
        functools.partial(pack_kernel, rows),
        tuple(pltpu.with_memory_space_constraint(v, pltpu.HBM) for v in (obs_pert, *scalars, *lists)),
        shape((rows + 16, size), bf16),
        [pltpu.VMEM(v.shape, v.dtype) for v in scalars]
        + [
            pltpu.VMEM(obs_owner.shape, jnp.int32),
            pltpu.VMEM(obs_slot.shape, jnp.int32),
            pltpu.SMEM(counts.shape, jnp.int32),
            pltpu.VMEM(local_weight.shape, f32),
            pltpu.VMEM((16, size), f32),
            pltpu.SemaphoreType.DMA((7,)),
        ],
        name="pack",
        in_hbm=True,
    )
    across = send(packed, "across")
    climb, descend = send(packed, "climb"), send(packed, "descend")
    across_climb, across_descend = send(across, "climb"), send(across, "descend")
    table = device_call(
        functools.partial(table_kernel, rows, cols),
        (*lists, across),
        shape((128, 128), f32),
        flops=6 * 2 * 48 * 256 * 128,
        name="table",
    )
    tall = size * cols + 16
    near = device_call(
        functools.partial(gram_near_kernel, rows, cols),
        (table, packed, climb, descend, across),
        shape((tall, size), f32),
        [
            pltpu.VMEM((size, 4 * rows), f32),
            pltpu.VMEM((4 * rows, size), bf16),
            pltpu.VMEM((tall, 4 * rows), bf16),
        ],
        flops=2 * tall * size * 4 * rows,
        name="gram_near",
    )
    block_scratch = [
        pltpu.VMEM((size, rows), f32),
        pltpu.VMEM((rows, size), bf16),
        pltpu.VMEM((tall, rows), bf16),
    ]
    near = device_call(
        functools.partial(gram_next_kernel, rows, cols, 5),
        (table, near, across_descend),
        shape((tall, size), f32),
        block_scratch,
        flops=2 * tall * size * rows,
        name="gram_next",
    )
    mine, rest = device_call(
        functools.partial(gram_last_kernel, rows, cols, 4),
        (table, near, across_climb),
        [shape((size * half + 8, size), f32)] * 2,
        block_scratch,
        flops=2 * tall * size * rows,
        name="gram_last",
    )
    total, half_sum = device_call(
        functools.partial(join_kernel, half),
        (mine, send(rest, "core")),
        [shape((size * half + 8, size), f32), shape((272, size), bf16)],
        name="join",
    )
    weights = device_call(
        functools.partial(solve_kernel, half),
        (total, send(half_sum, "half")),
        shape((size * half, size), bf16),
        flops=2 * 27 * half * size**3,
        name="solve",
    )
    pair = send(weights, "core")
    up, down = send(weights, "climb"), send(weights, "descend")
    levels, width_x, width_y, _ = members.shape
    patches = (width_x * 2 // SPACING, 2, levels * SPACING**2 // 4, size)
    part, pert = device_call(
        functools.partial(near_kernel, cols),
        (members, weights, pair),
        [shape(patches, f32), shape(patches, bf16)],
        [pltpu.VMEM((size, cols * size), bf16)],
        flops=2 * levels * width_x * width_y * size * 2 * size,
        name="apply_near",
    )
    up, down, part = lax.optimization_barrier((up, down, part))
    pair_up, pair_down = send(up, "core"), send(down, "core")
    early, span = cols // 2, SPACING // 2
    begun = device_call(
        functools.partial(far_first_kernel, cols, early),
        (part, pert, weights, up, down),
        shape((levels, early * span, width_y, size), bf16),
        [pltpu.VMEM((2, size, half * size), bf16)],
        flops=2 * levels * span * early * width_y * size * 2 * size,
        name="far_first",
    )
    count = patches[0] - early
    return device_call(
        functools.partial(far_rest_kernel, cols, count),
        (part, pert, weights, pair, up, down, pair_up, pair_down, begun),
        shape(members.shape, bf16),
        [
            pltpu.VMEM((2, size, (half + 1) * size), bf16),
            pltpu.VMEM(members.shape, bf16),
            pltpu.SemaphoreType.DMA((count + 1,)),
        ],
        flops=2 * levels * span * count * width_y * size * 2 * size,
        name="far_rest",
        out_hbm=True,
    )


def fits_pairs(mesh, members, obs_pert, obs_owner):
    sizes = dict(mesh.shape)
    return (
        sizes["tx"] == 2
        and sizes["lev"] == 4
        and obs_pert == (256, 128)
        and obs_owner == (4, 1, 256)
        and members[1:] == (64, 16, 128)
    )


def solution(mesh):
    placed = (
        P("lev", "tx", "ty", None),
        P(("tx", "ty", "lev"), None),
        P(("tx", "ty", "lev")),
        P(("tx", "ty", "lev")),
        P("tx", "ty", None),
        P("tx", "ty", None),
        P("tx", "ty"),
        P("tx", "ty", None),
    )

    def local(members, obs_pert, innovation, obs_precision, obs_owner, *rest):
        paired = fits_pairs(mesh, members.shape, obs_pert.shape, obs_owner.shape)
        return (paired_device if paired else per_device)(
            members, obs_pert, innovation, obs_precision, obs_owner, *rest
        )

    return jax.shard_map(
        local,
        mesh=mesh,
        in_specs=placed,
        out_specs=P("lev", "tx", "ty", None),
        check_vma=False,
    )
```

```python
import functools

import jax
import jax.numpy as jnp
from jax import lax
from jax.experimental import pallas as pl
from jax.experimental.pallas import tpu as pltpu
from jax.sharding import PartitionSpec as P

SPACING = 16
NS_STEPS = 4
VMEM_LIMIT = 12 << 20


def padded(array, sides, width):
    for axis, dim in sides:
        size, length = (lax.axis_size(axis), array.shape[dim])
        up = [(i, (i + 1) % size) for i in range(size - 1)]
        down = [(j, i) for i, j in up]
        last = lax.slice_in_dim(array, length - width, length, axis=dim)
        initial = lax.slice_in_dim(array, 0, width, axis=dim)
        before = lax.ppermute(last, axis, up)
        after = lax.ppermute(initial, axis, down)
        array = jnp.concatenate([before, array, after], axis=dim)
    return array


def finish_solve(gram_matrix, projected):
    member_count = gram_matrix.shape[1]
    spread = float(member_count - 1)
    identity = jnp.eye(member_count, dtype=jnp.float32)
    scale_norm = spread + jnp.sqrt(jnp.sum(gram_matrix * gram_matrix, axis=(1, 2)))
    sqrt_iter = (spread * identity + gram_matrix) / scale_norm[:, None, None]
    inv_iter = jnp.broadcast_to(identity, sqrt_iter.shape)
    for iteration in range(NS_STEPS):
        middle = 1.5 * identity - 0.5 * jnp.einsum(
            "bij,bjk->bik", inv_iter, sqrt_iter, precision=lax.Precision.HIGHEST
        )
        sqrt_iter = jnp.einsum("bij,bjk->bik", sqrt_iter, middle, precision=lax.Precision.HIGHEST)
        inv_iter = jnp.einsum("bij,bjk->bik", middle, inv_iter, precision=lax.Precision.HIGHEST)
    inner = jnp.einsum("bij,bj->bi", inv_iter, projected, precision=lax.Precision.HIGHEST)
    mean_weights = (
        jnp.einsum("bij,bj->bi", inv_iter, inner, precision=lax.Precision.HIGHEST)
        / scale_norm[:, None]
    )
    transform = (jnp.sqrt(spread) / jnp.sqrt(scale_norm))[:, None, None] * inv_iter + mean_weights[
        :, :, None
    ]
    return transform.astype(jnp.bfloat16)


def fractions(count, half_span):
    place = jnp.arange(count)[:, None]
    within = jnp.arange(half_span)[None, :].astype(jnp.float32)
    return jnp.where(
        place % 2 == 0,
        (within + half_span + 0.5) / (2 * half_span),
        (within + 0.5) / (2 * half_span),
    )


def solve_columns(lookup, counts, local_part, flat_pert, flat_values):
    column_count, slots = lookup.shape
    member_count = flat_pert.shape[1]
    block_len = min(slots, 128)
    live_blocks = (jnp.max(counts) + block_len - 1) // block_len

    def add_block(block_index, carry):
        gram_matrix, projected = carry
        offset = block_index * block_len
        slot_rows = lax.dynamic_slice_in_dim(lookup, offset, block_len, 1)
        slot_local = lax.dynamic_slice_in_dim(local_part, offset, block_len, 1)
        position = offset + jnp.arange(block_len)
        active = position[None, :] < counts[:, None]
        pert_rows = flat_pert[slot_rows].astype(jnp.float32)
        picked = flat_values[:, slot_rows]
        precision_w = jnp.where(active, picked[1].astype(jnp.float32) * slot_local, 0.0)
        departure = picked[0].astype(jnp.float32)
        gram_matrix = gram_matrix + jnp.einsum(
            "bsk,bsm->bkm",
            pert_rows * precision_w[:, :, None],
            pert_rows,
            precision=lax.Precision.HIGHEST,
        )
        projected = projected + jnp.einsum(
            "bsk,bs->bk", pert_rows, precision_w * departure, precision=lax.Precision.HIGHEST
        )
        return (gram_matrix, projected)

    start_gram = jnp.zeros((column_count, member_count, member_count), jnp.float32)
    start_proj = jnp.zeros((column_count, member_count), jnp.float32)
    gram_matrix, projected = lax.fori_loop(0, live_blocks, add_block, (start_gram, start_proj))
    return finish_solve(gram_matrix, projected)


def clamp_edges(rimmed, axis_index, axis_count, dim):
    lower = jnp.where(
        axis_index == 0,
        lax.slice_in_dim(rimmed, 1, 2, axis=dim),
        lax.slice_in_dim(rimmed, 0, 1, axis=dim),
    )
    last = rimmed.shape[dim]
    upper = jnp.where(
        axis_index == axis_count - 1,
        lax.slice_in_dim(rimmed, last - 2, last - 1, axis=dim),
        lax.slice_in_dim(rimmed, last - 1, last, axis=dim),
    )
    return jnp.concatenate(
        [lower, lax.slice_in_dim(rimmed, 1, last - 1, axis=dim), upper], axis=dim
    )


def per_device(
    members, obs_pert, innovation, obs_precision, obs_owner, obs_slot, obs_count, local_weight
):
    scalars = jnp.stack([innovation, obs_precision])
    tile_pert, tile_values = (
        lax.all_gather(obs_pert, "lev", axis=0, tiled=True),
        lax.all_gather(scalars, "lev", axis=1, tiled=True),
    )
    near_pert, near_values = (
        padded(tile_pert[None, None], (("tx", 0), ("ty", 1)), 1),
        padded(tile_values[None, None], (("tx", 0), ("ty", 1)), 1),
    )
    tile_len = near_pert.shape[2]
    member_count = near_pert.shape[3]
    flat_pert = near_pert.reshape(9 * tile_len, member_count)
    flat_values = jnp.transpose(near_values, (2, 0, 1, 3)).reshape(2, 9 * tile_len)
    column_x = lax.axis_index("tx")
    column_y = lax.axis_index("ty")
    tiles_x = lax.axis_size("tx")
    tiles_y = lax.axis_size("ty")
    near_x = obs_owner // tiles_y - column_x + 1
    near_y = obs_owner % tiles_y - column_y + 1
    lookup = (near_x * 3 + near_y) * tile_len + obs_slot
    coarse_x, coarse_y, slots = lookup.shape
    lookup = lookup.reshape(coarse_x * coarse_y, slots)
    counts = obs_count.reshape(coarse_x * coarse_y)
    local_part = local_weight.reshape(coarse_x * coarse_y, slots)
    weights = solve_columns(lookup, counts, local_part, flat_pert, flat_values)
    weights = weights.reshape(coarse_x, coarse_y, member_count, member_count)
    rimmed = padded(weights, (("tx", 0), ("ty", 1)), 1)
    rimmed = clamp_edges(rimmed, column_x, tiles_x, 0)
    rimmed = clamp_edges(rimmed, column_y, tiles_y, 1)
    doubled = jnp.repeat(jnp.repeat(rimmed, 2, axis=0), 2, axis=1)
    level_count, width_x, width_y, _ = members.shape
    half_span = SPACING // 2
    patch_x = width_x // half_span
    patch_y = width_y // half_span
    frac_x = fractions(patch_x, half_span)
    frac_y = fractions(patch_y, half_span)
    ens_mean = jnp.mean(members, axis=3, keepdims=True, dtype=jnp.float32)
    pert = (members.astype(jnp.float32) - ens_mean).astype(jnp.bfloat16)
    patched = pert.reshape(level_count, patch_x, half_span, patch_y, half_span, member_count)
    summed = jnp.zeros(patched.shape, jnp.float32)
    for upper_x in range(2):
        for upper_y in range(2):
            corner = doubled[
                1 + 2 * upper_x : 1 + 2 * upper_x + patch_x,
                1 + 2 * upper_y : 1 + 2 * upper_y + patch_y,
            ]
            product = jnp.einsum(
                "lxaybi,xyij->lxaybj", patched, corner, preferred_element_type=jnp.float32
            )
            factor_x = frac_x if upper_x == 1 else 1.0 - frac_x
            factor_y = frac_y if upper_y == 1 else 1.0 - frac_y
            summed = (
                summed
                + product
                * factor_x[None, :, :, None, None, None]
                * factor_y[None, None, None, :, :, None]
            )
    return (ens_mean + summed.reshape(members.shape)).astype(jnp.bfloat16)


def pair_patterns(mesh_axes):
    tiles_x, tiles_y, parts = (lax.axis_size(a) for a in mesh_axes)

    def flat(x, y, l):
        return (x * tiles_y + y) * parts + l

    def table(move):
        return [
            (flat(x, y, l), flat(*move(x, y, l)))
            for x in range(tiles_x)
            for y in range(tiles_y)
            for l in range(parts)
        ]

    def climb(x, y, l):
        if l % 2 == 0:
            return (x, y + 1, l) if y < tiles_y - 1 else (x, y, l + 1)
        return (x, y - 1, l) if y > 0 else (x, y, l - 1)

    climbing = table(climb)
    return {
        "across": table(lambda x, y, l: (1 - x, y, l)),
        "core": table(lambda x, y, l: (x, y, l ^ 1)),
        "half": table(lambda x, y, l: (x, y, l ^ 2)),
        "climb": climbing,
        "descend": [(b, a) for a, b in climbing],
    }


def device_call(kernel, operands, out_shape, scratch=(), flops=0, name=None, in_hbm=False, out_hbm=False):
    single = not isinstance(out_shape, (list, tuple))
    spec = pl.BlockSpec(memory_space=pltpu.VMEM)
    hbm = pl.BlockSpec(memory_space=pltpu.HBM)
    out_spec = hbm if out_hbm else spec
    return pl.pallas_call(
        kernel,
        out_shape=out_shape,
        in_specs=[hbm if in_hbm else spec] * len(operands),
        out_specs=out_spec if single else [out_spec] * len(out_shape),
        scratch_shapes=list(scratch),
        cost_estimate=pl.CostEstimate(flops=flops, bytes_accessed=1 << 18, transcendentals=0),
        compiler_params=pltpu.CompilerParams(vmem_limit_bytes=VMEM_LIMIT),
        name=name,
    )(*operands)


def split2(value):
    high = value.astype(jnp.bfloat16)
    return high, (value - high.astype(jnp.float32)).astype(jnp.bfloat16)


def split3(value):
    high, _ = split2(value)
    rest = value - high.astype(jnp.float32)
    middle, low = split2(rest)
    return high, middle, low


def dot(a, b, dims=((1,), (0,))):
    return lax.dot_general(a, b, (dims, ((), ())), preferred_element_type=jnp.float32)


def pack_kernel(
    rows, pert, inn, prec, owner, slot, count, local, out_ref, inn_ref, prec_ref, owner_ref, slot_ref, count_ref, local_ref, tail, sems
):
    sources = (owner, slot, count, local, inn, prec, pert)
    targets = (owner_ref, slot_ref, count_ref, local_ref, inn_ref, prec_ref, out_ref.at[0:rows, :])
    copies = [pltpu.make_async_copy(x, y, sems.at[k]) for k, (x, y) in enumerate(zip(sources, targets))]
    for copy in copies:
        copy.start()
    for copy in copies[:-1]:
        copy.wait()
    edge = jnp.where(lax.axis_index("tx") == 0, owner_ref.shape[0] - 1, 0)
    slots = owner_ref.shape[2]
    limit = jnp.where(edge == 0, count_ref[0, 0], count_ref[0, owner_ref.shape[0] - 1])
    active = lax.broadcasted_iota(jnp.int32, (1, slots), 1) < limit
    local_part = jnp.where(active, local_ref[edge], 0.0)
    slot_part = slot_ref[edge]
    for k, ref in enumerate((prec_ref, inn_ref)):
        tail[2 * k : 2 * k + 2, :] = ref[...].astype(jnp.float32)
    lists = [
        owner_ref[edge].astype(jnp.float32),
        (slot_part // 128).astype(jnp.float32),
        (slot_part % 128).astype(jnp.float32),
    ] + [piece.astype(jnp.float32) for piece in split3(local_part)]
    for k, row in enumerate(lists):
        for part in range(2):
            tail[4 + 2 * k + part : 5 + 2 * k + part, :] = row[:, 128 * part : 128 * (part + 1)]
    out_ref[rows : rows + 16, :] = tail[...].astype(jnp.bfloat16)
    copies[-1].wait()


def table_kernel(rows, cols, owner_ref, slot_ref, count_ref, local_ref, other_ref, out_ref):
    tile_x, tile_y, part = (lax.axis_index(a) for a in ("tx", "ty", "lev"))
    tiles_y = lax.axis_size("ty")
    core = lax.rem(part, 2)
    own, slots = owner_ref.shape[0], owner_ref.shape[2]
    received = other_ref[rows : rows + 16, :].astype(jnp.float32)

    def listed(k):
        return jnp.concatenate([received[2 * k : 2 * k + 1, :], received[2 * k + 1 : 2 * k + 2, :]], axis=1)

    far_owner = listed(2).astype(jnp.int32)
    far_slot = (listed(3) * 128.0 + listed(4)).astype(jnp.int32)
    far_local = listed(5) + listed(6) + listed(7)
    position_in = lax.broadcasted_iota(jnp.int32, (1, slots), 1)

    def own_list(k):
        return owner_ref[k], slot_ref[k], jnp.where(position_in < count_ref[0, k], local_ref[k], 0.0)

    def pick(use_far, k):
        return tuple(jnp.where(use_far, a, b) for a, b in zip((far_owner, far_slot, far_local), own_list(k)))

    lists = [pick(tile_x > 0, 0)] + [own_list(k) for k in range(own)] + [pick(tile_x == 0, own - 1)]
    half = cols // 2
    out_ref[...] = jnp.zeros_like(out_ref)
    for g, (owner, slot, local) in enumerate(lists):
        across = jnp.where(owner // tiles_y == tile_x, 0, 1)
        near = owner % tiles_y - tile_y
        first_way = jnp.where(core == 0, -1, 1)
        block = across * 3 + jnp.where(near == 0, 0, jnp.where(near == first_way, 1, 2))
        mine = slot // rows == part
        within = slot % rows
        high = jnp.where(mine, block * (rows // 128) + within // 128, -1)
        low = within % 128
        picked = jnp.where(lax.broadcasted_iota(jnp.int32, (16, slots), 0) == high, local, 0.0)
        hot = jnp.where(lax.broadcasted_iota(jnp.int32, (128, slots), 0) == low, 1.0, 0.0).astype(jnp.bfloat16)
        parts = split3(picked)
        total = dot(parts[0], hot, ((1,), (1,)))
        for piece in parts[1:]:
            total = total + dot(piece, hot, ((1,), (1,)))
        place = lax.rem(g - core * half + cols, cols)
        out_ref[pl.ds(place, 16, stride=8), :] = total


def gram_blocks(rows, cols, first, blocks, table_ref, turned, plain, scaled):
    per = rows // 128
    products, weights = [], []
    for k, ref in enumerate(blocks):
        tail = ref[rows : rows + 16, :].astype(jnp.float32)
        for part in range(per):
            hi = (first + k) * per + part
            row = table_ref[8 * hi : 8 * hi + 8, :] * tail[part : part + 1, :]
            weights.append(row)
            products.append(row * tail[per + part : per + part + 1, :])
        block = ref[0:rows, :]
        plain[rows * k : rows * (k + 1), :] = block
        turned[:, rows * k : rows * (k + 1)] = block.astype(jnp.float32).T
    weight = jnp.concatenate(weights, axis=1)
    high, low = split2(jnp.concatenate(products, axis=1))
    for position in range(cols):
        at = 128 * position
        scaled[at : at + 128, :] = (turned[...] * weight[position : position + 1, :]).astype(jnp.bfloat16)
    at = 128 * cols
    scaled[at : at + 16, :] = jnp.concatenate(
        [high.astype(jnp.float32), low.astype(jnp.float32)], axis=0
    ).astype(jnp.bfloat16)
    return dot(scaled[...], plain[...])


def gram_near_kernel(rows, cols, table_ref, b0, b1, b2, b3, out_ref, turned, plain, scaled):
    out_ref[...] = gram_blocks(rows, cols, 0, [b0, b1, b2, b3], table_ref, turned, plain, scaled)


def gram_next_kernel(rows, cols, first, table_ref, so_far_ref, block, out_ref, turned, plain, scaled):
    out_ref[...] = so_far_ref[...] + gram_blocks(rows, cols, first, [block], table_ref, turned, plain, scaled)


def gram_last_kernel(rows, cols, first, table_ref, so_far_ref, block, mine_ref, rest_ref, turned, plain, scaled):
    half = cols // 2
    total = so_far_ref[...] + gram_blocks(rows, cols, first, [block], table_ref, turned, plain, scaled)
    edge = 128 * half
    projected = total[2 * edge : 2 * edge + 8] + total[2 * edge + 8 : 2 * edge + 16]
    mine_ref[0:edge, :] = total[0:edge]
    rest_ref[0:edge, :] = total[edge : 2 * edge]
    mine_ref[edge : edge + 8, :] = projected
    rest_ref[edge : edge + 8, :] = jnp.concatenate(
        [projected[half : 2 * half], jnp.zeros((8 - half, 128), jnp.float32)], axis=0
    )


def lanes_from(lane, values, others=0.0):
    return jnp.where(lax.broadcasted_iota(jnp.int32, values.shape, 1) >= lane, values, others)


def fold(grams):
    top = [g[0:32] for g in grams]
    sides = [lanes_from(32, g[32:64], pltpu.roll(g[96:128], 32, 1)) for g in grams]
    third = [g[64:96] for g in grams]
    return above(*top, *sides, lanes_from(64, third[0], pltpu.roll(third[1], 64, 1)), third[2])


def unfold(folded, k, eye):
    side = folded[96 + 32 * k : 128 + 32 * k]
    third = folded[192:224] if k < 2 else folded[224:256]
    third = pltpu.roll(third, 64, 1) if k == 1 else third
    upper_part = above(
        folded[32 * k : 32 * k + 32],
        lanes_from(32, side),
        lanes_from(64, third),
        lanes_from(96, pltpu.roll(side, 96, 1)),
    )
    turned = dot(eye.astype(jnp.bfloat16), upper_part.astype(jnp.bfloat16), ((1,), (1,)))
    below = lax.broadcasted_iota(jnp.int32, eye.shape, 0) // 32 > lax.broadcasted_iota(jnp.int32, eye.shape, 1) // 32
    return jnp.where(below, turned, upper_part)


def join_kernel(half, mine_ref, got_ref, sum_ref, send_ref):
    total = mine_ref[...] + got_ref[...]
    sum_ref[...] = total
    edge = 128 * half
    folded = fold([total[128 * k : 128 * (k + 1)] for k in range(half)])
    high, low = split2(total[edge : edge + 8])
    send_ref[...] = above(folded, high.astype(jnp.float32), low.astype(jnp.float32)).astype(jnp.bfloat16)


def beside(*pieces):
    return jnp.concatenate(pieces, axis=1)


def above(*pieces):
    return jnp.concatenate(pieces, axis=0)


def product(a, b):
    (a_high, a_low), (b_high, b_low) = a, b
    return dot(beside(a_high, a_low), above(b_high, b_high)) + dot(a_high, b_low)


def wide(a, b):
    return beside(a[0], b[0]), beside(a[1], b[1])


def vector_product(rows, parts):
    left = above(*[p.astype(jnp.float32) for p in split2(rows)]).astype(jnp.bfloat16)
    full = dot(left, parts[0]) + dot(left, parts[1])
    return full[0:8] + full[8:16]


def solve_kernel(half, sum_ref, got_ref, out_ref):
    size = 128
    spread = float(size - 1)
    eye = identity(size)
    edge = size * half
    got = got_ref[...].astype(jnp.float32)
    projected = sum_ref[edge : edge + 8, :] + got[256:264] + got[264:272]
    norms, bases = [], []
    for k in range(half):
        gram = sum_ref[size * k : size * (k + 1), :] + unfold(got, k, eye)
        squared = jnp.sum(jnp.sum(gram * gram, axis=0, keepdims=True), axis=1, keepdims=True)
        norm = spread + jnp.sqrt(squared)
        norms.append(norm)
        bases.append((spread * eye + gram) / norm)
    base_parts = [split2(base) for base in bases]
    squares = [dot(high, high) for high, _ in base_parts]
    inverses = [
        1.5 * (1.5 * eye - 0.5 * base)
        - 0.5
        * dot(
            (1.5 * base - 0.5 * square).astype(jnp.bfloat16),
            (2.25 * eye - 1.5 * base + 0.25 * square).astype(jnp.bfloat16),
        )
        for base, square in zip(bases, squares)
    ]
    vectors = [jnp.broadcast_to(projected[k : k + 1, :], (8, size)) for k in range(half)]
    pushed = [vector_product(v, parts) for v, parts in zip(vectors, base_parts)]
    carried = None
    for step in range(NS_STEPS - 2):
        last = step == NS_STEPS - 3
        inverse_parts = [split2(z) for z in inverses]
        left = [split2(above(z, v, q)) for z, v, q in zip(inverses, vectors, pushed)] if last else inverse_parts
        both = [product(z, wide(b, y)) for z, b, y in zip(left, base_parts, inverse_parts)]
        forced = [x[:, 0:size] for x in both]
        square = [split2(x[0:size, size : 2 * size]) for x in both]
        if last:
            forced = [above(f[0:size], x[size + 8 : size + 16, size:], x[size + 8 : size + 16, size:]) for f, x in zip(forced, both)]
        cubes = [product(split2(f), y) for f, y in zip(forced, square)]
        if last:
            carried = [1.5 * x[size : size + 8, size:] - 0.5 * c[size : size + 8] for x, c in zip(both, cubes)]
        inverses = [1.5 * z - 0.5 * c[0:size] for z, c in zip(inverses, cubes)]
    scaled = [(jnp.sqrt(spread) / jnp.sqrt(norm)) * inverse for norm, inverse in zip(norms, inverses)]
    means = [
        vector_product(v, split2(inverse))[0:1] / norm for norm, inverse, v in zip(norms, inverses, carried)
    ]
    rest = jnp.zeros((8 - half, size), jnp.float32)
    high, low = split2(above(*means, rest))
    tail = above(high.astype(jnp.float32), low.astype(jnp.float32))
    out_ref[...] = above(fold(scaled), tail).astype(jnp.bfloat16)


def rebuild(folded, k, eye):
    means = folded[256 + k : 257 + k] + folded[264 + k : 265 + k]
    return (unfold(folded, k, eye) + means).astype(jnp.bfloat16)


def identity(size):
    same = lax.broadcasted_iota(jnp.int32, (size, size), 0) == lax.broadcasted_iota(jnp.int32, (size, size), 1)
    return jnp.where(same, 1.0, 0.0)


def shares(levels, size):
    span = SPACING // 2
    shape = (1, span, span, size)
    along_x = lax.broadcasted_iota(jnp.int32, shape, 1).astype(jnp.float32) / (2 * span)
    along_y = lax.broadcasted_iota(jnp.int32, shape, 2).astype(jnp.float32) / (2 * span)
    upper_y = [along_y + (span + 0.5) / (2 * span), along_y + 0.5 / (2 * span)]
    return along_x, upper_y


def mixed(both, share, upper_x, shape):
    high = share * upper_x
    return (share - high) * both[:, 0:128].reshape(shape) + high * both[:, 128:256].reshape(shape)


def near_kernel(cols, members_ref, own, pair, part_ref, pert_ref, table):
    half = cols // 2
    first = lax.rem(lax.axis_index("lev"), 2) == 0
    eye = identity(128)
    mine, theirs = own[...].astype(jnp.float32), pair[...].astype(jnp.float32)
    for at, folded in ((0, jnp.where(first, mine, theirs)), (half, jnp.where(first, theirs, mine))):
        for j in range(half):
            table[128 * (at + j) : 128 * (at + j + 1), :] = rebuild(folded, j, eye)
    levels, width_x, width_y, size = members_ref.shape
    span = SPACING // 2
    shape = (levels, span, span, size)
    rows = levels * span * span
    along_x, upper_y = shares(levels, size)
    for patch_x in range(width_x // span):
        states = members_ref[:, patch_x * span : (patch_x + 1) * span, :, :].astype(jnp.float32)
        mean = jnp.sum(states, axis=3, keepdims=True) * (1.0 / size)
        moved = states - mean
        column = (patch_x + 1) // 2
        upper_x = along_x + (span + 0.5 if patch_x % 2 == 0 else 0.5) / (2 * span)
        for patch_y in range(2):
            inside = slice(patch_y * span, (patch_y + 1) * span)
            left = moved[:, :, inside, :].reshape(rows, size).astype(jnp.bfloat16)
            pert_ref[patch_x, patch_y] = left
            both = dot(left, table[128 * column : 128 * (column + 2), :], ((1,), (1,)))
            share = upper_y[0] if patch_y == 0 else 1.0 - upper_y[1]
            part_ref[patch_x, patch_y] = (mean[:, :, inside, :] + mixed(both, share, upper_x, shape)).reshape(rows, size)


def add_far(first_patch, count, first_column, table, part_ref, pert_ref, keep):
    levels, size = part_ref.shape[2] // (SPACING // 2) ** 2, part_ref.shape[3]
    span = SPACING // 2
    shape = (levels, span, span, size)
    along_x, upper_y = shares(levels, size)
    for k in range(count):
        patch_x = first_patch + k
        column = lax.div(patch_x + 1, 2) - first_column
        lines = pl.ds(pl.multiple_of(128 * column, 128), 256)
        upper_x = along_x + jnp.where(lax.rem(patch_x, 2) == 0, span + 0.5, 0.5) / (2 * span)
        results = []
        for patch_y in range(2):
            both = dot(pert_ref[patch_x, patch_y], table[patch_y, lines, :], ((1,), (1,)))
            share = 1.0 - upper_y[0] if patch_y == 0 else upper_y[1]
            results.append(part_ref[patch_x, patch_y].reshape(shape) + mixed(both, share, upper_x, shape))
        keep(k, patch_x, jnp.concatenate(results, axis=2).astype(jnp.bfloat16))


def neighbours(climb, descend, own, first):
    tile_y = lax.axis_index("ty")
    up, down, mine = (ref[...].astype(jnp.float32) for ref in (climb, descend, own))
    before = jnp.where(tile_y == 0, mine, jnp.where(first, up, down))
    after = jnp.where(tile_y == lax.axis_size("ty") - 1, mine, jnp.where(first, down, up))
    return before, after


def far_first_kernel(cols, count, part_ref, pert_ref, own, climb, descend, out_ref, border_ref, table):
    half, span = cols // 2, SPACING // 2
    core = lax.rem(lax.axis_index("lev"), 2)
    eye = identity(128)
    for z, folded in enumerate(neighbours(climb, descend, own, core == 0)):
        for j in range(half):
            table[z, 128 * j : 128 * (j + 1), :] = rebuild(folded, j, eye)
    border = jnp.where(core == 0, half - 1, 0)
    border_ref[...] = table[:, pl.ds(pl.multiple_of(128 * border, 128), 128), :]

    def keep(k, _, value):
        out_ref[:, k * span : (k + 1) * span] = value

    add_far(core * (part_ref.shape[0] - count), count, core * half, table, part_ref, pert_ref, keep)


def far_rest_kernel(
    cols, count, part_ref, pert_ref, pair, pair_climb, pair_descend, begun, border_ref, out_hbm, table, staged, sems
):
    half, span = cols // 2, SPACING // 2
    core = lax.rem(lax.axis_index("lev"), 2)
    first = core == 0
    total = part_ref.shape[0]
    early = total - count
    start = core * (total - early) * span
    copies = [pltpu.make_async_copy(begun, out_hbm.at[:, pl.ds(start, early * span)], sems.at[count])]
    copies[0].start()
    eye = identity(128)
    for z, folded in enumerate(neighbours(pair_climb, pair_descend, pair, jnp.logical_not(first))):
        for j in range(half):
            at = pl.multiple_of(128 * j + jnp.where(first, 128, 0), 128)
            table[z, pl.ds(at, 128), :] = rebuild(folded, j, eye)
    at = pl.multiple_of(jnp.where(first, 0, 128 * half), 128)
    table[:, pl.ds(at, 128), :] = border_ref[...]

    def keep(k, patch_x, value):
        inside = pl.ds(patch_x * span, span)
        staged[:, inside] = value
        copies.append(pltpu.make_async_copy(staged.at[:, inside], out_hbm.at[:, inside], sems.at[k]))
        copies[-1].start()

    first_column = jnp.where(first, half - 1, 0)
    add_far((1 - core) * early, count, first_column, table, part_ref, pert_ref, keep)
    for copy in copies:
        copy.wait()


def paired_device(
    members, obs_pert, innovation, obs_precision, obs_owner, obs_slot, obs_count, local_weight
):
    axes = ("tx", "ty", "lev")
    ways = pair_patterns(axes)

    def send(value, way):
        return lax.ppermute(value, axes, ways[way])

    bf16, f32 = jnp.bfloat16, jnp.float32
    rows, size = obs_pert.shape
    cols = obs_owner.shape[0] + 2
    half = cols // 2
    shape = jax.ShapeDtypeStruct
    counts = obs_count.reshape(1, -1)
    lists = (obs_owner, obs_slot, counts, local_weight)
    scalars = [v.reshape(rows // size, size) for v in (innovation, obs_precision)]
    packed = device_call(
        functools.partial(pack_kernel, rows),
        tuple(pltpu.with_memory_space_constraint(v, pltpu.HBM) for v in (obs_pert, *scalars, *lists)),
        shape((rows + 16, size), bf16),
        [pltpu.VMEM(v.shape, v.dtype) for v in scalars]
        + [
            pltpu.VMEM(obs_owner.shape, jnp.int32),
            pltpu.VMEM(obs_slot.shape, jnp.int32),
            pltpu.SMEM(counts.shape, jnp.int32),
            pltpu.VMEM(local_weight.shape, f32),
            pltpu.VMEM((16, size), f32),
            pltpu.SemaphoreType.DMA((7,)),
        ],
        name="pack",
        in_hbm=True,
    )
    across = send(packed, "across")
    climb, descend = send(packed, "climb"), send(packed, "descend")
    across_climb, across_descend = send(across, "climb"), send(across, "descend")
    table = device_call(
        functools.partial(table_kernel, rows, cols),
        (*lists, across),
        shape((128, 128), f32),
        flops=6 * 2 * 48 * 256 * 128,
        name="table",
    )
    tall = size * cols + 16
    near = device_call(
        functools.partial(gram_near_kernel, rows, cols),
        (table, packed, climb, descend, across),
        shape((tall, size), f32),
        [
            pltpu.VMEM((size, 4 * rows), f32),
            pltpu.VMEM((4 * rows, size), bf16),
            pltpu.VMEM((tall, 4 * rows), bf16),
        ],
        flops=2 * tall * size * 4 * rows,
        name="gram_near",
    )
    block_scratch = [
        pltpu.VMEM((size, rows), f32),
        pltpu.VMEM((rows, size), bf16),
        pltpu.VMEM((tall, rows), bf16),
    ]
    near = device_call(
        functools.partial(gram_next_kernel, rows, cols, 5),
        (table, near, across_descend),
        shape((tall, size), f32),
        block_scratch,
        flops=2 * tall * size * rows,
        name="gram_next",
    )
    mine, rest = device_call(
        functools.partial(gram_last_kernel, rows, cols, 4),
        (table, near, across_climb),
        [shape((size * half + 8, size), f32)] * 2,
        block_scratch,
        flops=2 * tall * size * rows,
        name="gram_last",
    )
    total, half_sum = device_call(
        functools.partial(join_kernel, half),
        (mine, send(rest, "core")),
        [shape((size * half + 8, size), f32), shape((272, size), bf16)],
        name="join",
    )
    weights = device_call(
        functools.partial(solve_kernel, half),
        (total, send(half_sum, "half")),
        shape((272, size), bf16),
        flops=2 * 27 * half * size**3,
        name="solve",
    )
    pair = send(weights, "core")
    up, down = send(weights, "climb"), send(weights, "descend")
    levels, width_x, width_y, _ = members.shape
    patches = (width_x * 2 // SPACING, 2, levels * SPACING**2 // 4, size)
    part, pert = device_call(
        functools.partial(near_kernel, cols),
        (members, weights, pair),
        [shape(patches, f32), shape(patches, bf16)],
        [pltpu.VMEM((cols * size, size), bf16)],
        flops=2 * levels * width_x * width_y * size * 2 * size,
        name="apply_near",
    )
    up, down, part = lax.optimization_barrier((up, down, part))
    pair_up, pair_down = send(up, "core"), send(down, "core")
    early, span = cols // 2, SPACING // 2
    begun, border = device_call(
        functools.partial(far_first_kernel, cols, early),
        (part, pert, weights, up, down),
        [shape((levels, early * span, width_y, size), bf16), shape((2, size, size), bf16)],
        [pltpu.VMEM((2, half * size, size), bf16)],
        flops=2 * levels * span * early * width_y * size * 2 * size,
        name="far_first",
    )
    count = patches[0] - early
    return device_call(
        functools.partial(far_rest_kernel, cols, count),
        (part, pert, pair, pair_up, pair_down, begun, border),
        shape(members.shape, bf16),
        [
            pltpu.VMEM((2, (half + 1) * size, size), bf16),
            pltpu.VMEM(members.shape, bf16),
            pltpu.SemaphoreType.DMA((count + 1,)),
        ],
        flops=2 * levels * span * count * width_y * size * 2 * size,
        name="far_rest",
        out_hbm=True,
    )


def fits_pairs(mesh, members, obs_pert, obs_owner):
    sizes = dict(mesh.shape)
    return (
        sizes["tx"] == 2
        and sizes["lev"] == 4
        and obs_pert == (256, 128)
        and obs_owner == (4, 1, 256)
        and members[1:] == (64, 16, 128)
    )


def solution(mesh):
    placed = (
        P("lev", "tx", "ty", None),
        P(("tx", "ty", "lev"), None),
        P(("tx", "ty", "lev")),
        P(("tx", "ty", "lev")),
        P("tx", "ty", None),
        P("tx", "ty", None),
        P("tx", "ty"),
        P("tx", "ty", None),
    )

    def local(members, obs_pert, innovation, obs_precision, obs_owner, *rest):
        paired = fits_pairs(mesh, members.shape, obs_pert.shape, obs_owner.shape)
        return (paired_device if paired else per_device)(
            members, obs_pert, innovation, obs_precision, obs_owner, *rest
        )

    return jax.shard_map(
        local,
        mesh=mesh,
        in_specs=placed,
        out_specs=P("lev", "tx", "ty", None),
        check_vma=False,
    )
```

```python
import functools

import jax
import jax.numpy as jnp
from jax import lax
from jax.experimental import pallas as pl
from jax.experimental.pallas import tpu as pltpu
from jax.sharding import PartitionSpec as P

SPACING = 16
NS_STEPS = 4
VMEM_LIMIT = 12 << 20


def padded(array, sides, width):
    for axis, dim in sides:
        size, length = (lax.axis_size(axis), array.shape[dim])
        up = [(i, (i + 1) % size) for i in range(size - 1)]
        down = [(j, i) for i, j in up]
        last = lax.slice_in_dim(array, length - width, length, axis=dim)
        initial = lax.slice_in_dim(array, 0, width, axis=dim)
        before = lax.ppermute(last, axis, up)
        after = lax.ppermute(initial, axis, down)
        array = jnp.concatenate([before, array, after], axis=dim)
    return array


def finish_solve(gram_matrix, projected):
    member_count = gram_matrix.shape[1]
    spread = float(member_count - 1)
    identity = jnp.eye(member_count, dtype=jnp.float32)
    scale_norm = spread + jnp.sqrt(jnp.sum(gram_matrix * gram_matrix, axis=(1, 2)))
    sqrt_iter = (spread * identity + gram_matrix) / scale_norm[:, None, None]
    inv_iter = jnp.broadcast_to(identity, sqrt_iter.shape)
    for iteration in range(NS_STEPS):
        middle = 1.5 * identity - 0.5 * jnp.einsum(
            "bij,bjk->bik", inv_iter, sqrt_iter, precision=lax.Precision.HIGHEST
        )
        sqrt_iter = jnp.einsum("bij,bjk->bik", sqrt_iter, middle, precision=lax.Precision.HIGHEST)
        inv_iter = jnp.einsum("bij,bjk->bik", middle, inv_iter, precision=lax.Precision.HIGHEST)
    inner = jnp.einsum("bij,bj->bi", inv_iter, projected, precision=lax.Precision.HIGHEST)
    mean_weights = (
        jnp.einsum("bij,bj->bi", inv_iter, inner, precision=lax.Precision.HIGHEST)
        / scale_norm[:, None]
    )
    transform = (jnp.sqrt(spread) / jnp.sqrt(scale_norm))[:, None, None] * inv_iter + mean_weights[
        :, :, None
    ]
    return transform.astype(jnp.bfloat16)


def fractions(count, half_span):
    place = jnp.arange(count)[:, None]
    within = jnp.arange(half_span)[None, :].astype(jnp.float32)
    return jnp.where(
        place % 2 == 0,
        (within + half_span + 0.5) / (2 * half_span),
        (within + 0.5) / (2 * half_span),
    )


def solve_columns(lookup, counts, local_part, flat_pert, flat_values):
    column_count, slots = lookup.shape
    member_count = flat_pert.shape[1]
    block_len = min(slots, 128)
    live_blocks = (jnp.max(counts) + block_len - 1) // block_len

    def add_block(block_index, carry):
        gram_matrix, projected = carry
        offset = block_index * block_len
        slot_rows = lax.dynamic_slice_in_dim(lookup, offset, block_len, 1)
        slot_local = lax.dynamic_slice_in_dim(local_part, offset, block_len, 1)
        position = offset + jnp.arange(block_len)
        active = position[None, :] < counts[:, None]
        pert_rows = flat_pert[slot_rows].astype(jnp.float32)
        picked = flat_values[:, slot_rows]
        precision_w = jnp.where(active, picked[1].astype(jnp.float32) * slot_local, 0.0)
        departure = picked[0].astype(jnp.float32)
        gram_matrix = gram_matrix + jnp.einsum(
            "bsk,bsm->bkm",
            pert_rows * precision_w[:, :, None],
            pert_rows,
            precision=lax.Precision.HIGHEST,
        )
        projected = projected + jnp.einsum(
            "bsk,bs->bk", pert_rows, precision_w * departure, precision=lax.Precision.HIGHEST
        )
        return (gram_matrix, projected)

    start_gram = jnp.zeros((column_count, member_count, member_count), jnp.float32)
    start_proj = jnp.zeros((column_count, member_count), jnp.float32)
    gram_matrix, projected = lax.fori_loop(0, live_blocks, add_block, (start_gram, start_proj))
    return finish_solve(gram_matrix, projected)


def clamp_edges(rimmed, axis_index, axis_count, dim):
    lower = jnp.where(
        axis_index == 0,
        lax.slice_in_dim(rimmed, 1, 2, axis=dim),
        lax.slice_in_dim(rimmed, 0, 1, axis=dim),
    )
    last = rimmed.shape[dim]
    upper = jnp.where(
        axis_index == axis_count - 1,
        lax.slice_in_dim(rimmed, last - 2, last - 1, axis=dim),
        lax.slice_in_dim(rimmed, last - 1, last, axis=dim),
    )
    return jnp.concatenate(
        [lower, lax.slice_in_dim(rimmed, 1, last - 1, axis=dim), upper], axis=dim
    )


def per_device(
    members, obs_pert, innovation, obs_precision, obs_owner, obs_slot, obs_count, local_weight
):
    scalars = jnp.stack([innovation, obs_precision])
    tile_pert, tile_values = (
        lax.all_gather(obs_pert, "lev", axis=0, tiled=True),
        lax.all_gather(scalars, "lev", axis=1, tiled=True),
    )
    near_pert, near_values = (
        padded(tile_pert[None, None], (("tx", 0), ("ty", 1)), 1),
        padded(tile_values[None, None], (("tx", 0), ("ty", 1)), 1),
    )
    tile_len = near_pert.shape[2]
    member_count = near_pert.shape[3]
    flat_pert = near_pert.reshape(9 * tile_len, member_count)
    flat_values = jnp.transpose(near_values, (2, 0, 1, 3)).reshape(2, 9 * tile_len)
    column_x = lax.axis_index("tx")
    column_y = lax.axis_index("ty")
    tiles_x = lax.axis_size("tx")
    tiles_y = lax.axis_size("ty")
    near_x = obs_owner // tiles_y - column_x + 1
    near_y = obs_owner % tiles_y - column_y + 1
    lookup = (near_x * 3 + near_y) * tile_len + obs_slot
    coarse_x, coarse_y, slots = lookup.shape
    lookup = lookup.reshape(coarse_x * coarse_y, slots)
    counts = obs_count.reshape(coarse_x * coarse_y)
    local_part = local_weight.reshape(coarse_x * coarse_y, slots)
    weights = solve_columns(lookup, counts, local_part, flat_pert, flat_values)
    weights = weights.reshape(coarse_x, coarse_y, member_count, member_count)
    rimmed = padded(weights, (("tx", 0), ("ty", 1)), 1)
    rimmed = clamp_edges(rimmed, column_x, tiles_x, 0)
    rimmed = clamp_edges(rimmed, column_y, tiles_y, 1)
    doubled = jnp.repeat(jnp.repeat(rimmed, 2, axis=0), 2, axis=1)
    level_count, width_x, width_y, _ = members.shape
    half_span = SPACING // 2
    patch_x = width_x // half_span
    patch_y = width_y // half_span
    frac_x = fractions(patch_x, half_span)
    frac_y = fractions(patch_y, half_span)
    ens_mean = jnp.mean(members, axis=3, keepdims=True, dtype=jnp.float32)
    pert = (members.astype(jnp.float32) - ens_mean).astype(jnp.bfloat16)
    patched = pert.reshape(level_count, patch_x, half_span, patch_y, half_span, member_count)
    summed = jnp.zeros(patched.shape, jnp.float32)
    for upper_x in range(2):
        for upper_y in range(2):
            corner = doubled[
                1 + 2 * upper_x : 1 + 2 * upper_x + patch_x,
                1 + 2 * upper_y : 1 + 2 * upper_y + patch_y,
            ]
            product = jnp.einsum(
                "lxaybi,xyij->lxaybj", patched, corner, preferred_element_type=jnp.float32
            )
            factor_x = frac_x if upper_x == 1 else 1.0 - frac_x
            factor_y = frac_y if upper_y == 1 else 1.0 - frac_y
            summed = (
                summed
                + product
                * factor_x[None, :, :, None, None, None]
                * factor_y[None, None, None, :, :, None]
            )
    return (ens_mean + summed.reshape(members.shape)).astype(jnp.bfloat16)


def pair_patterns(mesh_axes):
    tiles_x, tiles_y, parts = (lax.axis_size(a) for a in mesh_axes)

    def flat(x, y, l):
        return (x * tiles_y + y) * parts + l

    def table(move):
        return [
            (flat(x, y, l), flat(*move(x, y, l)))
            for x in range(tiles_x)
            for y in range(tiles_y)
            for l in range(parts)
        ]

    def climb(x, y, l):
        if l % 2 == 0:
            return (x, y + 1, l) if y < tiles_y - 1 else (x, y, l + 1)
        return (x, y - 1, l) if y > 0 else (x, y, l - 1)

    climbing = table(climb)
    return {
        "across": table(lambda x, y, l: (1 - x, y, l)),
        "core": table(lambda x, y, l: (x, y, l ^ 1)),
        "half": table(lambda x, y, l: (x, y, l ^ 2)),
        "climb": climbing,
        "descend": [(b, a) for a, b in climbing],
    }


def device_call(kernel, operands, out_shape, scratch=(), flops=0, name=None, in_hbm=False, out_hbm=False):
    single = not isinstance(out_shape, (list, tuple))
    spec = pl.BlockSpec(memory_space=pltpu.VMEM)
    hbm = pl.BlockSpec(memory_space=pltpu.HBM)
    out_spec = hbm if out_hbm else spec
    return pl.pallas_call(
        kernel,
        out_shape=out_shape,
        in_specs=[hbm if in_hbm else spec] * len(operands),
        out_specs=out_spec if single else [out_spec] * len(out_shape),
        scratch_shapes=list(scratch),
        cost_estimate=pl.CostEstimate(flops=flops, bytes_accessed=1 << 18, transcendentals=0),
        compiler_params=pltpu.CompilerParams(vmem_limit_bytes=VMEM_LIMIT),
        name=name,
    )(*operands)


def split2(value):
    high = value.astype(jnp.bfloat16)
    return high, (value - high.astype(jnp.float32)).astype(jnp.bfloat16)


def split3(value):
    high, _ = split2(value)
    rest = value - high.astype(jnp.float32)
    middle, low = split2(rest)
    return high, middle, low


def dot(a, b, dims=((1,), (0,))):
    return lax.dot_general(a, b, (dims, ((), ())), preferred_element_type=jnp.float32)


def pack_kernel(
    rows, pert, inn, prec, owner, slot, count, local, out_ref, inn_ref, prec_ref, owner_ref, slot_ref, count_ref, local_ref, tail, sems
):
    sources = (owner, slot, count, local, inn, prec, pert)
    targets = (owner_ref, slot_ref, count_ref, local_ref, inn_ref, prec_ref, out_ref.at[0:rows, :])
    copies = [pltpu.make_async_copy(x, y, sems.at[k]) for k, (x, y) in enumerate(zip(sources, targets))]
    for copy in copies:
        copy.start()
    for copy in copies[:-1]:
        copy.wait()
    edge = jnp.where(lax.axis_index("tx") == 0, owner_ref.shape[0] - 1, 0)
    slots = owner_ref.shape[2]
    limit = jnp.where(edge == 0, count_ref[0, 0], count_ref[0, owner_ref.shape[0] - 1])
    active = lax.broadcasted_iota(jnp.int32, (1, slots), 1) < limit
    local_part = jnp.where(active, local_ref[edge], 0.0)
    slot_part = slot_ref[edge]
    for k, ref in enumerate((prec_ref, inn_ref)):
        tail[2 * k : 2 * k + 2, :] = ref[...].astype(jnp.float32)
    lists = [
        owner_ref[edge].astype(jnp.float32),
        (slot_part // 128).astype(jnp.float32),
        (slot_part % 128).astype(jnp.float32),
    ] + [piece.astype(jnp.float32) for piece in split3(local_part)]
    for k, row in enumerate(lists):
        for part in range(2):
            tail[4 + 2 * k + part : 5 + 2 * k + part, :] = row[:, 128 * part : 128 * (part + 1)]
    out_ref[rows : rows + 16, :] = tail[...].astype(jnp.bfloat16)
    copies[-1].wait()


def table_kernel(rows, cols, owner_ref, slot_ref, count_ref, local_ref, other_ref, out_ref):
    tile_x, tile_y, part = (lax.axis_index(a) for a in ("tx", "ty", "lev"))
    tiles_y = lax.axis_size("ty")
    core = lax.rem(part, 2)
    own, slots = owner_ref.shape[0], owner_ref.shape[2]
    received = other_ref[rows : rows + 16, :].astype(jnp.float32)

    def listed(k):
        return jnp.concatenate([received[2 * k : 2 * k + 1, :], received[2 * k + 1 : 2 * k + 2, :]], axis=1)

    far_owner = listed(2).astype(jnp.int32)
    far_slot = (listed(3) * 128.0 + listed(4)).astype(jnp.int32)
    far_local = listed(5) + listed(6) + listed(7)
    position_in = lax.broadcasted_iota(jnp.int32, (1, slots), 1)

    def own_list(k):
        return owner_ref[k], slot_ref[k], jnp.where(position_in < count_ref[0, k], local_ref[k], 0.0)

    def pick(use_far, k):
        return tuple(jnp.where(use_far, a, b) for a, b in zip((far_owner, far_slot, far_local), own_list(k)))

    lists = [pick(tile_x > 0, 0)] + [own_list(k) for k in range(own)] + [pick(tile_x == 0, own - 1)]
    half = cols // 2
    out_ref[...] = jnp.zeros_like(out_ref)
    for g, (owner, slot, local) in enumerate(lists):
        across = jnp.where(owner // tiles_y == tile_x, 0, 1)
        near = owner % tiles_y - tile_y
        first_way = jnp.where(core == 0, -1, 1)
        block = across * 3 + jnp.where(near == 0, 0, jnp.where(near == first_way, 1, 2))
        mine = slot // rows == part
        within = slot % rows
        high = jnp.where(mine, block * (rows // 128) + within // 128, -1)
        low = within % 128
        picked = jnp.where(lax.broadcasted_iota(jnp.int32, (16, slots), 0) == high, local, 0.0)
        hot = jnp.where(lax.broadcasted_iota(jnp.int32, (128, slots), 0) == low, 1.0, 0.0).astype(jnp.bfloat16)
        parts = split3(picked)
        total = dot(parts[0], hot, ((1,), (1,)))
        for piece in parts[1:]:
            total = total + dot(piece, hot, ((1,), (1,)))
        place = lax.rem(g - core * half + cols, cols)
        out_ref[pl.ds(place, 16, stride=8), :] = total


def gram_blocks(rows, cols, first, blocks, table_ref, turned, plain, scaled):
    per = rows // 128
    products, weights = [], []
    for k, ref in enumerate(blocks):
        tail = ref[rows : rows + 16, :].astype(jnp.float32)
        for part in range(per):
            hi = (first + k) * per + part
            row = table_ref[8 * hi : 8 * hi + 8, :] * tail[part : part + 1, :]
            weights.append(row)
            products.append(row * tail[per + part : per + part + 1, :])
        block = ref[0:rows, :]
        plain[rows * k : rows * (k + 1), :] = block
        turned[:, rows * k : rows * (k + 1)] = block.astype(jnp.float32).T
    weight = jnp.concatenate(weights, axis=1)
    high, low = split2(jnp.concatenate(products, axis=1))
    for position in range(cols):
        at = 128 * position
        scaled[at : at + 128, :] = (turned[...] * weight[position : position + 1, :]).astype(jnp.bfloat16)
    at = 128 * cols
    scaled[at : at + 16, :] = jnp.concatenate(
        [high.astype(jnp.float32), low.astype(jnp.float32)], axis=0
    ).astype(jnp.bfloat16)
    return dot(scaled[...], plain[...])


def gram_near_kernel(rows, cols, table_ref, b0, b1, b2, b3, out_ref, turned, plain, scaled):
    out_ref[...] = gram_blocks(rows, cols, 0, [b0, b1, b2, b3], table_ref, turned, plain, scaled)


def gram_block(rows, cols, first, block, table_ref, so_far_ref):
    per = rows // 128
    tail = block[rows : rows + 16, :].astype(jnp.float32)
    weights = [table_ref[8 * hi : 8 * hi + 8, :] * tail[hi - first * per : hi - first * per + 1, :] for hi in range(first * per, (first + 1) * per)]
    products = [w * tail[per + k : per + k + 1, :] for k, w in enumerate(weights)]
    plain = block[0:rows, :]
    turned = plain.astype(jnp.float32).T
    weight = jnp.concatenate(weights, axis=1)
    pieces = []
    for position in range(cols):
        scaled = (turned * weight[position : position + 1, :]).astype(jnp.bfloat16)
        pieces.append(so_far_ref[128 * position : 128 * (position + 1), :] + dot(scaled, plain))
    both = above(*[p.astype(jnp.float32) for p in split2(jnp.concatenate(products, axis=1))]).astype(jnp.bfloat16)
    pieces.append(so_far_ref[128 * cols : 128 * cols + 16, :] + dot(both, plain))
    return pieces


def gram_next_kernel(rows, cols, first, table_ref, so_far_ref, block, out_ref):
    for k, piece in enumerate(gram_block(rows, cols, first, block, table_ref, so_far_ref)):
        out_ref[128 * k : 128 * k + piece.shape[0], :] = piece


def gram_last_kernel(rows, cols, first, table_ref, so_far_ref, block, mine_ref, rest_ref):
    half = cols // 2
    pieces = gram_block(rows, cols, first, block, table_ref, so_far_ref)
    for k in range(half):
        mine_ref[128 * k : 128 * (k + 1), :] = pieces[k]
        rest_ref[128 * k : 128 * (k + 1), :] = pieces[half + k].astype(jnp.bfloat16)
    projected = pieces[cols][0:8] + pieces[cols][8:16]
    edge = 128 * half
    mine_ref[edge : edge + 8, :] = projected
    high, low = split2(above(projected[half : 2 * half], jnp.zeros((8 - half, 128), jnp.float32)))
    rest_ref[edge : edge + 16, :] = above(high.astype(jnp.float32), low.astype(jnp.float32)).astype(jnp.bfloat16)


def lanes_from(lane, values, others=0.0):
    return jnp.where(lax.broadcasted_iota(jnp.int32, values.shape, 1) >= lane, values, others)


def fold(grams):
    top = [g[0:32] for g in grams]
    sides = [lanes_from(32, g[32:64], pltpu.roll(g[96:128], 32, 1)) for g in grams]
    third = [g[64:96] for g in grams]
    return above(*top, *sides, lanes_from(64, third[0], pltpu.roll(third[1], 64, 1)), third[2])


def unfold(folded, k, eye):
    side = folded[96 + 32 * k : 128 + 32 * k]
    third = folded[192:224] if k < 2 else folded[224:256]
    third = pltpu.roll(third, 64, 1) if k == 1 else third
    upper_part = above(
        folded[32 * k : 32 * k + 32],
        lanes_from(32, side),
        lanes_from(64, third),
        lanes_from(96, pltpu.roll(side, 96, 1)),
    )
    turned = dot(eye.astype(jnp.bfloat16), upper_part.astype(jnp.bfloat16), ((1,), (1,)))
    below = lax.broadcasted_iota(jnp.int32, eye.shape, 0) // 32 > lax.broadcasted_iota(jnp.int32, eye.shape, 1) // 32
    return jnp.where(below, turned, upper_part)


def join_kernel(half, mine_ref, got_ref, sum_ref, send_ref):
    edge = 128 * half
    got = got_ref[...].astype(jnp.float32)
    total = mine_ref[...] + above(got[0:edge], got[edge : edge + 8] + got[edge + 8 : edge + 16])
    sum_ref[...] = total
    folded = fold([total[128 * k : 128 * (k + 1)] for k in range(half)])
    high, low = split2(total[edge : edge + 8])
    send_ref[...] = above(folded, high.astype(jnp.float32), low.astype(jnp.float32)).astype(jnp.bfloat16)


def beside(*pieces):
    return jnp.concatenate(pieces, axis=1)


def above(*pieces):
    return jnp.concatenate(pieces, axis=0)


def product(a, b):
    (a_high, a_low), (b_high, b_low) = a, b
    return dot(beside(a_high, a_low), above(b_high, b_high)) + dot(a_high, b_low)


def wide(a, b):
    return beside(a[0], b[0]), beside(a[1], b[1])


def vector_product(rows, parts):
    left = above(*[p.astype(jnp.float32) for p in split2(rows)]).astype(jnp.bfloat16)
    full = dot(left, parts[0]) + dot(left, parts[1])
    return full[0:8] + full[8:16]


def solve_kernel(half, sum_ref, got_ref, out_ref):
    size = 128
    spread = float(size - 1)
    eye = identity(size)
    edge = size * half
    got = got_ref[...].astype(jnp.float32)
    projected = sum_ref[edge : edge + 8, :] + got[256:264] + got[264:272]
    norms, bases = [], []
    for k in range(half):
        gram = sum_ref[size * k : size * (k + 1), :] + unfold(got, k, eye)
        squared = jnp.sum(jnp.sum(gram * gram, axis=0, keepdims=True), axis=1, keepdims=True)
        norm = spread + jnp.sqrt(squared)
        norms.append(norm)
        bases.append((spread * eye + gram) / norm)
    base_parts = [split2(base) for base in bases]
    squares = [dot(high, high) for high, _ in base_parts]
    inverses = [
        1.5 * (1.5 * eye - 0.5 * base)
        - 0.5
        * dot(
            (1.5 * base - 0.5 * square).astype(jnp.bfloat16),
            (2.25 * eye - 1.5 * base + 0.25 * square).astype(jnp.bfloat16),
        )
        for base, square in zip(bases, squares)
    ]
    vectors = [jnp.broadcast_to(projected[k : k + 1, :], (8, size)) for k in range(half)]
    pushed = [vector_product(v, parts) for v, parts in zip(vectors, base_parts)]
    carried = None
    for step in range(NS_STEPS - 2):
        last = step == NS_STEPS - 3
        inverse_parts = [split2(z) for z in inverses]
        left = [split2(above(z, v, q)) for z, v, q in zip(inverses, vectors, pushed)] if last else inverse_parts
        both = [product(z, wide(b, y)) for z, b, y in zip(left, base_parts, inverse_parts)]
        forced = [x[:, 0:size] for x in both]
        square = [split2(x[0:size, size : 2 * size]) for x in both]
        if last:
            forced = [above(f[0:size], x[size + 8 : size + 16, size:], x[size + 8 : size + 16, size:]) for f, x in zip(forced, both)]
        cubes = [product(split2(f), y) for f, y in zip(forced, square)]
        if last:
            carried = [1.5 * x[size : size + 8, size:] - 0.5 * c[size : size + 8] for x, c in zip(both, cubes)]
        inverses = [1.5 * z - 0.5 * c[0:size] for z, c in zip(inverses, cubes)]
    scaled = [(jnp.sqrt(spread) / jnp.sqrt(norm)) * inverse for norm, inverse in zip(norms, inverses)]
    means = [
        vector_product(v, split2(inverse))[0:1] / norm for norm, inverse, v in zip(norms, inverses, carried)
    ]
    rest = jnp.zeros((8 - half, size), jnp.float32)
    high, low = split2(above(*means, rest))
    tail = above(high.astype(jnp.float32), low.astype(jnp.float32))
    out_ref[...] = above(fold(scaled), tail).astype(jnp.bfloat16)


def rebuild(folded, k, eye):
    means = folded[256 + k : 257 + k] + folded[264 + k : 265 + k]
    return (unfold(folded, k, eye) + means).astype(jnp.bfloat16)


def identity(size):
    same = lax.broadcasted_iota(jnp.int32, (size, size), 0) == lax.broadcasted_iota(jnp.int32, (size, size), 1)
    return jnp.where(same, 1.0, 0.0)


def shares(levels, size):
    span = SPACING // 2
    shape = (1, span, span, size)
    along_x = lax.broadcasted_iota(jnp.int32, shape, 1).astype(jnp.float32) / (2 * span)
    along_y = lax.broadcasted_iota(jnp.int32, shape, 2).astype(jnp.float32) / (2 * span)
    upper_y = [along_y + (span + 0.5) / (2 * span), along_y + 0.5 / (2 * span)]
    return along_x, upper_y


def mixed(both, share, upper_x, shape):
    high = share * upper_x
    return (share - high) * both[:, 0:128].reshape(shape) + high * both[:, 128:256].reshape(shape)


def near_kernel(cols, members_ref, own, pair, part_ref, pert_ref, table):
    half = cols // 2
    first = lax.rem(lax.axis_index("lev"), 2) == 0
    eye = identity(128)
    mine, theirs = own[...].astype(jnp.float32), pair[...].astype(jnp.float32)
    for at, folded in ((0, jnp.where(first, mine, theirs)), (half, jnp.where(first, theirs, mine))):
        for j in range(half):
            table[128 * (at + j) : 128 * (at + j + 1), :] = rebuild(folded, j, eye)
    levels, width_x, width_y, size = members_ref.shape
    span = SPACING // 2
    shape = (levels, span, span, size)
    rows = levels * span * span
    along_x, upper_y = shares(levels, size)
    for patch_x in range(width_x // span):
        states = members_ref[:, patch_x * span : (patch_x + 1) * span, :, :].astype(jnp.float32)
        mean = jnp.sum(states, axis=3, keepdims=True) * (1.0 / size)
        moved = states - mean
        column = (patch_x + 1) // 2
        upper_x = along_x + (span + 0.5 if patch_x % 2 == 0 else 0.5) / (2 * span)
        for patch_y in range(2):
            inside = slice(patch_y * span, (patch_y + 1) * span)
            left = moved[:, :, inside, :].reshape(rows, size).astype(jnp.bfloat16)
            pert_ref[patch_x, patch_y] = left
            both = dot(left, table[128 * column : 128 * (column + 2), :], ((1,), (1,)))
            share = upper_y[0] if patch_y == 0 else 1.0 - upper_y[1]
            part_ref[patch_x, patch_y] = (mean[:, :, inside, :] + mixed(both, share, upper_x, shape)).reshape(rows, size)


def add_far(first_patch, count, first_column, table, part_ref, pert_ref, keep):
    levels, size = part_ref.shape[2] // (SPACING // 2) ** 2, part_ref.shape[3]
    span = SPACING // 2
    shape = (levels, span, span, size)
    along_x, upper_y = shares(levels, size)
    for k in range(count):
        patch_x = first_patch + k
        column = lax.div(patch_x + 1, 2) - first_column
        lines = pl.ds(pl.multiple_of(128 * column, 128), 256)
        upper_x = along_x + jnp.where(lax.rem(patch_x, 2) == 0, span + 0.5, 0.5) / (2 * span)
        results = []
        for patch_y in range(2):
            both = dot(pert_ref[patch_x, patch_y], table[patch_y, lines, :], ((1,), (1,)))
            share = 1.0 - upper_y[0] if patch_y == 0 else upper_y[1]
            results.append(part_ref[patch_x, patch_y].reshape(shape) + mixed(both, share, upper_x, shape))
        keep(k, patch_x, jnp.concatenate(results, axis=2).astype(jnp.bfloat16))


def neighbours(climb, descend, own, first):
    tile_y = lax.axis_index("ty")
    up, down, mine = climb[...], descend[...], own[...]
    before = jnp.where(tile_y == 0, mine, jnp.where(first, up, down))
    after = jnp.where(tile_y == lax.axis_size("ty") - 1, mine, jnp.where(first, down, up))
    return before.astype(jnp.float32), after.astype(jnp.float32)


def far_first_kernel(cols, count, part_ref, pert_ref, own, climb, descend, out_ref, border_ref, table):
    half, span = cols // 2, SPACING // 2
    core = lax.rem(lax.axis_index("lev"), 2)
    eye = identity(128)
    for z, folded in enumerate(neighbours(climb, descend, own, core == 0)):
        for j in range(half):
            table[z, 128 * j : 128 * (j + 1), :] = rebuild(folded, j, eye)
    border = jnp.where(core == 0, half - 1, 0)
    border_ref[...] = table[:, pl.ds(pl.multiple_of(128 * border, 128), 128), :]

    def keep(k, _, value):
        out_ref[:, k * span : (k + 1) * span] = value

    add_far(core * (part_ref.shape[0] - count), count, core * half, table, part_ref, pert_ref, keep)


def far_rest_kernel(
    cols, count, part_ref, pert_ref, pair, pair_climb, pair_descend, begun, border_ref, out_hbm, table, staged, sems
):
    half, span = cols // 2, SPACING // 2
    core = lax.rem(lax.axis_index("lev"), 2)
    first = core == 0
    total = part_ref.shape[0]
    early = total - count
    start = core * (total - early) * span
    copies = [pltpu.make_async_copy(begun, out_hbm.at[:, pl.ds(start, early * span)], sems.at[count])]
    copies[0].start()
    eye = identity(128)
    for z, folded in enumerate(neighbours(pair_climb, pair_descend, pair, jnp.logical_not(first))):
        for j in range(half):
            at = pl.multiple_of(128 * j + jnp.where(first, 128, 0), 128)
            table[z, pl.ds(at, 128), :] = rebuild(folded, j, eye)
    at = pl.multiple_of(jnp.where(first, 0, 128 * half), 128)
    table[:, pl.ds(at, 128), :] = border_ref[...]

    def keep(k, patch_x, value):
        inside = pl.ds(patch_x * span, span)
        staged[:, inside] = value
        copies.append(pltpu.make_async_copy(staged.at[:, inside], out_hbm.at[:, inside], sems.at[k]))
        copies[-1].start()

    first_column = jnp.where(first, half - 1, 0)
    add_far((1 - core) * early, count, first_column, table, part_ref, pert_ref, keep)
    for copy in copies:
        copy.wait()


def paired_device(
    members, obs_pert, innovation, obs_precision, obs_owner, obs_slot, obs_count, local_weight
):
    axes = ("tx", "ty", "lev")
    ways = pair_patterns(axes)

    def send(value, way):
        return lax.ppermute(value, axes, ways[way])

    bf16, f32 = jnp.bfloat16, jnp.float32
    rows, size = obs_pert.shape
    cols = obs_owner.shape[0] + 2
    half = cols // 2
    shape = jax.ShapeDtypeStruct
    counts = obs_count.reshape(1, -1)
    lists = (obs_owner, obs_slot, counts, local_weight)
    scalars = [v.reshape(rows // size, size) for v in (innovation, obs_precision)]
    packed = device_call(
        functools.partial(pack_kernel, rows),
        tuple(pltpu.with_memory_space_constraint(v, pltpu.HBM) for v in (obs_pert, *scalars, *lists)),
        shape((rows + 16, size), bf16),
        [pltpu.VMEM(v.shape, v.dtype) for v in scalars]
        + [
            pltpu.VMEM(obs_owner.shape, jnp.int32),
            pltpu.VMEM(obs_slot.shape, jnp.int32),
            pltpu.SMEM(counts.shape, jnp.int32),
            pltpu.VMEM(local_weight.shape, f32),
            pltpu.VMEM((16, size), f32),
            pltpu.SemaphoreType.DMA((7,)),
        ],
        name="pack",
        in_hbm=True,
    )
    across = send(packed, "across")
    climb, descend = send(packed, "climb"), send(packed, "descend")
    across_climb, across_descend = send(across, "climb"), send(across, "descend")
    table = device_call(
        functools.partial(table_kernel, rows, cols),
        (*lists, across),
        shape((128, 128), f32),
        flops=6 * 2 * 48 * 256 * 128,
        name="table",
    )
    tall = size * cols + 16
    near = device_call(
        functools.partial(gram_near_kernel, rows, cols),
        (table, packed, climb, descend, across),
        shape((tall, size), f32),
        [
            pltpu.VMEM((size, 4 * rows), f32),
            pltpu.VMEM((4 * rows, size), bf16),
            pltpu.VMEM((tall, 4 * rows), bf16),
        ],
        flops=2 * tall * size * 4 * rows,
        name="gram_near",
    )
    near = device_call(
        functools.partial(gram_next_kernel, rows, cols, 5),
        (table, near, across_descend),
        shape((tall, size), f32),
        flops=2 * tall * size * rows,
        name="gram_next",
    )
    mine, rest = device_call(
        functools.partial(gram_last_kernel, rows, cols, 4),
        (table, near, across_climb),
        [shape((size * half + 8, size), f32), shape((size * half + 16, size), bf16)],
        flops=2 * tall * size * rows,
        name="gram_last",
    )
    total, half_sum = device_call(
        functools.partial(join_kernel, half),
        (mine, send(rest, "core")),
        [shape((size * half + 8, size), f32), shape((272, size), bf16)],
        name="join",
    )
    weights = device_call(
        functools.partial(solve_kernel, half),
        (total, send(half_sum, "half")),
        shape((272, size), bf16),
        flops=2 * 27 * half * size**3,
        name="solve",
    )
    pair = send(weights, "core")
    up, down = send(weights, "climb"), send(weights, "descend")
    levels, width_x, width_y, _ = members.shape
    patches = (width_x * 2 // SPACING, 2, levels * SPACING**2 // 4, size)
    part, pert = device_call(
        functools.partial(near_kernel, cols),
        (members, weights, pair),
        [shape(patches, f32), shape(patches, bf16)],
        [pltpu.VMEM((cols * size, size), bf16)],
        flops=2 * levels * width_x * width_y * size * 2 * size,
        name="apply_near",
    )
    up, down, part = lax.optimization_barrier((up, down, part))
    pair_up, pair_down = send(up, "core"), send(down, "core")
    early, span = cols // 2, SPACING // 2
    begun, border = device_call(
        functools.partial(far_first_kernel, cols, early),
        (part, pert, weights, up, down),
        [shape((levels, early * span, width_y, size), bf16), shape((2, size, size), bf16)],
        [pltpu.VMEM((2, half * size, size), bf16)],
        flops=2 * levels * span * early * width_y * size * 2 * size,
        name="far_first",
    )
    count = patches[0] - early
    return device_call(
        functools.partial(far_rest_kernel, cols, count),
        (part, pert, pair, pair_up, pair_down, begun, border),
        shape(members.shape, bf16),
        [
            pltpu.VMEM((2, (half + 1) * size, size), bf16),
            pltpu.VMEM(members.shape, bf16),
            pltpu.SemaphoreType.DMA((count + 1,)),
        ],
        flops=2 * levels * span * count * width_y * size * 2 * size,
        name="far_rest",
        out_hbm=True,
    )


def fits_pairs(mesh, members, obs_pert, obs_owner):
    sizes = dict(mesh.shape)
    return (
        sizes["tx"] == 2
        and sizes["lev"] == 4
        and obs_pert == (256, 128)
        and obs_owner == (4, 1, 256)
        and members[1:] == (64, 16, 128)
    )


def solution(mesh):
    placed = (
        P("lev", "tx", "ty", None),
        P(("tx", "ty", "lev"), None),
        P(("tx", "ty", "lev")),
        P(("tx", "ty", "lev")),
        P("tx", "ty", None),
        P("tx", "ty", None),
        P("tx", "ty"),
        P("tx", "ty", None),
    )

    def local(members, obs_pert, innovation, obs_precision, obs_owner, *rest):
        paired = fits_pairs(mesh, members.shape, obs_pert.shape, obs_owner.shape)
        return (paired_device if paired else per_device)(
            members, obs_pert, innovation, obs_precision, obs_owner, *rest
        )

    return jax.shard_map(
        local,
        mesh=mesh,
        in_specs=placed,
        out_specs=P("lev", "tx", "ty", None),
        check_vma=False,
    )
```

```python
import functools

import jax
import jax.numpy as jnp
from jax import lax
from jax.experimental import pallas as pl
from jax.experimental.pallas import tpu as pltpu
from jax.sharding import PartitionSpec as P


SPACING = 16
NS_STEPS = 4
VMEM_LIMIT = 12 << 20


def padded(array, sides, width):
    for axis, dim in sides:
        size, length = (lax.axis_size(axis), array.shape[dim])
        up = [(i, (i + 1) % size) for i in range(size - 1)]
        down = [(j, i) for i, j in up]
        last = lax.slice_in_dim(array, length - width, length, axis=dim)
        initial = lax.slice_in_dim(array, 0, width, axis=dim)
        before = lax.ppermute(last, axis, up)
        after = lax.ppermute(initial, axis, down)
        array = jnp.concatenate([before, array, after], axis=dim)
    return array


def finish_solve(gram_matrix, projected):
    member_count = gram_matrix.shape[1]
    spread = float(member_count - 1)
    identity = jnp.eye(member_count, dtype=jnp.float32)
    scale_norm = spread + jnp.sqrt(jnp.sum(gram_matrix * gram_matrix, axis=(1, 2)))
    sqrt_iter = (spread * identity + gram_matrix) / scale_norm[:, None, None]
    inv_iter = jnp.broadcast_to(identity, sqrt_iter.shape)
    for _ in range(NS_STEPS):
        middle = 1.5 * identity - 0.5 * jnp.einsum(
            "bij,bjk->bik", inv_iter, sqrt_iter, precision=lax.Precision.HIGHEST
        )
        sqrt_iter = jnp.einsum("bij,bjk->bik", sqrt_iter, middle, precision=lax.Precision.HIGHEST)
        inv_iter = jnp.einsum("bij,bjk->bik", middle, inv_iter, precision=lax.Precision.HIGHEST)
    inner = jnp.einsum("bij,bj->bi", inv_iter, projected, precision=lax.Precision.HIGHEST)
    mean_weights = (
        jnp.einsum("bij,bj->bi", inv_iter, inner, precision=lax.Precision.HIGHEST)
        / scale_norm[:, None]
    )
    transform = (jnp.sqrt(spread) / jnp.sqrt(scale_norm))[:, None, None] * inv_iter + mean_weights[
        :, :, None
    ]
    return transform.astype(jnp.bfloat16)


def fractions(count, half_span):
    place = jnp.arange(count)[:, None]
    within = jnp.arange(half_span)[None, :].astype(jnp.float32)
    return jnp.where(
        place % 2 == 0,
        (within + half_span + 0.5) / (2 * half_span),
        (within + 0.5) / (2 * half_span),
    )


def solve_columns(lookup, counts, local_part, flat_pert, flat_values):
    column_count, slots = lookup.shape
    member_count = flat_pert.shape[1]
    block_len = min(slots, 128)
    live_blocks = (jnp.max(counts) + block_len - 1) // block_len

    def add_block(block_index, carry):
        gram_matrix, projected = carry
        offset = block_index * block_len
        slot_rows = lax.dynamic_slice_in_dim(lookup, offset, block_len, 1)
        slot_local = lax.dynamic_slice_in_dim(local_part, offset, block_len, 1)
        position = offset + jnp.arange(block_len)
        active = position[None, :] < counts[:, None]
        pert_rows = flat_pert[slot_rows].astype(jnp.float32)
        picked = flat_values[:, slot_rows]
        precision_w = jnp.where(active, picked[1].astype(jnp.float32) * slot_local, 0.0)
        departure = picked[0].astype(jnp.float32)
        gram_matrix = gram_matrix + jnp.einsum(
            "bsk,bsm->bkm",
            pert_rows * precision_w[:, :, None],
            pert_rows,
            precision=lax.Precision.HIGHEST,
        )
        projected = projected + jnp.einsum(
            "bsk,bs->bk", pert_rows, precision_w * departure, precision=lax.Precision.HIGHEST
        )
        return (gram_matrix, projected)

    start_gram = jnp.zeros((column_count, member_count, member_count), jnp.float32)
    start_proj = jnp.zeros((column_count, member_count), jnp.float32)
    gram_matrix, projected = lax.fori_loop(0, live_blocks, add_block, (start_gram, start_proj))
    return finish_solve(gram_matrix, projected)


def clamp_edges(rimmed, axis_index, axis_count, dim):
    lower = jnp.where(
        axis_index == 0,
        lax.slice_in_dim(rimmed, 1, 2, axis=dim),
        lax.slice_in_dim(rimmed, 0, 1, axis=dim),
    )
    last = rimmed.shape[dim]
    upper = jnp.where(
        axis_index == axis_count - 1,
        lax.slice_in_dim(rimmed, last - 2, last - 1, axis=dim),
        lax.slice_in_dim(rimmed, last - 1, last, axis=dim),
    )
    return jnp.concatenate(
        [lower, lax.slice_in_dim(rimmed, 1, last - 1, axis=dim), upper], axis=dim
    )


def per_device(
    members, obs_pert, innovation, obs_precision, obs_owner, obs_slot, obs_count, local_weight
):
    scalars = jnp.stack([innovation, obs_precision])
    tile_pert, tile_values = (
        lax.all_gather(obs_pert, "lev", axis=0, tiled=True),
        lax.all_gather(scalars, "lev", axis=1, tiled=True),
    )
    near_pert, near_values = (
        padded(tile_pert[None, None], (("tx", 0), ("ty", 1)), 1),
        padded(tile_values[None, None], (("tx", 0), ("ty", 1)), 1),
    )
    tile_len = near_pert.shape[2]
    member_count = near_pert.shape[3]
    flat_pert = near_pert.reshape(9 * tile_len, member_count)
    flat_values = jnp.transpose(near_values, (2, 0, 1, 3)).reshape(2, 9 * tile_len)
    column_x = lax.axis_index("tx")
    column_y = lax.axis_index("ty")
    tiles_x = lax.axis_size("tx")
    tiles_y = lax.axis_size("ty")
    near_x = obs_owner // tiles_y - column_x + 1
    near_y = obs_owner % tiles_y - column_y + 1
    lookup = (near_x * 3 + near_y) * tile_len + obs_slot
    coarse_x, coarse_y, slots = lookup.shape
    lookup = lookup.reshape(coarse_x * coarse_y, slots)
    counts = obs_count.reshape(coarse_x * coarse_y)
    local_part = local_weight.reshape(coarse_x * coarse_y, slots)
    weights = solve_columns(lookup, counts, local_part, flat_pert, flat_values)
    weights = weights.reshape(coarse_x, coarse_y, member_count, member_count)
    rimmed = padded(weights, (("tx", 0), ("ty", 1)), 1)
    rimmed = clamp_edges(rimmed, column_x, tiles_x, 0)
    rimmed = clamp_edges(rimmed, column_y, tiles_y, 1)
    doubled = jnp.repeat(jnp.repeat(rimmed, 2, axis=0), 2, axis=1)
    level_count, width_x, width_y, _ = members.shape
    half_span = SPACING // 2
    patch_x = width_x // half_span
    patch_y = width_y // half_span
    frac_x = fractions(patch_x, half_span)
    frac_y = fractions(patch_y, half_span)
    ens_mean = jnp.mean(members, axis=3, keepdims=True, dtype=jnp.float32)
    pert = (members.astype(jnp.float32) - ens_mean).astype(jnp.bfloat16)
    patched = pert.reshape(level_count, patch_x, half_span, patch_y, half_span, member_count)
    summed = jnp.zeros(patched.shape, jnp.float32)
    for upper_x in range(2):
        for upper_y in range(2):
            corner = doubled[
                1 + 2 * upper_x : 1 + 2 * upper_x + patch_x,
                1 + 2 * upper_y : 1 + 2 * upper_y + patch_y,
            ]
            product = jnp.einsum(
                "lxaybi,xyij->lxaybj", patched, corner, preferred_element_type=jnp.float32
            )
            factor_x = frac_x if upper_x == 1 else 1.0 - frac_x
            factor_y = frac_y if upper_y == 1 else 1.0 - frac_y
            summed = (
                summed
                + product
                * factor_x[None, :, :, None, None, None]
                * factor_y[None, None, None, :, :, None]
            )
    return (ens_mean + summed.reshape(members.shape)).astype(jnp.bfloat16)


def pair_patterns(mesh_axes):
    tiles_x, tiles_y, parts = (lax.axis_size(a) for a in mesh_axes)

    def flat(x, y, l):
        return (x * tiles_y + y) * parts + l

    def table(move):
        return [
            (flat(x, y, l), flat(*move(x, y, l)))
            for x in range(tiles_x)
            for y in range(tiles_y)
            for l in range(parts)
        ]

    def climb(x, y, l):
        if l % 2 == 0:
            return (x, y + 1, l) if y < tiles_y - 1 else (x, y, l + 1)
        return (x, y - 1, l) if y > 0 else (x, y, l - 1)

    climbing = table(climb)
    return {
        "across": table(lambda x, y, l: (1 - x, y, l)),
        "core": table(lambda x, y, l: (x, y, l ^ 1)),
        "half": table(lambda x, y, l: (x, y, l ^ 2)),
        "climb": climbing,
        "descend": [(b, a) for a, b in climbing],
    }


def device_call(kernel, operands, out_shape, scratch=(), flops=0, in_hbm=False, out_hbm=False):
    single = not isinstance(out_shape, (list, tuple))
    spec = pl.BlockSpec(memory_space=pltpu.VMEM)
    hbm = pl.BlockSpec(memory_space=pltpu.HBM)
    out_spec = hbm if out_hbm else spec
    return pl.pallas_call(
        kernel,
        out_shape=out_shape,
        in_specs=[hbm if in_hbm else spec] * len(operands),
        out_specs=out_spec if single else [out_spec] * len(out_shape),
        scratch_shapes=list(scratch),
        cost_estimate=pl.CostEstimate(flops=flops, bytes_accessed=1 << 18, transcendentals=0),
        compiler_params=pltpu.CompilerParams(vmem_limit_bytes=VMEM_LIMIT),
    )(*operands)


def split2(value):
    high = value.astype(jnp.bfloat16)
    return high, (value - high.astype(jnp.float32)).astype(jnp.bfloat16)


def split3(value):
    high, _ = split2(value)
    rest = value - high.astype(jnp.float32)
    middle, low = split2(rest)
    return high, middle, low


def dot(a, b, dims=((1,), (0,))):
    return lax.dot_general(a, b, (dims, ((), ())), preferred_element_type=jnp.float32)


def pack_kernel(
    rows, pert, inn, prec, owner, slot, count, local, out_ref, inn_ref, prec_ref, owner_ref, slot_ref, count_ref, local_ref, tail, sems
):
    sources = (owner, slot, count, local, inn, prec, pert)
    targets = (owner_ref, slot_ref, count_ref, local_ref, inn_ref, prec_ref, out_ref.at[0:rows, :])
    copies = [pltpu.make_async_copy(x, y, sems.at[k]) for k, (x, y) in enumerate(zip(sources, targets))]
    for copy in copies:
        copy.start()
    for copy in copies[:-1]:
        copy.wait()
    edge = jnp.where(lax.axis_index("tx") == 0, owner_ref.shape[0] - 1, 0)
    slots = owner_ref.shape[2]
    limit = jnp.where(edge == 0, count_ref[0, 0], count_ref[0, owner_ref.shape[0] - 1])
    active = lax.broadcasted_iota(jnp.int32, (1, slots), 1) < limit
    local_part = jnp.where(active, local_ref[edge], 0.0)
    slot_part = slot_ref[edge]
    for k, ref in enumerate((prec_ref, inn_ref)):
        tail[2 * k : 2 * k + 2, :] = ref[...].astype(jnp.float32)
    lists = [
        owner_ref[edge].astype(jnp.float32),
        (slot_part // 128).astype(jnp.float32),
        (slot_part % 128).astype(jnp.float32),
    ] + [piece.astype(jnp.float32) for piece in split3(local_part)]
    for k, row in enumerate(lists):
        for part in range(2):
            tail[4 + 2 * k + part : 5 + 2 * k + part, :] = row[:, 128 * part : 128 * (part + 1)]
    out_ref[rows : rows + 16, :] = tail[...].astype(jnp.bfloat16)
    copies[-1].wait()


def table_kernel(rows, cols, owner_ref, slot_ref, count_ref, local_ref, other_ref, out_ref):
    tile_x, tile_y, part = (lax.axis_index(a) for a in ("tx", "ty", "lev"))
    tiles_y = lax.axis_size("ty")
    core = lax.rem(part, 2)
    own, slots = owner_ref.shape[0], owner_ref.shape[2]
    received = other_ref[rows : rows + 16, :].astype(jnp.float32)

    def listed(k):
        return jnp.concatenate([received[2 * k : 2 * k + 1, :], received[2 * k + 1 : 2 * k + 2, :]], axis=1)

    far_owner = listed(2).astype(jnp.int32)
    far_slot = (listed(3) * 128.0 + listed(4)).astype(jnp.int32)
    far_local = listed(5) + listed(6) + listed(7)
    position_in = lax.broadcasted_iota(jnp.int32, (1, slots), 1)

    def own_list(k):
        return owner_ref[k], slot_ref[k], jnp.where(position_in < count_ref[0, k], local_ref[k], 0.0)

    def pick(use_far, k):
        return tuple(jnp.where(use_far, a, b) for a, b in zip((far_owner, far_slot, far_local), own_list(k)))

    lists = [pick(tile_x > 0, 0)] + [own_list(k) for k in range(own)] + [pick(tile_x == 0, own - 1)]
    half = cols // 2
    out_ref[...] = jnp.zeros_like(out_ref)
    for g, (owner, slot, local) in enumerate(lists):
        across = jnp.where(owner // tiles_y == tile_x, 0, 1)
        near = owner % tiles_y - tile_y
        first_way = jnp.where(core == 0, -1, 1)
        block = across * 3 + jnp.where(near == 0, 0, jnp.where(near == first_way, 1, 2))
        mine = slot // rows == part
        within = slot % rows
        high = jnp.where(mine, block * (rows // 128) + within // 128, -1)
        low = within % 128
        picked = jnp.where(lax.broadcasted_iota(jnp.int32, (16, slots), 0) == high, local, 0.0)
        hot = jnp.where(lax.broadcasted_iota(jnp.int32, (128, slots), 0) == low, 1.0, 0.0).astype(jnp.bfloat16)
        parts = split3(picked)
        total = dot(parts[0], hot, ((1,), (1,)))
        for piece in parts[1:]:
            total = total + dot(piece, hot, ((1,), (1,)))
        place = lax.rem(g - core * half + cols, cols)
        out_ref[pl.ds(place, 16, stride=8), :] = total


def gram_blocks(rows, cols, first, blocks, table_ref, turned, plain, scaled):
    per = rows // 128
    products, weights = [], []
    for k, ref in enumerate(blocks):
        tail = ref[rows : rows + 16, :].astype(jnp.float32)
        for part in range(per):
            hi = (first + k) * per + part
            row = table_ref[8 * hi : 8 * hi + 8, :] * tail[part : part + 1, :]
            weights.append(row)
            products.append(row * tail[per + part : per + part + 1, :])
        block = ref[0:rows, :]
        plain[rows * k : rows * (k + 1), :] = block
        turned[:, rows * k : rows * (k + 1)] = block.astype(jnp.float32).T
    weight = jnp.concatenate(weights, axis=1)
    high, low = split2(jnp.concatenate(products, axis=1))
    for position in range(cols):
        at = 128 * position
        scaled[at : at + 128, :] = (turned[...] * weight[position : position + 1, :]).astype(jnp.bfloat16)
    at = 128 * cols
    scaled[at : at + 16, :] = jnp.concatenate(
        [high.astype(jnp.float32), low.astype(jnp.float32)], axis=0
    ).astype(jnp.bfloat16)
    return dot(scaled[...], plain[...])


def gram_near_kernel(rows, cols, table_ref, b0, b1, b2, b3, out_ref, turned, plain, scaled):
    out_ref[...] = gram_blocks(rows, cols, 0, [b0, b1, b2, b3], table_ref, turned, plain, scaled)


def gram_block(rows, cols, first, block, table_ref, so_far_ref):
    per = rows // 128
    tail = block[rows : rows + 16, :].astype(jnp.float32)
    weights = [table_ref[8 * hi : 8 * hi + 8, :] * tail[hi - first * per : hi - first * per + 1, :] for hi in range(first * per, (first + 1) * per)]
    products = [w * tail[per + k : per + k + 1, :] for k, w in enumerate(weights)]
    plain = block[0:rows, :]
    turned = plain.astype(jnp.float32).T
    weight = jnp.concatenate(weights, axis=1)
    pieces = []
    for position in range(cols):
        scaled = (turned * weight[position : position + 1, :]).astype(jnp.bfloat16)
        pieces.append(so_far_ref[128 * position : 128 * (position + 1), :] + dot(scaled, plain))
    both = above(*[p.astype(jnp.float32) for p in split2(jnp.concatenate(products, axis=1))]).astype(jnp.bfloat16)
    pieces.append(so_far_ref[128 * cols : 128 * cols + 16, :] + dot(both, plain))
    return pieces


def gram_next_kernel(rows, cols, first, table_ref, so_far_ref, block, out_ref):
    for k, piece in enumerate(gram_block(rows, cols, first, block, table_ref, so_far_ref)):
        out_ref[128 * k : 128 * k + piece.shape[0], :] = piece


def gram_last_kernel(rows, cols, first, table_ref, so_far_ref, block, mine_ref, rest_ref):
    half = cols // 2
    pieces = gram_block(rows, cols, first, block, table_ref, so_far_ref)
    for k in range(half):
        mine_ref[128 * k : 128 * (k + 1), :] = pieces[k]
        rest_ref[128 * k : 128 * (k + 1), :] = pieces[half + k].astype(jnp.bfloat16)
    projected = pieces[cols][0:8] + pieces[cols][8:16]
    edge = 128 * half
    mine_ref[edge : edge + 8, :] = projected
    high, low = split2(above(projected[half : 2 * half], jnp.zeros((8 - half, 128), jnp.float32)))
    rest_ref[edge : edge + 16, :] = above(high.astype(jnp.float32), low.astype(jnp.float32)).astype(jnp.bfloat16)


def lanes_from(lane, values, others=0.0):
    return jnp.where(lax.broadcasted_iota(jnp.int32, values.shape, 1) >= lane, values, others)


def fold(grams):
    top = [g[0:32] for g in grams]
    sides = [lanes_from(32, g[32:64], pltpu.roll(g[96:128], 32, 1)) for g in grams]
    third = [g[64:96] for g in grams]
    return above(*top, *sides, lanes_from(64, third[0], pltpu.roll(third[1], 64, 1)), third[2])


def unfold(folded, k, eye):
    side = folded[96 + 32 * k : 128 + 32 * k]
    third = folded[192:224] if k < 2 else folded[224:256]
    third = pltpu.roll(third, 64, 1) if k == 1 else third
    upper_part = above(
        folded[32 * k : 32 * k + 32],
        lanes_from(32, side),
        lanes_from(64, third),
        lanes_from(96, pltpu.roll(side, 96, 1)),
    )
    turned = dot(eye.astype(jnp.bfloat16), upper_part.astype(jnp.bfloat16), ((1,), (1,)))
    below = lax.broadcasted_iota(jnp.int32, eye.shape, 0) // 32 > lax.broadcasted_iota(jnp.int32, eye.shape, 1) // 32
    return jnp.where(below, turned, upper_part)


def join_kernel(half, mine_ref, got_ref, sum_ref, send_ref):
    edge = 128 * half
    got = got_ref[...].astype(jnp.float32)
    total = mine_ref[...] + above(got[0:edge], got[edge : edge + 8] + got[edge + 8 : edge + 16])
    sum_ref[...] = total
    folded = fold([total[128 * k : 128 * (k + 1)] for k in range(half)])
    high, low = split2(total[edge : edge + 8])
    send_ref[...] = above(folded, high.astype(jnp.float32), low.astype(jnp.float32)).astype(jnp.bfloat16)


def beside(*pieces):
    return jnp.concatenate(pieces, axis=1)


def above(*pieces):
    return jnp.concatenate(pieces, axis=0)


def product(a, b):
    (a_high, a_low), (b_high, b_low) = a, b
    return dot(beside(a_high, a_low), above(b_high, b_high)) + dot(a_high, b_low)


def wide(a, b):
    return beside(a[0], b[0]), beside(a[1], b[1])


def vector_product(rows, parts):
    left = above(*[p.astype(jnp.float32) for p in split2(rows)]).astype(jnp.bfloat16)
    full = dot(left, parts[0]) + dot(left, parts[1])
    return full[0:8] + full[8:16]


def solve_kernel(half, sum_ref, got_ref, out_ref):
    size = 128
    spread = float(size - 1)
    eye = identity(size)
    edge = size * half
    got = got_ref[...].astype(jnp.float32)
    projected = sum_ref[edge : edge + 8, :] + got[256:264] + got[264:272]
    norms, bases = [], []
    for k in range(half):
        gram = sum_ref[size * k : size * (k + 1), :] + unfold(got, k, eye)
        squared = jnp.sum(jnp.sum(gram * gram, axis=0, keepdims=True), axis=1, keepdims=True)
        norm = spread + jnp.sqrt(squared)
        norms.append(norm)
        bases.append((spread * eye + gram) / norm)
    base_parts = [split2(base) for base in bases]
    squares = [dot(high, high) for high, _ in base_parts]
    inverses = [
        1.5 * (1.5 * eye - 0.5 * base)
        - 0.5
        * dot(
            (1.5 * base - 0.5 * square).astype(jnp.bfloat16),
            (2.25 * eye - 1.5 * base + 0.25 * square).astype(jnp.bfloat16),
        )
        for base, square in zip(bases, squares)
    ]
    vectors = [jnp.broadcast_to(projected[k : k + 1, :], (8, size)) for k in range(half)]
    pushed = [vector_product(v, parts) for v, parts in zip(vectors, base_parts)]
    carried = None
    for step in range(NS_STEPS - 2):
        last = step == NS_STEPS - 3
        inverse_parts = [split2(z) for z in inverses]
        left = [split2(above(z, v, q)) for z, v, q in zip(inverses, vectors, pushed)] if last else inverse_parts
        both = [product(z, wide(b, y)) for z, b, y in zip(left, base_parts, inverse_parts)]
        forced = [x[:, 0:size] for x in both]
        square = [split2(x[0:size, size : 2 * size]) for x in both]
        if last:
            forced = [above(f[0:size], x[size + 8 : size + 16, size:], x[size + 8 : size + 16, size:]) for f, x in zip(forced, both)]
        cubes = [product(split2(f), y) for f, y in zip(forced, square)]
        if last:
            carried = [1.5 * x[size : size + 8, size:] - 0.5 * c[size : size + 8] for x, c in zip(both, cubes)]
        inverses = [1.5 * z - 0.5 * c[0:size] for z, c in zip(inverses, cubes)]
    scaled = [(jnp.sqrt(spread) / jnp.sqrt(norm)) * inverse for norm, inverse in zip(norms, inverses)]
    means = [
        vector_product(v, split2(inverse))[0:1] / norm for norm, inverse, v in zip(norms, inverses, carried)
    ]
    rest = jnp.zeros((8 - half, size), jnp.float32)
    high, low = split2(above(*means, rest))
    tail = above(high.astype(jnp.float32), low.astype(jnp.float32))
    out_ref[...] = above(fold(scaled), tail).astype(jnp.bfloat16)


def rebuild(folded, k, eye):
    means = folded[256 + k : 257 + k] + folded[264 + k : 265 + k]
    return (unfold(folded, k, eye) + means).astype(jnp.bfloat16)


def identity(size):
    same = lax.broadcasted_iota(jnp.int32, (size, size), 0) == lax.broadcasted_iota(jnp.int32, (size, size), 1)
    return jnp.where(same, 1.0, 0.0)


def shares(size):
    span = SPACING // 2
    shape = (1, span, span, size)
    along_x = lax.broadcasted_iota(jnp.int32, shape, 1).astype(jnp.float32) / (2 * span)
    along_y = lax.broadcasted_iota(jnp.int32, shape, 2).astype(jnp.float32) / (2 * span)
    upper_y = [along_y + (span + 0.5) / (2 * span), along_y + 0.5 / (2 * span)]
    return along_x, upper_y


def mixed(both, share, upper_x, shape):
    high = share * upper_x
    return (share - high) * both[:, 0:128].reshape(shape) + high * both[:, 128:256].reshape(shape)


def near_kernel(cols, members_ref, own, pair, part_ref, pert_ref, table):
    half = cols // 2
    first = lax.rem(lax.axis_index("lev"), 2) == 0
    eye = identity(128)
    mine, theirs = own[...].astype(jnp.float32), pair[...].astype(jnp.float32)
    for at, folded in ((0, jnp.where(first, mine, theirs)), (half, jnp.where(first, theirs, mine))):
        for j in range(half):
            table[128 * (at + j) : 128 * (at + j + 1), :] = rebuild(folded, j, eye)
    levels, width_x, _, size = members_ref.shape
    span = SPACING // 2
    shape = (levels, span, span, size)
    rows = levels * span * span
    along_x, upper_y = shares(size)
    for patch_x in range(width_x // span):
        states = members_ref[:, patch_x * span : (patch_x + 1) * span, :, :].astype(jnp.float32)
        mean = jnp.sum(states, axis=3, keepdims=True) * (1.0 / size)
        moved = states - mean
        column = (patch_x + 1) // 2
        upper_x = along_x + (span + 0.5 if patch_x % 2 == 0 else 0.5) / (2 * span)
        for patch_y in range(2):
            inside = slice(patch_y * span, (patch_y + 1) * span)
            left = moved[:, :, inside, :].reshape(rows, size).astype(jnp.bfloat16)
            pert_ref[patch_x, patch_y] = left
            both = dot(left, table[128 * column : 128 * (column + 2), :], ((1,), (1,)))
            share = upper_y[0] if patch_y == 0 else 1.0 - upper_y[1]
            part_ref[patch_x, patch_y] = (mean[:, :, inside, :] + mixed(both, share, upper_x, shape)).reshape(rows, size)


def add_far(first_patch, count, first_column, table, part_ref, pert_ref, keep):
    levels, size = part_ref.shape[2] // (SPACING // 2) ** 2, part_ref.shape[3]
    span = SPACING // 2
    shape = (levels, span, span, size)
    along_x, upper_y = shares(size)
    for k in range(count):
        patch_x = first_patch + k
        column = lax.div(patch_x + 1, 2) - first_column
        lines = pl.ds(pl.multiple_of(128 * column, 128), 256)
        upper_x = along_x + jnp.where(lax.rem(patch_x, 2) == 0, span + 0.5, 0.5) / (2 * span)
        results = []
        for patch_y in range(2):
            both = dot(pert_ref[patch_x, patch_y], table[patch_y, lines, :], ((1,), (1,)))
            share = 1.0 - upper_y[0] if patch_y == 0 else upper_y[1]
            results.append(part_ref[patch_x, patch_y].reshape(shape) + mixed(both, share, upper_x, shape))
        keep(k, patch_x, jnp.concatenate(results, axis=2).astype(jnp.bfloat16))


def neighbours(climb, descend, own, first):
    tile_y = lax.axis_index("ty")
    up, down, mine = climb[...], descend[...], own[...]
    before = jnp.where(tile_y == 0, mine, jnp.where(first, up, down))
    after = jnp.where(tile_y == lax.axis_size("ty") - 1, mine, jnp.where(first, down, up))
    return before.astype(jnp.float32), after.astype(jnp.float32)


def far_first_kernel(cols, count, part_ref, pert_ref, own, climb, descend, out_ref, border_ref, table):
    half, span = cols // 2, SPACING // 2
    core = lax.rem(lax.axis_index("lev"), 2)
    eye = identity(128)
    for z, folded in enumerate(neighbours(climb, descend, own, core == 0)):
        for j in range(half):
            table[z, 128 * j : 128 * (j + 1), :] = rebuild(folded, j, eye)
    border = jnp.where(core == 0, half - 1, 0)
    border_ref[...] = table[:, pl.ds(pl.multiple_of(128 * border, 128), 128), :]

    def keep(k, _, value):
        out_ref[:, k * span : (k + 1) * span] = value

    add_far(core * (part_ref.shape[0] - count), count, core * half, table, part_ref, pert_ref, keep)


def far_rest_kernel(
    cols, count, part_ref, pert_ref, pair, pair_climb, pair_descend, begun, border_ref, out_hbm, table, staged, sems
):
    half, span = cols // 2, SPACING // 2
    core = lax.rem(lax.axis_index("lev"), 2)
    first = core == 0
    total = part_ref.shape[0]
    early = total - count
    start = core * (total - early) * span
    copies = [pltpu.make_async_copy(begun, out_hbm.at[:, pl.ds(start, early * span)], sems.at[count])]
    copies[0].start()
    eye = identity(128)
    for z, folded in enumerate(neighbours(pair_climb, pair_descend, pair, jnp.logical_not(first))):
        for j in range(half):
            at = pl.multiple_of(128 * j + jnp.where(first, 128, 0), 128)
            table[z, pl.ds(at, 128), :] = rebuild(folded, j, eye)
    at = pl.multiple_of(jnp.where(first, 0, 128 * half), 128)
    table[:, pl.ds(at, 128), :] = border_ref[...]

    def keep(k, patch_x, value):
        inside = pl.ds(patch_x * span, span)
        staged[:, inside] = value
        copies.append(pltpu.make_async_copy(staged.at[:, inside], out_hbm.at[:, inside], sems.at[k]))
        copies[-1].start()

    first_column = jnp.where(first, half - 1, 0)
    add_far((1 - core) * early, count, first_column, table, part_ref, pert_ref, keep)
    for copy in copies:
        copy.wait()


def paired_device(
    members, obs_pert, innovation, obs_precision, obs_owner, obs_slot, obs_count, local_weight
):
    axes = ("tx", "ty", "lev")
    ways = pair_patterns(axes)

    def send(value, way):
        return lax.ppermute(value, axes, ways[way])

    bf16, f32 = jnp.bfloat16, jnp.float32
    rows, size = obs_pert.shape
    cols = obs_owner.shape[0] + 2
    half = cols // 2
    shape = jax.ShapeDtypeStruct
    counts = obs_count.reshape(1, -1)
    lists = (obs_owner, obs_slot, counts, local_weight)
    scalars = [v.reshape(rows // size, size) for v in (innovation, obs_precision)]
    packed = device_call(
        functools.partial(pack_kernel, rows),
        tuple(pltpu.with_memory_space_constraint(v, pltpu.HBM) for v in (obs_pert, *scalars, *lists)),
        shape((rows + 16, size), bf16),
        [pltpu.VMEM(v.shape, v.dtype) for v in scalars]
        + [
            pltpu.VMEM(obs_owner.shape, jnp.int32),
            pltpu.VMEM(obs_slot.shape, jnp.int32),
            pltpu.SMEM(counts.shape, jnp.int32),
            pltpu.VMEM(local_weight.shape, f32),
            pltpu.VMEM((16, size), f32),
            pltpu.SemaphoreType.DMA((7,)),
        ],
        in_hbm=True,
    )
    across = send(packed, "across")
    climb, descend = send(packed, "climb"), send(packed, "descend")
    across_climb, across_descend = send(across, "climb"), send(across, "descend")
    table = device_call(
        functools.partial(table_kernel, rows, cols),
        (*lists, across),
        shape((128, 128), f32),
        flops=6 * 2 * 48 * 256 * 128,
    )
    tall = size * cols + 16
    near = device_call(
        functools.partial(gram_near_kernel, rows, cols),
        (table, packed, climb, descend, across),
        shape((tall, size), f32),
        [
            pltpu.VMEM((size, 4 * rows), f32),
            pltpu.VMEM((4 * rows, size), bf16),
            pltpu.VMEM((tall, 4 * rows), bf16),
        ],
        flops=2 * tall * size * 4 * rows,
    )
    near = device_call(
        functools.partial(gram_next_kernel, rows, cols, 5),
        (table, near, across_descend),
        shape((tall, size), f32),
        flops=2 * tall * size * rows,
    )
    mine, rest = device_call(
        functools.partial(gram_last_kernel, rows, cols, 4),
        (table, near, across_climb),
        [shape((size * half + 8, size), f32), shape((size * half + 16, size), bf16)],
        flops=2 * tall * size * rows,
    )
    total, half_sum = device_call(
        functools.partial(join_kernel, half),
        (mine, send(rest, "core")),
        [shape((size * half + 8, size), f32), shape((272, size), bf16)],
    )
    weights = device_call(
        functools.partial(solve_kernel, half),
        (total, send(half_sum, "half")),
        shape((272, size), bf16),
        flops=2 * 27 * half * size**3,
    )
    pair = send(weights, "core")
    up = send(weights, "climb")
    down = send(weights, "descend")
    levels, width_x, width_y, _ = members.shape
    patches = (width_x * 2 // SPACING, 2, levels * SPACING**2 // 4, size)
    part, pert = device_call(
        functools.partial(near_kernel, cols),
        (members, weights, pair),
        [shape(patches, f32), shape(patches, bf16)],
        [pltpu.VMEM((cols * size, size), bf16)],
        flops=2 * levels * width_x * width_y * size * 2 * size,
    )
    up, down, part = lax.optimization_barrier((up, down, part))
    pair_up, pair_down = send(up, "core"), send(down, "core")
    early, span = cols // 2, SPACING // 2
    begun, border = device_call(
        functools.partial(far_first_kernel, cols, early),
        (part, pert, weights, up, down),
        [shape((levels, early * span, width_y, size), bf16), shape((2, size, size), bf16)],
        [pltpu.VMEM((2, half * size, size), bf16)],
        flops=2 * levels * span * early * width_y * size * 2 * size,
    )
    count = patches[0] - early
    return device_call(
        functools.partial(far_rest_kernel, cols, count),
        (part, pert, pair, pair_up, pair_down, begun, border),
        shape(members.shape, bf16),
        [
            pltpu.VMEM((2, (half + 1) * size, size), bf16),
            pltpu.VMEM(members.shape, bf16),
            pltpu.SemaphoreType.DMA((count + 1,)),
        ],
        flops=2 * levels * span * count * width_y * size * 2 * size,
        out_hbm=True,
    )


def fits_pairs(mesh, members, obs_pert, obs_owner):
    sizes = dict(mesh.shape)
    return (
        sizes["tx"] == 2
        and sizes["lev"] == 4
        and obs_pert == (256, 128)
        and obs_owner == (4, 1, 256)
        and members[1:] == (64, 16, 128)
    )


def solution(mesh):
    placed = (
        P("lev", "tx", "ty", None),
        P(("tx", "ty", "lev"), None),
        P(("tx", "ty", "lev")),
        P(("tx", "ty", "lev")),
        P("tx", "ty", None),
        P("tx", "ty", None),
        P("tx", "ty"),
        P("tx", "ty", None),
    )

    def local(members, obs_pert, innovation, obs_precision, obs_owner, *rest):
        paired = fits_pairs(mesh, members.shape, obs_pert.shape, obs_owner.shape)
        return (paired_device if paired else per_device)(
            members, obs_pert, innovation, obs_precision, obs_owner, *rest
        )

    return jax.shard_map(
        local,
        mesh=mesh,
        in_specs=placed,
        out_specs=P("lev", "tx", "ty", None),
        check_vma=False,
    )
```

```python
import functools

import jax
import jax.numpy as jnp
from jax import lax
from jax.experimental import pallas as pl
from jax.experimental.pallas import tpu as pltpu
from jax.sharding import PartitionSpec as P


SPACING = 16
NS_STEPS = 4
VMEM_LIMIT = 12 << 20


def padded(array, sides, width):
    for axis, dim in sides:
        size, length = (lax.axis_size(axis), array.shape[dim])
        up = [(i, (i + 1) % size) for i in range(size - 1)]
        down = [(j, i) for i, j in up]
        last = lax.slice_in_dim(array, length - width, length, axis=dim)
        initial = lax.slice_in_dim(array, 0, width, axis=dim)
        before = lax.ppermute(last, axis, up)
        after = lax.ppermute(initial, axis, down)
        array = jnp.concatenate([before, array, after], axis=dim)
    return array


def finish_solve(gram_matrix, projected):
    member_count = gram_matrix.shape[1]
    spread = float(member_count - 1)
    identity = jnp.eye(member_count, dtype=jnp.float32)
    scale_norm = spread + jnp.sqrt(jnp.sum(gram_matrix * gram_matrix, axis=(1, 2)))
    sqrt_iter = (spread * identity + gram_matrix) / scale_norm[:, None, None]
    inv_iter = jnp.broadcast_to(identity, sqrt_iter.shape)
    for _ in range(NS_STEPS):
        middle = 1.5 * identity - 0.5 * jnp.einsum(
            "bij,bjk->bik", inv_iter, sqrt_iter, precision=lax.Precision.HIGHEST
        )
        sqrt_iter = jnp.einsum("bij,bjk->bik", sqrt_iter, middle, precision=lax.Precision.HIGHEST)
        inv_iter = jnp.einsum("bij,bjk->bik", middle, inv_iter, precision=lax.Precision.HIGHEST)
    inner = jnp.einsum("bij,bj->bi", inv_iter, projected, precision=lax.Precision.HIGHEST)
    mean_weights = (
        jnp.einsum("bij,bj->bi", inv_iter, inner, precision=lax.Precision.HIGHEST)
        / scale_norm[:, None]
    )
    transform = (jnp.sqrt(spread) / jnp.sqrt(scale_norm))[:, None, None] * inv_iter + mean_weights[
        :, :, None
    ]
    return transform.astype(jnp.bfloat16)


def fractions(count, half_span):
    place = jnp.arange(count)[:, None]
    within = jnp.arange(half_span)[None, :].astype(jnp.float32)
    return jnp.where(
        place % 2 == 0,
        (within + half_span + 0.5) / (2 * half_span),
        (within + 0.5) / (2 * half_span),
    )


def solve_columns(lookup, counts, local_part, flat_pert, flat_values):
    column_count, slots = lookup.shape
    member_count = flat_pert.shape[1]
    block_len = min(slots, 128)
    live_blocks = (jnp.max(counts) + block_len - 1) // block_len

    def add_block(block_index, carry):
        gram_matrix, projected = carry
        offset = block_index * block_len
        slot_rows = lax.dynamic_slice_in_dim(lookup, offset, block_len, 1)
        slot_local = lax.dynamic_slice_in_dim(local_part, offset, block_len, 1)
        position = offset + jnp.arange(block_len)
        active = position[None, :] < counts[:, None]
        pert_rows = flat_pert[slot_rows].astype(jnp.float32)
        picked = flat_values[:, slot_rows]
        precision_w = jnp.where(active, picked[1].astype(jnp.float32) * slot_local, 0.0)
        departure = picked[0].astype(jnp.float32)
        gram_matrix = gram_matrix + jnp.einsum(
            "bsk,bsm->bkm",
            pert_rows * precision_w[:, :, None],
            pert_rows,
            precision=lax.Precision.HIGHEST,
        )
        projected = projected + jnp.einsum(
            "bsk,bs->bk", pert_rows, precision_w * departure, precision=lax.Precision.HIGHEST
        )
        return (gram_matrix, projected)

    start_gram = jnp.zeros((column_count, member_count, member_count), jnp.float32)
    start_proj = jnp.zeros((column_count, member_count), jnp.float32)
    gram_matrix, projected = lax.fori_loop(0, live_blocks, add_block, (start_gram, start_proj))
    return finish_solve(gram_matrix, projected)


def clamp_edges(rimmed, axis_index, axis_count, dim):
    lower = jnp.where(
        axis_index == 0,
        lax.slice_in_dim(rimmed, 1, 2, axis=dim),
        lax.slice_in_dim(rimmed, 0, 1, axis=dim),
    )
    last = rimmed.shape[dim]
    upper = jnp.where(
        axis_index == axis_count - 1,
        lax.slice_in_dim(rimmed, last - 2, last - 1, axis=dim),
        lax.slice_in_dim(rimmed, last - 1, last, axis=dim),
    )
    return jnp.concatenate(
        [lower, lax.slice_in_dim(rimmed, 1, last - 1, axis=dim), upper], axis=dim
    )


def per_device(
    members, obs_pert, innovation, obs_precision, obs_owner, obs_slot, obs_count, local_weight
):
    scalars = jnp.stack([innovation, obs_precision])
    tile_pert, tile_values = (
        lax.all_gather(obs_pert, "lev", axis=0, tiled=True),
        lax.all_gather(scalars, "lev", axis=1, tiled=True),
    )
    near_pert, near_values = (
        padded(tile_pert[None, None], (("tx", 0), ("ty", 1)), 1),
        padded(tile_values[None, None], (("tx", 0), ("ty", 1)), 1),
    )
    tile_len = near_pert.shape[2]
    member_count = near_pert.shape[3]
    flat_pert = near_pert.reshape(9 * tile_len, member_count)
    flat_values = jnp.transpose(near_values, (2, 0, 1, 3)).reshape(2, 9 * tile_len)
    column_x = lax.axis_index("tx")
    column_y = lax.axis_index("ty")
    tiles_x = lax.axis_size("tx")
    tiles_y = lax.axis_size("ty")
    near_x = obs_owner // tiles_y - column_x + 1
    near_y = obs_owner % tiles_y - column_y + 1
    lookup = (near_x * 3 + near_y) * tile_len + obs_slot
    coarse_x, coarse_y, slots = lookup.shape
    lookup = lookup.reshape(coarse_x * coarse_y, slots)
    counts = obs_count.reshape(coarse_x * coarse_y)
    local_part = local_weight.reshape(coarse_x * coarse_y, slots)
    weights = solve_columns(lookup, counts, local_part, flat_pert, flat_values)
    weights = weights.reshape(coarse_x, coarse_y, member_count, member_count)
    rimmed = padded(weights, (("tx", 0), ("ty", 1)), 1)
    rimmed = clamp_edges(rimmed, column_x, tiles_x, 0)
    rimmed = clamp_edges(rimmed, column_y, tiles_y, 1)
    doubled = jnp.repeat(jnp.repeat(rimmed, 2, axis=0), 2, axis=1)
    level_count, width_x, width_y, _ = members.shape
    half_span = SPACING // 2
    patch_x = width_x // half_span
    patch_y = width_y // half_span
    frac_x = fractions(patch_x, half_span)
    frac_y = fractions(patch_y, half_span)
    ens_mean = jnp.mean(members, axis=3, keepdims=True, dtype=jnp.float32)
    pert = (members.astype(jnp.float32) - ens_mean).astype(jnp.bfloat16)
    patched = pert.reshape(level_count, patch_x, half_span, patch_y, half_span, member_count)
    summed = jnp.zeros(patched.shape, jnp.float32)
    for upper_x in range(2):
        for upper_y in range(2):
            corner = doubled[
                1 + 2 * upper_x : 1 + 2 * upper_x + patch_x,
                1 + 2 * upper_y : 1 + 2 * upper_y + patch_y,
            ]
            product = jnp.einsum(
                "lxaybi,xyij->lxaybj", patched, corner, preferred_element_type=jnp.float32
            )
            factor_x = frac_x if upper_x == 1 else 1.0 - frac_x
            factor_y = frac_y if upper_y == 1 else 1.0 - frac_y
            summed = (
                summed
                + product
                * factor_x[None, :, :, None, None, None]
                * factor_y[None, None, None, :, :, None]
            )
    return (ens_mean + summed.reshape(members.shape)).astype(jnp.bfloat16)


def pair_patterns(mesh_axes):
    tiles_x, tiles_y, parts = (lax.axis_size(a) for a in mesh_axes)

    def flat(x, y, l):
        return (x * tiles_y + y) * parts + l

    def table(move):
        return [
            (flat(x, y, l), flat(*move(x, y, l)))
            for x in range(tiles_x)
            for y in range(tiles_y)
            for l in range(parts)
        ]

    def climb(x, y, l):
        if l % 2 == 0:
            return (x, y + 1, l) if y < tiles_y - 1 else (x, y, l + 1)
        return (x, y - 1, l) if y > 0 else (x, y, l - 1)

    climbing = table(climb)
    return {
        "across": table(lambda x, y, l: (1 - x, y, l)),
        "core": table(lambda x, y, l: (x, y, l ^ 1)),
        "half": table(lambda x, y, l: (x, y, l ^ 2)),
        "climb": climbing,
        "descend": [(b, a) for a, b in climbing],
    }


def device_call(kernel, operands, out_shape, scratch=(), flops=0, in_hbm=False, out_hbm=False):
    single = not isinstance(out_shape, (list, tuple))
    spec = pl.BlockSpec(memory_space=pltpu.VMEM)
    hbm = pl.BlockSpec(memory_space=pltpu.HBM)
    out_spec = hbm if out_hbm else spec
    return pl.pallas_call(
        kernel,
        out_shape=out_shape,
        in_specs=[hbm if in_hbm else spec] * len(operands),
        out_specs=out_spec if single else [out_spec] * len(out_shape),
        scratch_shapes=list(scratch),
        cost_estimate=pl.CostEstimate(flops=flops, bytes_accessed=1 << 18, transcendentals=0),
        compiler_params=pltpu.CompilerParams(vmem_limit_bytes=VMEM_LIMIT),
    )(*operands)


def split2(value):
    high = value.astype(jnp.bfloat16)
    return high, (value - high.astype(jnp.float32)).astype(jnp.bfloat16)


def split3(value):
    high, _ = split2(value)
    rest = value - high.astype(jnp.float32)
    middle, low = split2(rest)
    return high, middle, low


def dot(a, b, dims=((1,), (0,))):
    return lax.dot_general(a, b, (dims, ((), ())), preferred_element_type=jnp.float32)


def pack_kernel(
    rows, pert, inn, prec, owner, slot, count, local, out_ref, inn_ref, prec_ref, owner_ref, slot_ref, count_ref, local_ref, tail, sems
):
    sources = (owner, slot, count, local, inn, prec, pert)
    targets = (owner_ref, slot_ref, count_ref, local_ref, inn_ref, prec_ref, out_ref.at[0:rows, :])
    copies = [pltpu.make_async_copy(x, y, sems.at[k]) for k, (x, y) in enumerate(zip(sources, targets))]
    for copy in copies:
        copy.start()
    for copy in copies[:-1]:
        copy.wait()
    edge = jnp.where(lax.axis_index("tx") == 0, owner_ref.shape[0] - 1, 0)
    slots = owner_ref.shape[2]
    limit = jnp.where(edge == 0, count_ref[0, 0], count_ref[0, owner_ref.shape[0] - 1])
    active = lax.broadcasted_iota(jnp.int32, (1, slots), 1) < limit
    local_part = jnp.where(active, local_ref[edge], 0.0)
    slot_part = slot_ref[edge]
    for k, ref in enumerate((prec_ref, inn_ref)):
        tail[2 * k : 2 * k + 2, :] = ref[...].astype(jnp.float32)
    lists = [
        owner_ref[edge].astype(jnp.float32),
        (slot_part // 128).astype(jnp.float32),
        (slot_part % 128).astype(jnp.float32),
    ] + [piece.astype(jnp.float32) for piece in split3(local_part)]
    for k, row in enumerate(lists):
        for part in range(2):
            tail[4 + 2 * k + part : 5 + 2 * k + part, :] = row[:, 128 * part : 128 * (part + 1)]
    out_ref[rows : rows + 16, :] = tail[...].astype(jnp.bfloat16)
    copies[-1].wait()


def table_kernel(rows, cols, owner_ref, slot_ref, count_ref, local_ref, other_ref, out_ref):
    tile_x, tile_y, part = (lax.axis_index(a) for a in ("tx", "ty", "lev"))
    tiles_y = lax.axis_size("ty")
    core = lax.rem(part, 2)
    own, slots = owner_ref.shape[0], owner_ref.shape[2]
    received = other_ref[rows : rows + 16, :].astype(jnp.float32)

    def listed(k):
        return jnp.concatenate([received[2 * k : 2 * k + 1, :], received[2 * k + 1 : 2 * k + 2, :]], axis=1)

    far_owner = listed(2).astype(jnp.int32)
    far_slot = (listed(3) * 128.0 + listed(4)).astype(jnp.int32)
    far_local = listed(5) + listed(6) + listed(7)
    position_in = lax.broadcasted_iota(jnp.int32, (1, slots), 1)

    def own_list(k):
        return owner_ref[k], slot_ref[k], jnp.where(position_in < count_ref[0, k], local_ref[k], 0.0)

    def pick(use_far, k):
        return tuple(jnp.where(use_far, a, b) for a, b in zip((far_owner, far_slot, far_local), own_list(k)))

    lists = [pick(tile_x > 0, 0)] + [own_list(k) for k in range(own)] + [pick(tile_x == 0, own - 1)]
    half = cols // 2
    out_ref[...] = jnp.zeros_like(out_ref)
    for g, (owner, slot, local) in enumerate(lists):
        across = jnp.where(owner // tiles_y == tile_x, 0, 1)
        near = owner % tiles_y - tile_y
        first_way = jnp.where(core == 0, -1, 1)
        block = across * 3 + jnp.where(near == 0, 0, jnp.where(near == first_way, 1, 2))
        mine = slot // rows == part
        within = slot % rows
        high = jnp.where(mine, block * (rows // 128) + within // 128, -1)
        low = within % 128
        picked = jnp.where(lax.broadcasted_iota(jnp.int32, (16, slots), 0) == high, local, 0.0)
        hot = jnp.where(lax.broadcasted_iota(jnp.int32, (128, slots), 0) == low, 1.0, 0.0).astype(jnp.bfloat16)
        parts = split3(picked)
        total = dot(parts[0], hot, ((1,), (1,)))
        for piece in parts[1:]:
            total = total + dot(piece, hot, ((1,), (1,)))
        place = lax.rem(g - core * half + cols, cols)
        out_ref[pl.ds(place, 16, stride=8), :] = total


def gram_blocks(rows, cols, first, blocks, table_ref, turned, plain, scaled):
    per = rows // 128
    products, weights = [], []
    for k, ref in enumerate(blocks):
        tail = ref[rows : rows + 16, :].astype(jnp.float32)
        for part in range(per):
            hi = (first + k) * per + part
            row = table_ref[8 * hi : 8 * hi + 8, :] * tail[part : part + 1, :]
            weights.append(row)
            products.append(row * tail[per + part : per + part + 1, :])
        block = ref[0:rows, :]
        plain[rows * k : rows * (k + 1), :] = block
        turned[:, rows * k : rows * (k + 1)] = block.astype(jnp.float32).T
    weight = jnp.concatenate(weights, axis=1)
    high, low = split2(jnp.concatenate(products, axis=1))
    for position in range(cols):
        at = 128 * position
        scaled[at : at + 128, :] = (turned[...] * weight[position : position + 1, :]).astype(jnp.bfloat16)
    at = 128 * cols
    scaled[at : at + 16, :] = jnp.concatenate(
        [high.astype(jnp.float32), low.astype(jnp.float32)], axis=0
    ).astype(jnp.bfloat16)
    return dot(scaled[...], plain[...])


def gram_near_kernel(rows, cols, table_ref, b0, b1, b2, b3, out_ref, turned, plain, scaled):
    out_ref[...] = gram_blocks(rows, cols, 0, [b0, b1, b2, b3], table_ref, turned, plain, scaled)


def block_sums(rows, first, block, table_ref, positions):
    per = rows // 128
    tail = block[rows : rows + 16, :].astype(jnp.float32)
    weights = [table_ref[8 * hi : 8 * hi + 8, :] * tail[k : k + 1, :] for k, hi in enumerate(range(first * per, (first + 1) * per))]
    products = [w * tail[per + k : per + k + 1, :] for k, w in enumerate(weights)]
    plain = block[0:rows, :]
    turned = plain.astype(jnp.float32).T
    weight = beside(*weights)
    both = above(*[p.astype(jnp.float32) for p in split2(beside(*products))]).astype(jnp.bfloat16)
    return [dot((turned * weight[p : p + 1, :]).astype(jnp.bfloat16), plain) for p in positions] + [dot(both, plain)]


def earlier_sums(cols, so_far_ref, positions):
    return [so_far_ref[128 * p : 128 * (p + 1), :] for p in positions] + [so_far_ref[128 * cols : 128 * cols + 16, :]]


def rest_next_kernel(rows, cols, first, table_ref, so_far_ref, block, out_ref):
    positions = range(cols // 2, cols)
    pieces = zip(earlier_sums(cols, so_far_ref, positions), block_sums(rows, first, block, table_ref, positions))
    for k, (x, y) in enumerate(pieces):
        out_ref[128 * k : 128 * k + x.shape[0], :] = x + y


def rest_last_kernel(rows, cols, first, table_ref, so_far_ref, block, out_ref):
    half = cols // 2
    edge = 128 * half
    news = block_sums(rows, first, block, table_ref, range(half, cols))
    for k in range(half):
        part = slice(128 * k, 128 * (k + 1))
        out_ref[part, :] = (so_far_ref[part, :] + news[k]).astype(jnp.bfloat16)
    both = so_far_ref[edge : edge + 16, :] + news[half]
    projected = both[0:8] + both[8:16]
    high, low = split2(above(projected[half : 2 * half], jnp.zeros((8 - half, 128), jnp.float32)))
    out_ref[edge : edge + 16, :] = above(high.astype(jnp.float32), low.astype(jnp.float32)).astype(jnp.bfloat16)


def mine_kernel(rows, cols, first, table_ref, so_far_ref, b4, b5, out_ref):
    half = cols // 2
    positions = range(half)
    groups = [earlier_sums(cols, so_far_ref, positions)]
    groups += [block_sums(rows, first + k, block, table_ref, positions) for k, block in enumerate((b4, b5))]
    sums = [x + y + z for x, y, z in zip(*groups)]
    for k in range(half):
        out_ref[128 * k : 128 * (k + 1), :] = sums[k]
    out_ref[128 * half : 128 * half + 8, :] = sums[half][0:8] + sums[half][8:16]


def lanes_from(lane, values, others=0.0):
    return jnp.where(lax.broadcasted_iota(jnp.int32, values.shape, 1) >= lane, values, others)


def fold(grams):
    top = [g[0:32] for g in grams]
    sides = [lanes_from(32, g[32:64], pltpu.roll(g[96:128], 32, 1)) for g in grams]
    third = [g[64:96] for g in grams]
    return above(*top, *sides, lanes_from(64, third[0], pltpu.roll(third[1], 64, 1)), third[2])


def unfold(folded, k, eye):
    side = folded[96 + 32 * k : 128 + 32 * k]
    third = folded[192:224] if k < 2 else folded[224:256]
    third = pltpu.roll(third, 64, 1) if k == 1 else third
    upper_part = above(
        folded[32 * k : 32 * k + 32],
        lanes_from(32, side),
        lanes_from(64, third),
        lanes_from(96, pltpu.roll(side, 96, 1)),
    )
    turned = dot(eye.astype(jnp.bfloat16), upper_part.astype(jnp.bfloat16), ((1,), (1,)))
    below = lax.broadcasted_iota(jnp.int32, eye.shape, 0) // 32 > lax.broadcasted_iota(jnp.int32, eye.shape, 1) // 32
    return jnp.where(below, turned, upper_part)


def join_kernel(half, mine_ref, got_ref, sum_ref, send_ref):
    edge = 128 * half
    got = got_ref[...].astype(jnp.float32)
    total = mine_ref[...] + above(got[0:edge], got[edge : edge + 8] + got[edge + 8 : edge + 16])
    sum_ref[...] = total
    folded = fold([total[128 * k : 128 * (k + 1)] for k in range(half)])
    high, low = split2(total[edge : edge + 8])
    send_ref[...] = above(folded, high.astype(jnp.float32), low.astype(jnp.float32)).astype(jnp.bfloat16)


def beside(*pieces):
    return jnp.concatenate(pieces, axis=1)


def above(*pieces):
    return jnp.concatenate(pieces, axis=0)


def product(a, b):
    (a_high, a_low), (b_high, b_low) = a, b
    return dot(beside(a_high, a_low), above(b_high, b_high)) + dot(a_high, b_low)


def wide(a, b):
    return beside(a[0], b[0]), beside(a[1], b[1])


def vector_product(rows, parts):
    left = above(*[p.astype(jnp.float32) for p in split2(rows)]).astype(jnp.bfloat16)
    full = dot(left, parts[0]) + dot(left, parts[1])
    return full[0:8] + full[8:16]


def solve_kernel(half, sum_ref, got_ref, out_ref):
    size = 128
    spread = float(size - 1)
    eye = identity(size)
    edge = size * half
    got = got_ref[...].astype(jnp.float32)
    projected = sum_ref[edge : edge + 8, :] + got[256:264] + got[264:272]
    norms, bases = [], []
    for k in range(half):
        gram = sum_ref[size * k : size * (k + 1), :] + unfold(got, k, eye)
        squared = jnp.sum(jnp.sum(gram * gram, axis=0, keepdims=True), axis=1, keepdims=True)
        norm = spread + jnp.sqrt(squared)
        norms.append(norm)
        bases.append((spread * eye + gram) / norm)
    base_parts = [split2(base) for base in bases]
    squares = [dot(high, high) for high, _ in base_parts]
    inverses = [
        1.5 * (1.5 * eye - 0.5 * base)
        - 0.5
        * dot(
            (1.5 * base - 0.5 * square).astype(jnp.bfloat16),
            (2.25 * eye - 1.5 * base + 0.25 * square).astype(jnp.bfloat16),
        )
        for base, square in zip(bases, squares)
    ]
    vectors = [jnp.broadcast_to(projected[k : k + 1, :], (8, size)) for k in range(half)]
    pushed = [vector_product(v, parts) for v, parts in zip(vectors, base_parts)]
    carried = None
    for step in range(NS_STEPS - 2):
        last = step == NS_STEPS - 3
        inverse_parts = [split2(z) for z in inverses]
        left = [split2(above(z, v, q)) for z, v, q in zip(inverses, vectors, pushed)] if last else inverse_parts
        both = [product(z, wide(b, y)) for z, b, y in zip(left, base_parts, inverse_parts)]
        forced = [x[:, 0:size] for x in both]
        square = [split2(x[0:size, size : 2 * size]) for x in both]
        if last:
            forced = [above(f[0:size], x[size + 8 : size + 16, size:], x[size + 8 : size + 16, size:]) for f, x in zip(forced, both)]
        cubes = [product(split2(f), y) for f, y in zip(forced, square)]
        if last:
            carried = [1.5 * x[size : size + 8, size:] - 0.5 * c[size : size + 8] for x, c in zip(both, cubes)]
        inverses = [1.5 * z - 0.5 * c[0:size] for z, c in zip(inverses, cubes)]
    scaled = [(jnp.sqrt(spread) / jnp.sqrt(norm)) * inverse for norm, inverse in zip(norms, inverses)]
    means = [
        vector_product(v, split2(inverse))[0:1] / norm for norm, inverse, v in zip(norms, inverses, carried)
    ]
    rest = jnp.zeros((8 - half, size), jnp.float32)
    high, low = split2(above(*means, rest))
    tail = above(high.astype(jnp.float32), low.astype(jnp.float32))
    out_ref[...] = above(fold(scaled), tail).astype(jnp.bfloat16)


def rebuild(folded, k, eye):
    means = folded[256 + k : 257 + k] + folded[264 + k : 265 + k]
    return (unfold(folded, k, eye) + means).astype(jnp.bfloat16)


def identity(size):
    same = lax.broadcasted_iota(jnp.int32, (size, size), 0) == lax.broadcasted_iota(jnp.int32, (size, size), 1)
    return jnp.where(same, 1.0, 0.0)


def shares(size):
    span = SPACING // 2
    shape = (1, span, span, size)
    along_x = lax.broadcasted_iota(jnp.int32, shape, 1).astype(jnp.float32) / (2 * span)
    along_y = lax.broadcasted_iota(jnp.int32, shape, 2).astype(jnp.float32) / (2 * span)
    upper_y = [along_y + (span + 0.5) / (2 * span), along_y + 0.5 / (2 * span)]
    return along_x, upper_y


def mixed(both, share, upper_x, shape):
    high = share * upper_x
    return (share - high) * both[:, 0:128].reshape(shape) + high * both[:, 128:256].reshape(shape)


def near_kernel(cols, members_ref, own, pair, part_ref, pert_ref, table):
    half = cols // 2
    first = lax.rem(lax.axis_index("lev"), 2) == 0
    eye = identity(128)
    mine, theirs = own[...].astype(jnp.float32), pair[...].astype(jnp.float32)
    for at, folded in ((0, jnp.where(first, mine, theirs)), (half, jnp.where(first, theirs, mine))):
        for j in range(half):
            table[128 * (at + j) : 128 * (at + j + 1), :] = rebuild(folded, j, eye)
    levels, width_x, _, size = members_ref.shape
    span = SPACING // 2
    shape = (levels, span, span, size)
    rows = levels * span * span
    along_x, upper_y = shares(size)
    for patch_x in range(width_x // span):
        states = members_ref[:, patch_x * span : (patch_x + 1) * span, :, :].astype(jnp.float32)
        mean = jnp.sum(states, axis=3, keepdims=True) * (1.0 / size)
        moved = states - mean
        column = (patch_x + 1) // 2
        upper_x = along_x + (span + 0.5 if patch_x % 2 == 0 else 0.5) / (2 * span)
        for patch_y in range(2):
            inside = slice(patch_y * span, (patch_y + 1) * span)
            left = moved[:, :, inside, :].reshape(rows, size).astype(jnp.bfloat16)
            pert_ref[patch_x, patch_y] = left
            both = dot(left, table[128 * column : 128 * (column + 2), :], ((1,), (1,)))
            share = upper_y[0] if patch_y == 0 else 1.0 - upper_y[1]
            part_ref[patch_x, patch_y] = (mean[:, :, inside, :] + mixed(both, share, upper_x, shape)).reshape(rows, size)


def add_far(first_patch, count, first_column, table, part_ref, pert_ref, keep):
    levels, size = part_ref.shape[2] // (SPACING // 2) ** 2, part_ref.shape[3]
    span = SPACING // 2
    shape = (levels, span, span, size)
    along_x, upper_y = shares(size)
    for k in range(count):
        patch_x = first_patch + k
        column = lax.div(patch_x + 1, 2) - first_column
        lines = pl.ds(pl.multiple_of(128 * column, 128), 256)
        upper_x = along_x + jnp.where(lax.rem(patch_x, 2) == 0, span + 0.5, 0.5) / (2 * span)
        results = []
        for patch_y in range(2):
            both = dot(pert_ref[patch_x, patch_y], table[patch_y, lines, :], ((1,), (1,)))
            share = 1.0 - upper_y[0] if patch_y == 0 else upper_y[1]
            results.append(part_ref[patch_x, patch_y].reshape(shape) + mixed(both, share, upper_x, shape))
        keep(k, patch_x, jnp.concatenate(results, axis=2).astype(jnp.bfloat16))


def neighbours(climb, descend, own, first):
    tile_y = lax.axis_index("ty")
    up, down, mine = climb[...], descend[...], own[...]
    before = jnp.where(tile_y == 0, mine, jnp.where(first, up, down))
    after = jnp.where(tile_y == lax.axis_size("ty") - 1, mine, jnp.where(first, down, up))
    return before.astype(jnp.float32), after.astype(jnp.float32)


def far_first_kernel(cols, count, part_ref, pert_ref, own, climb, descend, out_ref, border_ref, table):
    half, span = cols // 2, SPACING // 2
    core = lax.rem(lax.axis_index("lev"), 2)
    eye = identity(128)
    for z, folded in enumerate(neighbours(climb, descend, own, core == 0)):
        for j in range(half):
            table[z, 128 * j : 128 * (j + 1), :] = rebuild(folded, j, eye)
    border = jnp.where(core == 0, half - 1, 0)
    border_ref[...] = table[:, pl.ds(pl.multiple_of(128 * border, 128), 128), :]

    def keep(k, _, value):
        out_ref[:, k * span : (k + 1) * span] = value

    add_far(core * (part_ref.shape[0] - count), count, core * half, table, part_ref, pert_ref, keep)


def far_rest_kernel(
    cols, count, part_ref, pert_ref, pair, pair_climb, pair_descend, begun, border_ref, out_hbm, table, staged, sems
):
    half, span = cols // 2, SPACING // 2
    core = lax.rem(lax.axis_index("lev"), 2)
    first = core == 0
    total = part_ref.shape[0]
    early = total - count
    start = core * (total - early) * span
    copies = [pltpu.make_async_copy(begun, out_hbm.at[:, pl.ds(start, early * span)], sems.at[count])]
    copies[0].start()
    eye = identity(128)
    for z, folded in enumerate(neighbours(pair_climb, pair_descend, pair, jnp.logical_not(first))):
        for j in range(half):
            at = pl.multiple_of(128 * j + jnp.where(first, 128, 0), 128)
            table[z, pl.ds(at, 128), :] = rebuild(folded, j, eye)
    at = pl.multiple_of(jnp.where(first, 0, 128 * half), 128)
    table[:, pl.ds(at, 128), :] = border_ref[...]

    def keep(k, patch_x, value):
        inside = pl.ds(patch_x * span, span)
        staged[:, inside] = value
        copies.append(pltpu.make_async_copy(staged.at[:, inside], out_hbm.at[:, inside], sems.at[k]))
        copies[-1].start()

    first_column = jnp.where(first, half - 1, 0)
    add_far((1 - core) * early, count, first_column, table, part_ref, pert_ref, keep)
    for copy in copies:
        copy.wait()


def paired_device(
    members, obs_pert, innovation, obs_precision, obs_owner, obs_slot, obs_count, local_weight
):
    axes = ("tx", "ty", "lev")
    ways = pair_patterns(axes)

    def send(value, way):
        return lax.ppermute(value, axes, ways[way])

    bf16, f32 = jnp.bfloat16, jnp.float32
    rows, size = obs_pert.shape
    cols = obs_owner.shape[0] + 2
    half = cols // 2
    shape = jax.ShapeDtypeStruct
    counts = obs_count.reshape(1, -1)
    lists = (obs_owner, obs_slot, counts, local_weight)
    scalars = [v.reshape(rows // size, size) for v in (innovation, obs_precision)]
    packed = device_call(
        functools.partial(pack_kernel, rows),
        tuple(pltpu.with_memory_space_constraint(v, pltpu.HBM) for v in (obs_pert, *scalars, *lists)),
        shape((rows + 16, size), bf16),
        [pltpu.VMEM(v.shape, v.dtype) for v in scalars]
        + [
            pltpu.VMEM(obs_owner.shape, jnp.int32),
            pltpu.VMEM(obs_slot.shape, jnp.int32),
            pltpu.SMEM(counts.shape, jnp.int32),
            pltpu.VMEM(local_weight.shape, f32),
            pltpu.VMEM((16, size), f32),
            pltpu.SemaphoreType.DMA((7,)),
        ],
        in_hbm=True,
    )
    across = send(packed, "across")
    climb, descend = send(packed, "climb"), send(packed, "descend")
    across_climb, across_descend = send(across, "climb"), send(across, "descend")
    table = device_call(
        functools.partial(table_kernel, rows, cols),
        (*lists, across),
        shape((128, 128), f32),
        flops=6 * 2 * 48 * 256 * 128,
    )
    tall = size * cols + 16
    near = device_call(
        functools.partial(gram_near_kernel, rows, cols),
        (table, packed, climb, descend, across),
        shape((tall, size), f32),
        [
            pltpu.VMEM((size, 4 * rows), f32),
            pltpu.VMEM((4 * rows, size), bf16),
            pltpu.VMEM((tall, 4 * rows), bf16),
        ],
        flops=2 * tall * size * 4 * rows,
    )
    rest = device_call(
        functools.partial(rest_next_kernel, rows, cols, 5),
        (table, near, across_descend),
        shape((size * half + 16, size), f32),
        flops=tall * size * rows,
    )
    rest = device_call(
        functools.partial(rest_last_kernel, rows, cols, 4),
        (table, rest, across_climb),
        shape((size * half + 16, size), bf16),
        flops=tall * size * rows,
    )
    mine = device_call(
        functools.partial(mine_kernel, rows, cols, 4),
        (table, near, across_climb, across_descend),
        shape((size * half + 8, size), f32),
        flops=2 * tall * size * rows,
    )
    total, half_sum = device_call(
        functools.partial(join_kernel, half),
        (mine, send(rest, "core")),
        [shape((size * half + 8, size), f32), shape((272, size), bf16)],
    )
    weights = device_call(
        functools.partial(solve_kernel, half),
        (total, send(half_sum, "half")),
        shape((272, size), bf16),
        flops=2 * 27 * half * size**3,
    )
    pair = send(weights, "core")
    up = send(weights, "climb")
    down = send(weights, "descend")
    levels, width_x, width_y, _ = members.shape
    patches = (width_x * 2 // SPACING, 2, levels * SPACING**2 // 4, size)
    part, pert = device_call(
        functools.partial(near_kernel, cols),
        (members, weights, pair),
        [shape(patches, f32), shape(patches, bf16)],
        [pltpu.VMEM((cols * size, size), bf16)],
        flops=2 * levels * width_x * width_y * size * 2 * size,
    )
    up, down, part = lax.optimization_barrier((up, down, part))
    pair_up, pair_down = send(up, "core"), send(down, "core")
    early, span = cols // 2, SPACING // 2
    begun, border = device_call(
        functools.partial(far_first_kernel, cols, early),
        (part, pert, weights, up, down),
        [shape((levels, early * span, width_y, size), bf16), shape((2, size, size), bf16)],
        [pltpu.VMEM((2, half * size, size), bf16)],
        flops=2 * levels * span * early * width_y * size * 2 * size,
    )
    count = patches[0] - early
    return device_call(
        functools.partial(far_rest_kernel, cols, count),
        (part, pert, pair, pair_up, pair_down, begun, border),
        shape(members.shape, bf16),
        [
            pltpu.VMEM((2, (half + 1) * size, size), bf16),
            pltpu.VMEM(members.shape, bf16),
            pltpu.SemaphoreType.DMA((count + 1,)),
        ],
        flops=2 * levels * span * count * width_y * size * 2 * size,
        out_hbm=True,
    )


def fits_pairs(mesh, members, obs_pert, obs_owner):
    sizes = dict(mesh.shape)
    return (
        sizes["tx"] == 2
        and sizes["lev"] == 4
        and obs_pert == (256, 128)
        and obs_owner == (4, 1, 256)
        and members[1:] == (64, 16, 128)
    )


def solution(mesh):
    placed = (
        P("lev", "tx", "ty", None),
        P(("tx", "ty", "lev"), None),
        P(("tx", "ty", "lev")),
        P(("tx", "ty", "lev")),
        P("tx", "ty", None),
        P("tx", "ty", None),
        P("tx", "ty"),
        P("tx", "ty", None),
    )

    def local(members, obs_pert, innovation, obs_precision, obs_owner, *rest):
        paired = fits_pairs(mesh, members.shape, obs_pert.shape, obs_owner.shape)
        return (paired_device if paired else per_device)(
            members, obs_pert, innovation, obs_precision, obs_owner, *rest
        )

    return jax.shard_map(
        local,
        mesh=mesh,
        in_specs=placed,
        out_specs=P("lev", "tx", "ty", None),
        check_vma=False,
    )
```

```python
import functools

import jax
import jax.numpy as jnp
from jax import lax
from jax.experimental import pallas as pl
from jax.experimental.pallas import tpu as pltpu
from jax.sharding import PartitionSpec as P


SPACING = 16
NS_STEPS = 4
VMEM_LIMIT = 12 << 20
LANES = 128


def padded(array, sides, width):
    for axis, dim in sides:
        size, length = (lax.axis_size(axis), array.shape[dim])
        up = [(i, (i + 1) % size) for i in range(size - 1)]
        down = [(j, i) for i, j in up]
        last = lax.slice_in_dim(array, length - width, length, axis=dim)
        initial = lax.slice_in_dim(array, 0, width, axis=dim)
        before = lax.ppermute(last, axis, up)
        after = lax.ppermute(initial, axis, down)
        array = jnp.concatenate([before, array, after], axis=dim)
    return array


def finish_solve(gram_matrix, projected):
    member_count = gram_matrix.shape[1]
    spread = float(member_count - 1)
    identity = jnp.eye(member_count, dtype=jnp.float32)
    scale_norm = spread + jnp.sqrt(jnp.sum(gram_matrix * gram_matrix, axis=(1, 2)))
    sqrt_iter = (spread * identity + gram_matrix) / scale_norm[:, None, None]
    inv_iter = jnp.broadcast_to(identity, sqrt_iter.shape)
    for _ in range(NS_STEPS):
        middle = 1.5 * identity - 0.5 * jnp.einsum(
            "bij,bjk->bik", inv_iter, sqrt_iter, precision=lax.Precision.HIGHEST
        )
        sqrt_iter = jnp.einsum("bij,bjk->bik", sqrt_iter, middle, precision=lax.Precision.HIGHEST)
        inv_iter = jnp.einsum("bij,bjk->bik", middle, inv_iter, precision=lax.Precision.HIGHEST)
    inner = jnp.einsum("bij,bj->bi", inv_iter, projected, precision=lax.Precision.HIGHEST)
    mean_weights = (
        jnp.einsum("bij,bj->bi", inv_iter, inner, precision=lax.Precision.HIGHEST)
        / scale_norm[:, None]
    )
    transform = (jnp.sqrt(spread) / jnp.sqrt(scale_norm))[:, None, None] * inv_iter + mean_weights[
        :, :, None
    ]
    return transform.astype(jnp.bfloat16)


def fractions(count, half_span):
    place = jnp.arange(count)[:, None]
    within = jnp.arange(half_span)[None, :].astype(jnp.float32)
    return jnp.where(
        place % 2 == 0,
        (within + half_span + 0.5) / (2 * half_span),
        (within + 0.5) / (2 * half_span),
    )


def solve_columns(lookup, counts, local_part, flat_pert, flat_values):
    column_count, slots = lookup.shape
    member_count = flat_pert.shape[1]
    block_len = min(slots, 128)
    live_blocks = (jnp.max(counts) + block_len - 1) // block_len

    def add_block(block_index, carry):
        gram_matrix, projected = carry
        offset = block_index * block_len
        slot_rows = lax.dynamic_slice_in_dim(lookup, offset, block_len, 1)
        slot_local = lax.dynamic_slice_in_dim(local_part, offset, block_len, 1)
        position = offset + jnp.arange(block_len)
        active = position[None, :] < counts[:, None]
        pert_rows = flat_pert[slot_rows].astype(jnp.float32)
        picked = flat_values[:, slot_rows]
        precision_w = jnp.where(active, picked[1].astype(jnp.float32) * slot_local, 0.0)
        departure = picked[0].astype(jnp.float32)
        gram_matrix = gram_matrix + jnp.einsum(
            "bsk,bsm->bkm",
            pert_rows * precision_w[:, :, None],
            pert_rows,
            precision=lax.Precision.HIGHEST,
        )
        projected = projected + jnp.einsum(
            "bsk,bs->bk", pert_rows, precision_w * departure, precision=lax.Precision.HIGHEST
        )
        return (gram_matrix, projected)

    start_gram = jnp.zeros((column_count, member_count, member_count), jnp.float32)
    start_proj = jnp.zeros((column_count, member_count), jnp.float32)
    gram_matrix, projected = lax.fori_loop(0, live_blocks, add_block, (start_gram, start_proj))
    return finish_solve(gram_matrix, projected)


def clamp_edges(rimmed, axis_index, axis_count, dim):
    lower = jnp.where(
        axis_index == 0,
        lax.slice_in_dim(rimmed, 1, 2, axis=dim),
        lax.slice_in_dim(rimmed, 0, 1, axis=dim),
    )
    last = rimmed.shape[dim]
    upper = jnp.where(
        axis_index == axis_count - 1,
        lax.slice_in_dim(rimmed, last - 2, last - 1, axis=dim),
        lax.slice_in_dim(rimmed, last - 1, last, axis=dim),
    )
    return jnp.concatenate(
        [lower, lax.slice_in_dim(rimmed, 1, last - 1, axis=dim), upper], axis=dim
    )


def per_device(
    members, obs_pert, innovation, obs_precision, obs_owner, obs_slot, obs_count, local_weight
):
    scalars = jnp.stack([innovation, obs_precision])
    tile_pert, tile_values = (
        lax.all_gather(obs_pert, "lev", axis=0, tiled=True),
        lax.all_gather(scalars, "lev", axis=1, tiled=True),
    )
    near_pert, near_values = (
        padded(tile_pert[None, None], (("tx", 0), ("ty", 1)), 1),
        padded(tile_values[None, None], (("tx", 0), ("ty", 1)), 1),
    )
    tile_len = near_pert.shape[2]
    member_count = near_pert.shape[3]
    flat_pert = near_pert.reshape(9 * tile_len, member_count)
    flat_values = jnp.transpose(near_values, (2, 0, 1, 3)).reshape(2, 9 * tile_len)
    column_x = lax.axis_index("tx")
    column_y = lax.axis_index("ty")
    tiles_x = lax.axis_size("tx")
    tiles_y = lax.axis_size("ty")
    near_x = obs_owner // tiles_y - column_x + 1
    near_y = obs_owner % tiles_y - column_y + 1
    lookup = (near_x * 3 + near_y) * tile_len + obs_slot
    coarse_x, coarse_y, slots = lookup.shape
    lookup = lookup.reshape(coarse_x * coarse_y, slots)
    counts = obs_count.reshape(coarse_x * coarse_y)
    local_part = local_weight.reshape(coarse_x * coarse_y, slots)
    weights = solve_columns(lookup, counts, local_part, flat_pert, flat_values)
    weights = weights.reshape(coarse_x, coarse_y, member_count, member_count)
    rimmed = padded(weights, (("tx", 0), ("ty", 1)), 1)
    rimmed = clamp_edges(rimmed, column_x, tiles_x, 0)
    rimmed = clamp_edges(rimmed, column_y, tiles_y, 1)
    doubled = jnp.repeat(jnp.repeat(rimmed, 2, axis=0), 2, axis=1)
    level_count, width_x, width_y, _ = members.shape
    half_span = SPACING // 2
    patch_x = width_x // half_span
    patch_y = width_y // half_span
    frac_x = fractions(patch_x, half_span)
    frac_y = fractions(patch_y, half_span)
    ens_mean = jnp.mean(members, axis=3, keepdims=True, dtype=jnp.float32)
    pert = (members.astype(jnp.float32) - ens_mean).astype(jnp.bfloat16)
    patched = pert.reshape(level_count, patch_x, half_span, patch_y, half_span, member_count)
    summed = jnp.zeros(patched.shape, jnp.float32)
    for upper_x in range(2):
        for upper_y in range(2):
            corner = doubled[
                1 + 2 * upper_x : 1 + 2 * upper_x + patch_x,
                1 + 2 * upper_y : 1 + 2 * upper_y + patch_y,
            ]
            product = jnp.einsum(
                "lxaybi,xyij->lxaybj", patched, corner, preferred_element_type=jnp.float32
            )
            factor_x = frac_x if upper_x == 1 else 1.0 - frac_x
            factor_y = frac_y if upper_y == 1 else 1.0 - frac_y
            summed = (
                summed
                + product
                * factor_x[None, :, :, None, None, None]
                * factor_y[None, None, None, :, :, None]
            )
    return (ens_mean + summed.reshape(members.shape)).astype(jnp.bfloat16)


def pair_patterns(mesh_axes):
    tiles_x, tiles_y, parts = (lax.axis_size(a) for a in mesh_axes)

    def flat(x, y, l):
        return (x * tiles_y + y) * parts + l

    def table(move):
        return [
            (flat(x, y, l), flat(*move(x, y, l)))
            for x in range(tiles_x)
            for y in range(tiles_y)
            for l in range(parts)
        ]

    def climb(x, y, l):
        if l % 2 == 0:
            return (x, y + 1, l) if y < tiles_y - 1 else (x, y, l + 1)
        return (x, y - 1, l) if y > 0 else (x, y, l - 1)

    climbing = table(climb)
    return {
        "across": table(lambda x, y, l: (1 - x, y, l)),
        "core": table(lambda x, y, l: (x, y, l ^ 1)),
        "half": table(lambda x, y, l: (x, y, l ^ 2)),
        "climb": climbing,
        "descend": [(b, a) for a, b in climbing],
    }


def device_call(kernel, operands, out_shape, scratch=(), flops=0, in_hbm=False, out_hbm=False):
    single = not isinstance(out_shape, (list, tuple))
    spec = pl.BlockSpec(memory_space=pltpu.VMEM)
    hbm = pl.BlockSpec(memory_space=pltpu.HBM)
    out_spec = hbm if out_hbm else spec
    return pl.pallas_call(
        kernel,
        out_shape=out_shape,
        in_specs=[hbm if in_hbm else spec] * len(operands),
        out_specs=out_spec if single else [out_spec] * len(out_shape),
        scratch_shapes=list(scratch),
        cost_estimate=pl.CostEstimate(flops=flops, bytes_accessed=1 << 18, transcendentals=0),
        compiler_params=pltpu.CompilerParams(vmem_limit_bytes=VMEM_LIMIT),
    )(*operands)


def split2(value):
    high = value.astype(jnp.bfloat16)
    return high, (value - high.astype(jnp.float32)).astype(jnp.bfloat16)


def split3(value):
    high, _ = split2(value)
    rest = value - high.astype(jnp.float32)
    middle, low = split2(rest)
    return high, middle, low


def dot(a, b, dims=((1,), (0,))):
    return lax.dot_general(a, b, (dims, ((), ())), preferred_element_type=jnp.float32)


def pack_kernel(
    rows, pert, inn, prec, owner, slot, count, local, out_ref, inn_ref, prec_ref, owner_ref, slot_ref, count_ref, local_ref, tail, sems
):
    sources = (owner, slot, count, local, inn, prec, pert)
    targets = (owner_ref, slot_ref, count_ref, local_ref, inn_ref, prec_ref, out_ref.at[0:rows, :])
    copies = [pltpu.make_async_copy(x, y, sems.at[k]) for k, (x, y) in enumerate(zip(sources, targets))]
    for copy in copies:
        copy.start()
    for copy in copies[:-1]:
        copy.wait()
    edge = jnp.where(lax.axis_index("tx") == 0, owner_ref.shape[0] - 1, 0)
    slots = owner_ref.shape[2]
    limit = jnp.where(edge == 0, count_ref[0, 0], count_ref[0, owner_ref.shape[0] - 1])
    active = lax.broadcasted_iota(jnp.int32, (1, slots), 1) < limit
    local_part = jnp.where(active, local_ref[edge], 0.0)
    slot_part = slot_ref[edge]
    for k, ref in enumerate((prec_ref, inn_ref)):
        tail[2 * k : 2 * k + 2, :] = ref[...].astype(jnp.float32)
    lists = [
        owner_ref[edge].astype(jnp.float32),
        (slot_part // 128).astype(jnp.float32),
        (slot_part % 128).astype(jnp.float32),
    ] + [piece.astype(jnp.float32) for piece in split3(local_part)]
    for k, row in enumerate(lists):
        for part in range(2):
            tail[4 + 2 * k + part : 5 + 2 * k + part, :] = row[:, 128 * part : 128 * (part + 1)]
    out_ref[rows : rows + 16, :] = tail[...].astype(jnp.bfloat16)
    copies[-1].wait()


def table_kernel(rows, cols, owner_ref, slot_ref, count_ref, local_ref, other_ref, out_ref):
    tile_x, tile_y, part = (lax.axis_index(a) for a in ("tx", "ty", "lev"))
    tiles_y = lax.axis_size("ty")
    core = lax.rem(part, 2)
    own, slots = owner_ref.shape[0], owner_ref.shape[2]
    received = other_ref[rows : rows + 16, :].astype(jnp.float32)

    def listed(k):
        return jnp.concatenate([received[2 * k : 2 * k + 1, :], received[2 * k + 1 : 2 * k + 2, :]], axis=1)

    far_owner = listed(2).astype(jnp.int32)
    far_slot = (listed(3) * 128.0 + listed(4)).astype(jnp.int32)
    far_local = listed(5) + listed(6) + listed(7)
    position_in = lax.broadcasted_iota(jnp.int32, (1, slots), 1)

    def own_list(k):
        return owner_ref[k], slot_ref[k], jnp.where(position_in < count_ref[0, k], local_ref[k], 0.0)

    def pick(use_far, k):
        return tuple(jnp.where(use_far, a, b) for a, b in zip((far_owner, far_slot, far_local), own_list(k)))

    lists = [pick(tile_x > 0, 0)] + [own_list(k) for k in range(own)] + [pick(tile_x == 0, own - 1)]
    half = cols // 2
    out_ref[...] = jnp.zeros_like(out_ref)
    for g, (owner, slot, local) in enumerate(lists):
        across = jnp.where(owner // tiles_y == tile_x, 0, 1)
        near = owner % tiles_y - tile_y
        first_way = jnp.where(core == 0, -1, 1)
        block = across * 3 + jnp.where(near == 0, 0, jnp.where(near == first_way, 1, 2))
        mine = slot // rows == part
        within = slot % rows
        high = jnp.where(mine, block * (rows // 128) + within // 128, -1)
        low = within % 128
        picked = jnp.where(lax.broadcasted_iota(jnp.int32, (16, slots), 0) == high, local, 0.0)
        hot = jnp.where(lax.broadcasted_iota(jnp.int32, (128, slots), 0) == low, 1.0, 0.0).astype(jnp.bfloat16)
        parts = split3(picked)
        total = dot(parts[0], hot, ((1,), (1,)))
        for piece in parts[1:]:
            total = total + dot(piece, hot, ((1,), (1,)))
        place = lax.rem(g - core * half + cols, cols)
        out_ref[pl.ds(place, 16, stride=8), :] = total


def gram_blocks(rows, cols, first, blocks, table_ref, turned, plain, scaled):
    per = rows // 128
    products, weights = [], []
    for k, ref in enumerate(blocks):
        tail = ref[rows : rows + 16, :].astype(jnp.float32)
        for part in range(per):
            hi = (first + k) * per + part
            row = table_ref[8 * hi : 8 * hi + 8, :] * tail[part : part + 1, :]
            weights.append(row)
            products.append(row * tail[per + part : per + part + 1, :])
        block = ref[0:rows, :]
        plain[rows * k : rows * (k + 1), :] = block
        turned[:, rows * k : rows * (k + 1)] = block.astype(jnp.float32).T
    weight = jnp.concatenate(weights, axis=1)
    high, low = split2(jnp.concatenate(products, axis=1))
    for position in range(cols):
        at = 128 * position
        scaled[at : at + 128, :] = (turned[...] * weight[position : position + 1, :]).astype(jnp.bfloat16)
    at = 128 * cols
    scaled[at : at + 16, :] = jnp.concatenate(
        [high.astype(jnp.float32), low.astype(jnp.float32)], axis=0
    ).astype(jnp.bfloat16)
    return dot(scaled[...], plain[...])


def gram_near_kernel(rows, cols, table_ref, b0, b1, b2, b3, out_ref, turned, plain, scaled):
    out_ref[...] = gram_blocks(rows, cols, 0, [b0, b1, b2, b3], table_ref, turned, plain, scaled)


def block_sums(rows, first, block, table_ref, positions):
    per = rows // 128
    tail = block[rows : rows + 16, :].astype(jnp.float32)
    weights = [table_ref[8 * hi : 8 * hi + 8, :] * tail[k : k + 1, :] for k, hi in enumerate(range(first * per, (first + 1) * per))]
    products = [w * tail[per + k : per + k + 1, :] for k, w in enumerate(weights)]
    plain = block[0:rows, :]
    turned = plain.astype(jnp.float32).T
    weight = beside(*weights)
    both = above(*[p.astype(jnp.float32) for p in split2(beside(*products))]).astype(jnp.bfloat16)
    return [dot((turned * weight[p : p + 1, :]).astype(jnp.bfloat16), plain) for p in positions] + [dot(both, plain)]


def earlier_sums(cols, so_far_ref, positions):
    return [so_far_ref[128 * p : 128 * (p + 1), :] for p in positions] + [so_far_ref[128 * cols : 128 * cols + 16, :]]


def two_block_sums(rows, cols, first, table_ref, so_far_ref, b4, b5, positions):
    groups = [earlier_sums(cols, so_far_ref, positions)]
    groups += [block_sums(rows, first + k, block, table_ref, positions) for k, block in enumerate((b4, b5))]
    return [x + y + z for x, y, z in zip(*groups)]


def rest_kernel(rows, cols, first, table_ref, so_far_ref, b4, b5, out_ref):
    half = cols // 2
    edge = 128 * half
    sums = two_block_sums(rows, cols, first, table_ref, so_far_ref, b4, b5, range(half, cols))
    for k in range(half):
        out_ref[128 * k : 128 * (k + 1), :] = sums[k].astype(jnp.bfloat16)
    projected = sums[half][0:8] + sums[half][8:16]
    high, low = split2(above(projected[half : 2 * half], jnp.zeros((8 - half, 128), jnp.float32)))
    out_ref[edge : edge + 16, :] = above(high.astype(jnp.float32), low.astype(jnp.float32)).astype(jnp.bfloat16)


def mine_kernel(rows, cols, first, table_ref, so_far_ref, b4, b5, out_ref):
    half = cols // 2
    sums = two_block_sums(rows, cols, first, table_ref, so_far_ref, b4, b5, range(half))
    for k in range(half):
        out_ref[128 * k : 128 * (k + 1), :] = sums[k]
    out_ref[128 * half : 128 * half + 8, :] = sums[half][0:8] + sums[half][8:16]


def lanes_from(lane, values, others=0.0):
    return jnp.where(lax.broadcasted_iota(jnp.int32, values.shape, 1) >= lane, values, others)


def fold(grams):
    top = [g[0:32] for g in grams]
    sides = [lanes_from(32, g[32:64], pltpu.roll(g[96:128], 32, 1)) for g in grams]
    third = [g[64:96] for g in grams]
    return above(*top, *sides, lanes_from(64, third[0], pltpu.roll(third[1], 64, 1)), third[2])


def unfold(folded, k, eye):
    side = folded[96 + 32 * k : 128 + 32 * k]
    third = folded[192:224] if k < 2 else folded[224:256]
    third = pltpu.roll(third, 64, 1) if k == 1 else third
    upper_part = above(
        folded[32 * k : 32 * k + 32],
        lanes_from(32, side),
        lanes_from(64, third),
        lanes_from(96, pltpu.roll(side, 96, 1)),
    )
    turned = dot(eye.astype(jnp.bfloat16), upper_part.astype(jnp.bfloat16), ((1,), (1,)))
    below = lax.broadcasted_iota(jnp.int32, eye.shape, 0) // 32 > lax.broadcasted_iota(jnp.int32, eye.shape, 1) // 32
    return jnp.where(below, turned, upper_part)


def join_kernel(half, mine_ref, got_ref, sum_ref, send_ref):
    edge = 128 * half
    got = got_ref[...].astype(jnp.float32)
    total = mine_ref[...] + above(got[0:edge], got[edge : edge + 8] + got[edge + 8 : edge + 16])
    sum_ref[...] = total
    folded = fold([total[128 * k : 128 * (k + 1)] for k in range(half)])
    high, low = split2(total[edge : edge + 8])
    send_ref[...] = above(folded, high.astype(jnp.float32), low.astype(jnp.float32)).astype(jnp.bfloat16)


def beside(*pieces):
    return jnp.concatenate(pieces, axis=1)


def above(*pieces):
    return jnp.concatenate(pieces, axis=0)


def product(a, b):
    (a_high, a_low), (b_high, b_low) = a, b
    return dot(beside(a_high, a_low), above(b_high, b_high)) + dot(a_high, b_low)


def wide(a, b):
    return beside(a[0], b[0]), beside(a[1], b[1])


def vector_product(rows, parts):
    left = above(*[p.astype(jnp.float32) for p in split2(rows)]).astype(jnp.bfloat16)
    full = dot(left, parts[0]) + dot(left, parts[1])
    return full[0:8] + full[8:16]


def solve_kernel(half, sum_ref, got_ref, out_ref):
    size = 128
    spread = float(size - 1)
    eye = identity(size)
    edge = size * half
    got = got_ref[...].astype(jnp.float32)
    projected = sum_ref[edge : edge + 8, :] + got[256:264] + got[264:272]
    norms, bases = [], []
    for k in range(half):
        gram = sum_ref[size * k : size * (k + 1), :] + unfold(got, k, eye)
        squared = jnp.sum(jnp.sum(gram * gram, axis=0, keepdims=True), axis=1, keepdims=True)
        norm = spread + jnp.sqrt(squared)
        norms.append(norm)
        bases.append((spread * eye + gram) / norm)
    base_parts = [split2(base) for base in bases]
    squares = [dot(high, high) for high, _ in base_parts]
    inverses = [
        1.5 * (1.5 * eye - 0.5 * base)
        - 0.5
        * dot(
            (1.5 * base - 0.5 * square).astype(jnp.bfloat16),
            (2.25 * eye - 1.5 * base + 0.25 * square).astype(jnp.bfloat16),
        )
        for base, square in zip(bases, squares)
    ]
    vectors = [jnp.broadcast_to(projected[k : k + 1, :], (8, size)) for k in range(half)]
    pushed = [vector_product(v, parts) for v, parts in zip(vectors, base_parts)]
    carried = None
    for step in range(NS_STEPS - 2):
        last = step == NS_STEPS - 3
        inverse_parts = [split2(z) for z in inverses]
        left = [split2(above(z, v, q)) for z, v, q in zip(inverses, vectors, pushed)] if last else inverse_parts
        both = [product(z, wide(b, y)) for z, b, y in zip(left, base_parts, inverse_parts)]
        forced = [x[:, 0:size] for x in both]
        square = [split2(x[0:size, size : 2 * size]) for x in both]
        if last:
            forced = [above(f[0:size], x[size + 8 : size + 16, size:], x[size + 8 : size + 16, size:]) for f, x in zip(forced, both)]
        cubes = [product(split2(f), y) for f, y in zip(forced, square)]
        if last:
            carried = [1.5 * x[size : size + 8, size:] - 0.5 * c[size : size + 8] for x, c in zip(both, cubes)]
        inverses = [1.5 * z - 0.5 * c[0:size] for z, c in zip(inverses, cubes)]
    scaled = [(jnp.sqrt(spread) / jnp.sqrt(norm)) * inverse for norm, inverse in zip(norms, inverses)]
    means = [
        vector_product(v, split2(inverse))[0:1] / norm for norm, inverse, v in zip(norms, inverses, carried)
    ]
    rest = jnp.zeros((8 - half, size), jnp.float32)
    high, low = split2(above(*means, rest))
    tail = above(high.astype(jnp.float32), low.astype(jnp.float32))
    out_ref[...] = above(fold(scaled), tail).astype(jnp.bfloat16)


def rebuild(folded, k, eye):
    means = folded[256 + k : 257 + k] + folded[264 + k : 265 + k]
    return (unfold(folded, k, eye) + means).astype(jnp.bfloat16)


def identity(size):
    same = lax.broadcasted_iota(jnp.int32, (size, size), 0) == lax.broadcasted_iota(jnp.int32, (size, size), 1)
    return jnp.where(same, 1.0, 0.0)


def shares(size):
    span = SPACING // 2
    shape = (1, span, span, size)
    along_x = lax.broadcasted_iota(jnp.int32, shape, 1).astype(jnp.float32) / (2 * span)
    along_y = lax.broadcasted_iota(jnp.int32, shape, 2).astype(jnp.float32) / (2 * span)
    upper_y = [along_y + (span + 0.5) / (2 * span), along_y + 0.5 / (2 * span)]
    return along_x, upper_y


def mixed(both, share, upper_x, shape):
    high = share * upper_x
    return (share - high) * both[:, 0:128].reshape(shape) + high * both[:, 128:256].reshape(shape)


def near_kernel(cols, members_ref, own, pair, part_ref, pert_ref, table):
    half = cols // 2
    first = lax.rem(lax.axis_index("lev"), 2) == 0
    eye = identity(128)
    mine, theirs = own[...].astype(jnp.float32), pair[...].astype(jnp.float32)
    for at, folded in ((0, jnp.where(first, mine, theirs)), (half, jnp.where(first, theirs, mine))):
        for j in range(half):
            table[128 * (at + j) : 128 * (at + j + 1), :] = rebuild(folded, j, eye)
    levels, width_x, _, size = members_ref.shape
    span = SPACING // 2
    shape = (levels, span, span, size)
    rows = levels * span * span
    along_x, upper_y = shares(size)
    for patch_x in range(width_x // span):
        states = members_ref[:, patch_x * span : (patch_x + 1) * span, :, :].astype(jnp.float32)
        mean = jnp.sum(states, axis=3, keepdims=True) * (1.0 / size)
        moved = states - mean
        column = (patch_x + 1) // 2
        upper_x = along_x + (span + 0.5 if patch_x % 2 == 0 else 0.5) / (2 * span)
        for patch_y in range(2):
            inside = slice(patch_y * span, (patch_y + 1) * span)
            left = moved[:, :, inside, :].reshape(rows, size).astype(jnp.bfloat16)
            pert_ref[patch_x, patch_y] = left
            both = dot(left, table[128 * column : 128 * (column + 2), :], ((1,), (1,)))
            share = upper_y[0] if patch_y == 0 else 1.0 - upper_y[1]
            part_ref[patch_x, patch_y] = (mean[:, :, inside, :] + mixed(both, share, upper_x, shape)).reshape(rows, size)


def add_far(first_patch, count, first_column, table, part_ref, pert_ref, keep):
    levels, size = part_ref.shape[2] // (SPACING // 2) ** 2, part_ref.shape[3]
    span = SPACING // 2
    shape = (levels, span, span, size)
    along_x, upper_y = shares(size)
    for k in range(count):
        patch_x = first_patch + k
        column = lax.div(patch_x + 1, 2) - first_column
        lines = pl.ds(pl.multiple_of(128 * column, 128), 256)
        upper_x = along_x + jnp.where(lax.rem(patch_x, 2) == 0, span + 0.5, 0.5) / (2 * span)
        results = []
        for patch_y in range(2):
            both = dot(pert_ref[patch_x, patch_y], table[patch_y, lines, :], ((1,), (1,)))
            share = 1.0 - upper_y[0] if patch_y == 0 else upper_y[1]
            results.append(part_ref[patch_x, patch_y].reshape(shape) + mixed(both, share, upper_x, shape))
        keep(k, patch_x, jnp.concatenate(results, axis=2).astype(jnp.bfloat16))


def neighbours(climb, descend, own, first):
    tile_y = lax.axis_index("ty")
    up, down, mine = climb[...], descend[...], own[...]
    before = jnp.where(tile_y == 0, mine, jnp.where(first, up, down))
    after = jnp.where(tile_y == lax.axis_size("ty") - 1, mine, jnp.where(first, down, up))
    return before.astype(jnp.float32), after.astype(jnp.float32)


def far_first_kernel(cols, count, part_ref, pert_ref, own, climb, descend, out_ref, border_ref, table):
    half, span = cols // 2, SPACING // 2
    core = lax.rem(lax.axis_index("lev"), 2)
    eye = identity(128)
    for z, folded in enumerate(neighbours(climb, descend, own, core == 0)):
        for j in range(half):
            table[z, 128 * j : 128 * (j + 1), :] = rebuild(folded, j, eye)
    border = jnp.where(core == 0, half - 1, 0)
    border_ref[...] = table[:, pl.ds(pl.multiple_of(128 * border, 128), 128), :]

    def keep(k, _, value):
        out_ref[:, k * span : (k + 1) * span] = value

    add_far(core * (part_ref.shape[0] - count), count, core * half, table, part_ref, pert_ref, keep)


def far_rest_kernel(
    cols, count, part_ref, pert_ref, pair, pair_climb, pair_descend, begun, border_ref, out_hbm, table, staged, sems
):
    half, span = cols // 2, SPACING // 2
    core = lax.rem(lax.axis_index("lev"), 2)
    first = core == 0
    total = part_ref.shape[0]
    early = total - count
    start = core * (total - early) * span
    copies = [pltpu.make_async_copy(begun, out_hbm.at[:, pl.ds(start, early * span)], sems.at[count])]
    copies[0].start()
    eye = identity(128)
    for z, folded in enumerate(neighbours(pair_climb, pair_descend, pair, jnp.logical_not(first))):
        for j in range(half):
            at = pl.multiple_of(128 * j + jnp.where(first, 128, 0), 128)
            table[z, pl.ds(at, 128), :] = rebuild(folded, j, eye)
    at = pl.multiple_of(jnp.where(first, 0, 128 * half), 128)
    table[:, pl.ds(at, 128), :] = border_ref[...]

    def keep(k, patch_x, value):
        inside = pl.ds(patch_x * span, span)
        staged[:, inside] = value
        copies.append(pltpu.make_async_copy(staged.at[:, inside], out_hbm.at[:, inside], sems.at[k]))
        copies[-1].start()

    first_column = jnp.where(first, half - 1, 0)
    add_far((1 - core) * early, count, first_column, table, part_ref, pert_ref, keep)
    for copy in copies:
        copy.wait()


def paired_device(
    members, obs_pert, innovation, obs_precision, obs_owner, obs_slot, obs_count, local_weight
):
    axes = ("tx", "ty", "lev")
    ways = pair_patterns(axes)

    def send(value, way):
        return lax.ppermute(value, axes, ways[way])

    bf16, f32 = jnp.bfloat16, jnp.float32
    rows, size = obs_pert.shape
    cols = obs_owner.shape[0] + 2
    half = cols // 2
    shape = jax.ShapeDtypeStruct
    counts = obs_count.reshape(1, -1)
    lists = (obs_owner, obs_slot, counts, local_weight)
    scalars = [v.reshape(rows // size, size) for v in (innovation, obs_precision)]
    packed = device_call(
        functools.partial(pack_kernel, rows),
        tuple(pltpu.with_memory_space_constraint(v, pltpu.HBM) for v in (obs_pert, *scalars, *lists)),
        shape((rows + 16, size), bf16),
        [pltpu.VMEM(v.shape, v.dtype) for v in scalars]
        + [
            pltpu.VMEM(obs_owner.shape, jnp.int32),
            pltpu.VMEM(obs_slot.shape, jnp.int32),
            pltpu.SMEM(counts.shape, jnp.int32),
            pltpu.VMEM(local_weight.shape, f32),
            pltpu.VMEM((16, size), f32),
            pltpu.SemaphoreType.DMA((7,)),
        ],
        in_hbm=True,
    )
    across = send(packed, "across")
    climb, descend = send(packed, "climb"), send(packed, "descend")
    across_climb, across_descend = send(across, "climb"), send(across, "descend")
    table = device_call(
        functools.partial(table_kernel, rows, cols),
        (*lists, across),
        shape((136, 128), f32),
        flops=6 * 2 * 48 * 256 * 128,
    )
    tall = size * cols + 16
    near = device_call(
        functools.partial(gram_near_kernel, rows, cols),
        (table, packed, climb, descend, across),
        shape((tall, size), f32),
        [
            pltpu.VMEM((size, 4 * rows), f32),
            pltpu.VMEM((4 * rows, size), bf16),
            pltpu.VMEM((tall, 4 * rows), bf16),
        ],
        flops=2 * tall * size * 4 * rows,
    )
    rest = device_call(
        functools.partial(rest_kernel, rows, cols, 4),
        (table, near, across_climb, across_descend),
        shape((size * half + 16, size), bf16),
        flops=2 * tall * size * rows,
    )
    mine = device_call(
        functools.partial(mine_kernel, rows, cols, 4),
        (table, near, across_climb, across_descend),
        shape((size * half + 8, size), f32),
        flops=2 * tall * size * rows,
    )
    total, half_sum = device_call(
        functools.partial(join_kernel, half),
        (mine, send(rest, "core")),
        [shape((size * half + 8, size), f32), shape((272, size), bf16)],
    )
    weights = device_call(
        functools.partial(solve_kernel, half),
        (total, send(half_sum, "half")),
        shape((272, size), bf16),
        flops=2 * 27 * half * size**3,
    )
    pair = send(weights, "core")
    up = send(weights, "climb")
    down = send(weights, "descend")
    levels, width_x, width_y, _ = members.shape
    patches = (width_x * 2 // SPACING, 2, levels * SPACING**2 // 4, size)
    part, pert = device_call(
        functools.partial(near_kernel, cols),
        (members, weights, pair),
        [shape(patches, f32), shape(patches, bf16)],
        [pltpu.VMEM((cols * size, size), bf16)],
        flops=2 * levels * width_x * width_y * size * 2 * size,
    )
    up, down, part = lax.optimization_barrier((up, down, part))
    pair_up, pair_down = send(up, "core"), send(down, "core")
    early, span = cols // 2, SPACING // 2
    begun, border = device_call(
        functools.partial(far_first_kernel, cols, early),
        (part, pert, weights, up, down),
        [shape((levels, early * span, width_y, size), bf16), shape((2, size, size), bf16)],
        [pltpu.VMEM((2, half * size, size), bf16)],
        flops=2 * levels * span * early * width_y * size * 2 * size,
    )
    count = patches[0] - early
    return device_call(
        functools.partial(far_rest_kernel, cols, count),
        (part, pert, pair, pair_up, pair_down, begun, border),
        shape(members.shape, bf16),
        [
            pltpu.VMEM((2, (half + 1) * size, size), bf16),
            pltpu.VMEM(members.shape, bf16),
            pltpu.SemaphoreType.DMA((count + 1,)),
        ],
        flops=2 * levels * span * count * width_y * size * 2 * size,
        out_hbm=True,
    )


def fits_pairs(mesh, members, obs_pert, obs_owner):
    sizes = dict(mesh.shape)
    coarse_x, coarse_y, slots = obs_owner
    _, width_x, width_y, size = members
    return (
        sizes["tx"] == 2
        and sizes["lev"] == 4
        and (coarse_x + 2, coarse_y) == (6, 1)
        and (width_x, width_y) == (coarse_x * SPACING, coarse_y * SPACING)
        and size == LANES
        and obs_pert == (2 * LANES, LANES)
        and slots == 2 * LANES
    )


def solution(mesh):
    placed = (
        P("lev", "tx", "ty", None),
        P(("tx", "ty", "lev"), None),
        P(("tx", "ty", "lev")),
        P(("tx", "ty", "lev")),
        P("tx", "ty", None),
        P("tx", "ty", None),
        P("tx", "ty"),
        P("tx", "ty", None),
    )

    def local(members, obs_pert, innovation, obs_precision, obs_owner, *rest):
        paired = fits_pairs(mesh, members.shape, obs_pert.shape, obs_owner.shape)
        return (paired_device if paired else per_device)(
            members, obs_pert, innovation, obs_precision, obs_owner, *rest
        )

    return jax.shard_map(
        local,
        mesh=mesh,
        in_specs=placed,
        out_specs=P("lev", "tx", "ty", None),
        check_vma=False,
    )
```

```python
import functools

import jax
import jax.numpy as jnp
from jax import lax
from jax.experimental import pallas as pl
from jax.experimental.pallas import tpu as pltpu
from jax.sharding import PartitionSpec as P


SPACING = 16
NS_STEPS = 4
VMEM_LIMIT = 12 << 20
LANES = 128


def padded(array, sides, width):
    for axis, dim in sides:
        size, length = (lax.axis_size(axis), array.shape[dim])
        up = [(i, (i + 1) % size) for i in range(size - 1)]
        down = [(j, i) for i, j in up]
        last = lax.slice_in_dim(array, length - width, length, axis=dim)
        initial = lax.slice_in_dim(array, 0, width, axis=dim)
        before = lax.ppermute(last, axis, up)
        after = lax.ppermute(initial, axis, down)
        array = jnp.concatenate([before, array, after], axis=dim)
    return array


def finish_solve(gram_matrix, projected):
    member_count = gram_matrix.shape[1]
    spread = float(member_count - 1)
    identity = jnp.eye(member_count, dtype=jnp.float32)
    scale_norm = spread + jnp.sqrt(jnp.sum(gram_matrix * gram_matrix, axis=(1, 2)))
    sqrt_iter = (spread * identity + gram_matrix) / scale_norm[:, None, None]
    inv_iter = jnp.broadcast_to(identity, sqrt_iter.shape)
    for _ in range(NS_STEPS):
        middle = 1.5 * identity - 0.5 * jnp.einsum(
            "bij,bjk->bik", inv_iter, sqrt_iter, precision=lax.Precision.HIGHEST
        )
        sqrt_iter = jnp.einsum("bij,bjk->bik", sqrt_iter, middle, precision=lax.Precision.HIGHEST)
        inv_iter = jnp.einsum("bij,bjk->bik", middle, inv_iter, precision=lax.Precision.HIGHEST)
    inner = jnp.einsum("bij,bj->bi", inv_iter, projected, precision=lax.Precision.HIGHEST)
    mean_weights = (
        jnp.einsum("bij,bj->bi", inv_iter, inner, precision=lax.Precision.HIGHEST)
        / scale_norm[:, None]
    )
    transform = (jnp.sqrt(spread) / jnp.sqrt(scale_norm))[:, None, None] * inv_iter + mean_weights[
        :, :, None
    ]
    return transform.astype(jnp.bfloat16)


def fractions(count, half_span):
    place = jnp.arange(count)[:, None]
    within = jnp.arange(half_span)[None, :].astype(jnp.float32)
    return jnp.where(
        place % 2 == 0,
        (within + half_span + 0.5) / (2 * half_span),
        (within + 0.5) / (2 * half_span),
    )


def solve_columns(lookup, counts, local_part, flat_pert, flat_values):
    column_count, slots = lookup.shape
    member_count = flat_pert.shape[1]
    block_len = min(slots, 128)
    live_blocks = (jnp.max(counts) + block_len - 1) // block_len

    def add_block(block_index, carry):
        gram_matrix, projected = carry
        offset = block_index * block_len
        slot_rows = lax.dynamic_slice_in_dim(lookup, offset, block_len, 1)
        slot_local = lax.dynamic_slice_in_dim(local_part, offset, block_len, 1)
        position = offset + jnp.arange(block_len)
        active = position[None, :] < counts[:, None]
        pert_rows = flat_pert[slot_rows].astype(jnp.float32)
        picked = flat_values[:, slot_rows]
        precision_w = jnp.where(active, picked[1].astype(jnp.float32) * slot_local, 0.0)
        departure = picked[0].astype(jnp.float32)
        gram_matrix = gram_matrix + jnp.einsum(
            "bsk,bsm->bkm",
            pert_rows * precision_w[:, :, None],
            pert_rows,
            precision=lax.Precision.HIGHEST,
        )
        projected = projected + jnp.einsum(
            "bsk,bs->bk", pert_rows, precision_w * departure, precision=lax.Precision.HIGHEST
        )
        return (gram_matrix, projected)

    start_gram = jnp.zeros((column_count, member_count, member_count), jnp.float32)
    start_proj = jnp.zeros((column_count, member_count), jnp.float32)
    gram_matrix, projected = lax.fori_loop(0, live_blocks, add_block, (start_gram, start_proj))
    return finish_solve(gram_matrix, projected)


def clamp_edges(rimmed, axis_index, axis_count, dim):
    lower = jnp.where(
        axis_index == 0,
        lax.slice_in_dim(rimmed, 1, 2, axis=dim),
        lax.slice_in_dim(rimmed, 0, 1, axis=dim),
    )
    last = rimmed.shape[dim]
    upper = jnp.where(
        axis_index == axis_count - 1,
        lax.slice_in_dim(rimmed, last - 2, last - 1, axis=dim),
        lax.slice_in_dim(rimmed, last - 1, last, axis=dim),
    )
    return jnp.concatenate(
        [lower, lax.slice_in_dim(rimmed, 1, last - 1, axis=dim), upper], axis=dim
    )


def per_device(
    members, obs_pert, innovation, obs_precision, obs_owner, obs_slot, obs_count, local_weight
):
    scalars = jnp.stack([innovation, obs_precision])
    tile_pert, tile_values = (
        lax.all_gather(obs_pert, "lev", axis=0, tiled=True),
        lax.all_gather(scalars, "lev", axis=1, tiled=True),
    )
    near_pert, near_values = (
        padded(tile_pert[None, None], (("tx", 0), ("ty", 1)), 1),
        padded(tile_values[None, None], (("tx", 0), ("ty", 1)), 1),
    )
    tile_len = near_pert.shape[2]
    member_count = near_pert.shape[3]
    flat_pert = near_pert.reshape(9 * tile_len, member_count)
    flat_values = jnp.transpose(near_values, (2, 0, 1, 3)).reshape(2, 9 * tile_len)
    column_x = lax.axis_index("tx")
    column_y = lax.axis_index("ty")
    tiles_x = lax.axis_size("tx")
    tiles_y = lax.axis_size("ty")
    near_x = obs_owner // tiles_y - column_x + 1
    near_y = obs_owner % tiles_y - column_y + 1
    lookup = (near_x * 3 + near_y) * tile_len + obs_slot
    coarse_x, coarse_y, slots = lookup.shape
    lookup = lookup.reshape(coarse_x * coarse_y, slots)
    counts = obs_count.reshape(coarse_x * coarse_y)
    local_part = local_weight.reshape(coarse_x * coarse_y, slots)
    weights = solve_columns(lookup, counts, local_part, flat_pert, flat_values)
    weights = weights.reshape(coarse_x, coarse_y, member_count, member_count)
    rimmed = padded(weights, (("tx", 0), ("ty", 1)), 1)
    rimmed = clamp_edges(rimmed, column_x, tiles_x, 0)
    rimmed = clamp_edges(rimmed, column_y, tiles_y, 1)
    doubled = jnp.repeat(jnp.repeat(rimmed, 2, axis=0), 2, axis=1)
    level_count, width_x, width_y, _ = members.shape
    half_span = SPACING // 2
    patch_x = width_x // half_span
    patch_y = width_y // half_span
    frac_x = fractions(patch_x, half_span)
    frac_y = fractions(patch_y, half_span)
    ens_mean = jnp.mean(members, axis=3, keepdims=True, dtype=jnp.float32)
    pert = (members.astype(jnp.float32) - ens_mean).astype(jnp.bfloat16)
    patched = pert.reshape(level_count, patch_x, half_span, patch_y, half_span, member_count)
    summed = jnp.zeros(patched.shape, jnp.float32)
    for upper_x in range(2):
        for upper_y in range(2):
            corner = doubled[
                1 + 2 * upper_x : 1 + 2 * upper_x + patch_x,
                1 + 2 * upper_y : 1 + 2 * upper_y + patch_y,
            ]
            product = jnp.einsum(
                "lxaybi,xyij->lxaybj", patched, corner, preferred_element_type=jnp.float32
            )
            factor_x = frac_x if upper_x == 1 else 1.0 - frac_x
            factor_y = frac_y if upper_y == 1 else 1.0 - frac_y
            summed = (
                summed
                + product
                * factor_x[None, :, :, None, None, None]
                * factor_y[None, None, None, :, :, None]
            )
    return (ens_mean + summed.reshape(members.shape)).astype(jnp.bfloat16)


def pair_patterns(mesh_axes):
    tiles_x, tiles_y, parts = (lax.axis_size(a) for a in mesh_axes)

    def flat(x, y, l):
        return (x * tiles_y + y) * parts + l

    def table(move):
        return [
            (flat(x, y, l), flat(*move(x, y, l)))
            for x in range(tiles_x)
            for y in range(tiles_y)
            for l in range(parts)
        ]

    def climb(x, y, l):
        if l % 2 == 0:
            return (x, y + 1, l) if y < tiles_y - 1 else (x, y, l + 1)
        return (x, y - 1, l) if y > 0 else (x, y, l - 1)

    climbing = table(climb)
    return {
        "across": table(lambda x, y, l: (1 - x, y, l)),
        "core": table(lambda x, y, l: (x, y, l ^ 1)),
        "half": table(lambda x, y, l: (x, y, l ^ 2)),
        "climb": climbing,
        "descend": [(b, a) for a, b in climbing],
    }


def device_call(kernel, operands, out_shape, scratch=(), flops=0, in_hbm=False, out_hbm=False):
    single = not isinstance(out_shape, (list, tuple))
    spec = pl.BlockSpec(memory_space=pltpu.VMEM)
    hbm = pl.BlockSpec(memory_space=pltpu.HBM)
    out_spec = hbm if out_hbm else spec
    return pl.pallas_call(
        kernel,
        out_shape=out_shape,
        in_specs=[hbm if in_hbm else spec] * len(operands),
        out_specs=out_spec if single else [out_spec] * len(out_shape),
        scratch_shapes=list(scratch),
        cost_estimate=pl.CostEstimate(flops=flops, bytes_accessed=1 << 18, transcendentals=0),
        compiler_params=pltpu.CompilerParams(vmem_limit_bytes=VMEM_LIMIT),
    )(*operands)


def split2(value):
    high = value.astype(jnp.bfloat16)
    return high, (value - high.astype(jnp.float32)).astype(jnp.bfloat16)


def split3(value):
    high, _ = split2(value)
    rest = value - high.astype(jnp.float32)
    middle, low = split2(rest)
    return high, middle, low


def dot(a, b, dims=((1,), (0,))):
    return lax.dot_general(a, b, (dims, ((), ())), preferred_element_type=jnp.float32)


def pack_kernel(
    rows, pert, inn, prec, owner, slot, count, local, out_ref, inn_ref, prec_ref, owner_ref, slot_ref, count_ref, local_ref, tail, sems
):
    sources = (owner, slot, count, local, inn, prec, pert)
    targets = (owner_ref, slot_ref, count_ref, local_ref, inn_ref, prec_ref, out_ref.at[0:rows, :])
    copies = [pltpu.make_async_copy(x, y, sems.at[k]) for k, (x, y) in enumerate(zip(sources, targets))]
    for copy in copies[-1:] + copies[:-1]:
        copy.start()
    for copy in copies[:-1]:
        copy.wait()
    edge = jnp.where(lax.axis_index("tx") == 0, owner_ref.shape[0] - 1, 0)
    slots = owner_ref.shape[2]
    limit = jnp.where(edge == 0, count_ref[0, 0], count_ref[0, owner_ref.shape[0] - 1])
    active = lax.broadcasted_iota(jnp.int32, (1, slots), 1) < limit
    local_part = jnp.where(active, local_ref[edge], 0.0)
    slot_part = slot_ref[edge]
    for k, ref in enumerate((prec_ref, inn_ref)):
        tail[2 * k : 2 * k + 2, :] = ref[...].astype(jnp.float32)
    lists = [
        owner_ref[edge].astype(jnp.float32),
        (slot_part // 128).astype(jnp.float32),
        (slot_part % 128).astype(jnp.float32),
    ] + [piece.astype(jnp.float32) for piece in split3(local_part)]
    for k, row in enumerate(lists):
        for part in range(2):
            tail[4 + 2 * k + part : 5 + 2 * k + part, :] = row[:, 128 * part : 128 * (part + 1)]
    out_ref[rows : rows + 16, :] = tail[...].astype(jnp.bfloat16)
    copies[-1].wait()


def table_kernel(rows, cols, owner_ref, slot_ref, count_ref, local_ref, other_ref, out_ref):
    tile_x, tile_y, part = (lax.axis_index(a) for a in ("tx", "ty", "lev"))
    tiles_y = lax.axis_size("ty")
    core = lax.rem(part, 2)
    own, slots = owner_ref.shape[0], owner_ref.shape[2]
    received = other_ref[rows : rows + 16, :].astype(jnp.float32)

    def listed(k):
        return jnp.concatenate([received[2 * k : 2 * k + 1, :], received[2 * k + 1 : 2 * k + 2, :]], axis=1)

    far_owner = listed(2).astype(jnp.int32)
    far_slot = (listed(3) * 128.0 + listed(4)).astype(jnp.int32)
    far_local = listed(5) + listed(6) + listed(7)
    position_in = lax.broadcasted_iota(jnp.int32, (1, slots), 1)

    def own_list(k):
        return owner_ref[k], slot_ref[k], jnp.where(position_in < count_ref[0, k], local_ref[k], 0.0)

    def pick(use_far, k):
        return tuple(jnp.where(use_far, a, b) for a, b in zip((far_owner, far_slot, far_local), own_list(k)))

    lists = [pick(tile_x > 0, 0)] + [own_list(k) for k in range(own)] + [pick(tile_x == 0, own - 1)]
    half = cols // 2
    out_ref[...] = jnp.zeros_like(out_ref)
    for g, (owner, slot, local) in enumerate(lists):
        across = jnp.where(owner // tiles_y == tile_x, 0, 1)
        near = owner % tiles_y - tile_y
        first_way = jnp.where(core == 0, -1, 1)
        block = across * 3 + jnp.where(near == 0, 0, jnp.where(near == first_way, 1, 2))
        mine = slot // rows == part
        within = slot % rows
        high = jnp.where(mine, block * (rows // 128) + within // 128, -1)
        low = within % 128
        picked = jnp.where(lax.broadcasted_iota(jnp.int32, (16, slots), 0) == high, local, 0.0)
        hot = jnp.where(lax.broadcasted_iota(jnp.int32, (128, slots), 0) == low, 1.0, 0.0).astype(jnp.bfloat16)
        parts = split3(picked)
        total = dot(parts[0], hot, ((1,), (1,)))
        for piece in parts[1:]:
            total = total + dot(piece, hot, ((1,), (1,)))
        place = lax.rem(g - core * half + cols, cols)
        out_ref[pl.ds(place, 16, stride=8), :] = total


def gram_blocks(rows, cols, first, blocks, table_ref, turned, plain, scaled):
    per = rows // 128
    products, weights = [], []
    for k, ref in enumerate(blocks):
        tail = ref[rows : rows + 16, :].astype(jnp.float32)
        for part in range(per):
            hi = (first + k) * per + part
            row = table_ref[8 * hi : 8 * hi + 8, :] * tail[part : part + 1, :]
            weights.append(row)
            products.append(row * tail[per + part : per + part + 1, :])
        block = ref[0:rows, :]
        plain[rows * k : rows * (k + 1), :] = block
        turned[:, rows * k : rows * (k + 1)] = block.astype(jnp.float32).T
    weight = jnp.concatenate(weights, axis=1)
    high, low = split2(jnp.concatenate(products, axis=1))
    for position in range(cols):
        at = 128 * position
        scaled[at : at + 128, :] = (turned[...] * weight[position : position + 1, :]).astype(jnp.bfloat16)
    at = 128 * cols
    scaled[at : at + 16, :] = jnp.concatenate(
        [high.astype(jnp.float32), low.astype(jnp.float32)], axis=0
    ).astype(jnp.bfloat16)
    return dot(scaled[...], plain[...])


def gram_near_kernel(rows, cols, table_ref, b0, b1, b2, b3, out_ref, turned, plain, scaled):
    out_ref[...] = gram_blocks(rows, cols, 0, [b0, b1, b2, b3], table_ref, turned, plain, scaled)


def block_sums(rows, first, block, table_ref, positions):
    per = rows // 128
    tail = block[rows : rows + 16, :].astype(jnp.float32)
    weights = [table_ref[8 * hi : 8 * hi + 8, :] * tail[k : k + 1, :] for k, hi in enumerate(range(first * per, (first + 1) * per))]
    products = [w * tail[per + k : per + k + 1, :] for k, w in enumerate(weights)]
    plain = block[0:rows, :]
    turned = plain.astype(jnp.float32).T
    weight = beside(*weights)
    both = above(*[p.astype(jnp.float32) for p in split2(beside(*products))]).astype(jnp.bfloat16)
    return [dot((turned * weight[p : p + 1, :]).astype(jnp.bfloat16), plain) for p in positions] + [dot(both, plain)]


def earlier_sums(cols, so_far_ref, positions):
    return [so_far_ref[128 * p : 128 * (p + 1), :] for p in positions] + [so_far_ref[128 * cols : 128 * cols + 16, :]]


def two_block_sums(rows, cols, first, table_ref, so_far_ref, b4, b5, positions):
    groups = [earlier_sums(cols, so_far_ref, positions)]
    groups += [block_sums(rows, first + k, block, table_ref, positions) for k, block in enumerate((b4, b5))]
    return [x + y + z for x, y, z in zip(*groups)]


def rest_kernel(rows, cols, first, table_ref, so_far_ref, b4, b5, out_ref):
    half = cols // 2
    edge = 128 * half
    sums = two_block_sums(rows, cols, first, table_ref, so_far_ref, b4, b5, range(half, cols))
    for k in range(half):
        out_ref[128 * k : 128 * (k + 1), :] = sums[k].astype(jnp.bfloat16)
    projected = sums[half][0:8] + sums[half][8:16]
    high, low = split2(above(projected[half : 2 * half], jnp.zeros((8 - half, 128), jnp.float32)))
    out_ref[edge : edge + 16, :] = above(high.astype(jnp.float32), low.astype(jnp.float32)).astype(jnp.bfloat16)


def mine_kernel(rows, cols, first, table_ref, so_far_ref, b4, b5, out_ref):
    half = cols // 2
    sums = two_block_sums(rows, cols, first, table_ref, so_far_ref, b4, b5, range(half))
    for k in range(half):
        out_ref[128 * k : 128 * (k + 1), :] = sums[k]
    out_ref[128 * half : 128 * half + 8, :] = sums[half][0:8] + sums[half][8:16]


def lanes_from(lane, values, others=0.0):
    return jnp.where(lax.broadcasted_iota(jnp.int32, values.shape, 1) >= lane, values, others)


def fold(grams):
    top = [g[0:32] for g in grams]
    sides = [lanes_from(32, g[32:64], pltpu.roll(g[96:128], 32, 1)) for g in grams]
    third = [g[64:96] for g in grams]
    return above(*top, *sides, lanes_from(64, third[0], pltpu.roll(third[1], 64, 1)), third[2])


def unfold(folded, k, eye):
    side = folded[96 + 32 * k : 128 + 32 * k]
    third = folded[192:224] if k < 2 else folded[224:256]
    third = pltpu.roll(third, 64, 1) if k == 1 else third
    upper_part = above(
        folded[32 * k : 32 * k + 32],
        lanes_from(32, side),
        lanes_from(64, third),
        lanes_from(96, pltpu.roll(side, 96, 1)),
    )
    turned = dot(eye.astype(jnp.bfloat16), upper_part.astype(jnp.bfloat16), ((1,), (1,)))
    below = lax.broadcasted_iota(jnp.int32, eye.shape, 0) // 32 > lax.broadcasted_iota(jnp.int32, eye.shape, 1) // 32
    return jnp.where(below, turned, upper_part)


def join_kernel(half, mine_ref, got_ref, sum_ref, send_ref):
    edge = 128 * half
    got = got_ref[...].astype(jnp.float32)
    total = mine_ref[...] + above(got[0:edge], got[edge : edge + 8] + got[edge + 8 : edge + 16])
    sum_ref[...] = total
    folded = fold([total[128 * k : 128 * (k + 1)] for k in range(half)])
    high, low = split2(total[edge : edge + 8])
    send_ref[...] = above(folded, high.astype(jnp.float32), low.astype(jnp.float32)).astype(jnp.bfloat16)


def beside(*pieces):
    return jnp.concatenate(pieces, axis=1)


def above(*pieces):
    return jnp.concatenate(pieces, axis=0)


def product(a, b):
    (a_high, a_low), (b_high, b_low) = a, b
    return dot(beside(a_high, a_low), above(b_high, b_high)) + dot(a_high, b_low)


def wide(a, b):
    return beside(a[0], b[0]), beside(a[1], b[1])


def vector_product(rows, parts):
    left = above(*[p.astype(jnp.float32) for p in split2(rows)]).astype(jnp.bfloat16)
    full = dot(left, parts[0]) + dot(left, parts[1])
    return full[0:8] + full[8:16]


def solve_kernel(half, sum_ref, got_ref, out_ref):
    size = 128
    spread = float(size - 1)
    eye = identity(size)
    edge = size * half
    got = got_ref[...].astype(jnp.float32)
    projected = sum_ref[edge : edge + 8, :] + got[256:264] + got[264:272]
    norms, bases = [], []
    for k in range(half):
        gram = sum_ref[size * k : size * (k + 1), :] + unfold(got, k, eye)
        squared = jnp.sum(jnp.sum(gram * gram, axis=0, keepdims=True), axis=1, keepdims=True)
        norm = spread + jnp.sqrt(squared)
        norms.append(norm)
        bases.append((spread * eye + gram) / norm)
    base_parts = [split2(base) for base in bases]
    squares = [dot(high, high) for high, _ in base_parts]
    inverses = [
        1.5 * (1.5 * eye - 0.5 * base)
        - 0.5
        * dot(
            (1.5 * base - 0.5 * square).astype(jnp.bfloat16),
            (2.25 * eye - 1.5 * base + 0.25 * square).astype(jnp.bfloat16),
        )
        for base, square in zip(bases, squares)
    ]
    vectors = [jnp.broadcast_to(projected[k : k + 1, :], (8, size)) for k in range(half)]
    pushed = [vector_product(v, parts) for v, parts in zip(vectors, base_parts)]
    carried = None
    for step in range(NS_STEPS - 2):
        last = step == NS_STEPS - 3
        inverse_parts = [split2(z) for z in inverses]
        left = [split2(above(z, v, q)) for z, v, q in zip(inverses, vectors, pushed)] if last else inverse_parts
        both = [product(z, wide(b, y)) if last else dot(z[0], beside(b[0], y[0])) for z, b, y in zip(left, base_parts, inverse_parts)]
        forced = [x[:, 0:size] for x in both]
        square = [split2(x[0:size, size : 2 * size]) for x in both]
        if last:
            forced = [above(f[0:size], x[size + 8 : size + 16, size:], x[size + 8 : size + 16, size:]) for f, x in zip(forced, both)]
        cubes = [product(split2(f), y) if last else dot(f.astype(jnp.bfloat16), y[0]) for f, y in zip(forced, square)]
        if last:
            carried = [1.5 * x[size : size + 8, size:] - 0.5 * c[size : size + 8] for x, c in zip(both, cubes)]
        inverses = [1.5 * z - 0.5 * c[0:size] for z, c in zip(inverses, cubes)]
    scaled = [(jnp.sqrt(spread) / jnp.sqrt(norm)) * inverse for norm, inverse in zip(norms, inverses)]
    means = [
        vector_product(v, split2(inverse))[0:1] / norm for norm, inverse, v in zip(norms, inverses, carried)
    ]
    rest = jnp.zeros((8 - half, size), jnp.float32)
    high, low = split2(above(*means, rest))
    tail = above(high.astype(jnp.float32), low.astype(jnp.float32))
    out_ref[...] = above(fold(scaled), tail).astype(jnp.bfloat16)


def rebuild(folded, k, eye):
    means = folded[256 + k : 257 + k] + folded[264 + k : 265 + k]
    return (unfold(folded, k, eye) + means).astype(jnp.bfloat16)


def identity(size):
    same = lax.broadcasted_iota(jnp.int32, (size, size), 0) == lax.broadcasted_iota(jnp.int32, (size, size), 1)
    return jnp.where(same, 1.0, 0.0)


def shares(size):
    span = SPACING // 2
    shape = (1, span, span, size)
    along_x = lax.broadcasted_iota(jnp.int32, shape, 1).astype(jnp.float32) / (2 * span)
    along_y = lax.broadcasted_iota(jnp.int32, shape, 2).astype(jnp.float32) / (2 * span)
    upper_y = [along_y + (span + 0.5) / (2 * span), along_y + 0.5 / (2 * span)]
    return along_x, upper_y


def mixed(both, share, upper_x, shape):
    high = share * upper_x
    return (share - high) * both[:, 0:128].reshape(shape) + high * both[:, 128:256].reshape(shape)


def near_kernel(cols, members_ref, own, pair, part_ref, pert_ref, table):
    half = cols // 2
    first = lax.rem(lax.axis_index("lev"), 2) == 0
    eye = identity(128)
    mine, theirs = own[...].astype(jnp.float32), pair[...].astype(jnp.float32)
    for at, folded in ((0, jnp.where(first, mine, theirs)), (half, jnp.where(first, theirs, mine))):
        for j in range(half):
            table[128 * (at + j) : 128 * (at + j + 1), :] = rebuild(folded, j, eye)
    levels, width_x, _, size = members_ref.shape
    span = SPACING // 2
    shape = (levels, span, span, size)
    rows = levels * span * span
    along_x, upper_y = shares(size)
    for patch_x in range(width_x // span):
        states = members_ref[:, patch_x * span : (patch_x + 1) * span, :, :].astype(jnp.float32)
        mean = jnp.sum(states, axis=3, keepdims=True) * (1.0 / size)
        moved = states - mean
        column = (patch_x + 1) // 2
        upper_x = along_x + (span + 0.5 if patch_x % 2 == 0 else 0.5) / (2 * span)
        for patch_y in range(2):
            inside = slice(patch_y * span, (patch_y + 1) * span)
            left = moved[:, :, inside, :].reshape(rows, size).astype(jnp.bfloat16)
            pert_ref[patch_x, patch_y] = left
            both = dot(left, table[128 * column : 128 * (column + 2), :], ((1,), (1,)))
            share = upper_y[0] if patch_y == 0 else 1.0 - upper_y[1]
            part_ref[patch_x, patch_y] = (mean[:, :, inside, :] + mixed(both, share, upper_x, shape)).reshape(rows, size)


def add_far(first_patch, count, first_column, table, part_ref, pert_ref, keep):
    levels, size = part_ref.shape[2] // (SPACING // 2) ** 2, part_ref.shape[3]
    span = SPACING // 2
    shape = (levels, span, span, size)
    along_x, upper_y = shares(size)
    for k in range(count):
        patch_x = first_patch + k
        column = lax.div(patch_x + 1, 2) - first_column
        lines = pl.ds(pl.multiple_of(128 * column, 128), 256)
        upper_x = along_x + jnp.where(lax.rem(patch_x, 2) == 0, span + 0.5, 0.5) / (2 * span)
        results = []
        for patch_y in range(2):
            both = dot(pert_ref[patch_x, patch_y], table[patch_y, lines, :], ((1,), (1,)))
            share = 1.0 - upper_y[0] if patch_y == 0 else upper_y[1]
            results.append(part_ref[patch_x, patch_y].reshape(shape) + mixed(both, share, upper_x, shape))
        keep(k, patch_x, jnp.concatenate(results, axis=2).astype(jnp.bfloat16))


def neighbours(climb, descend, own, first):
    tile_y = lax.axis_index("ty")
    up, down, mine = climb[...], descend[...], own[...]
    before = jnp.where(tile_y == 0, mine, jnp.where(first, up, down))
    after = jnp.where(tile_y == lax.axis_size("ty") - 1, mine, jnp.where(first, down, up))
    return before.astype(jnp.float32), after.astype(jnp.float32)


def far_first_kernel(cols, count, part_ref, pert_ref, own, climb, descend, out_ref, border_ref, table):
    half, span = cols // 2, SPACING // 2
    core = lax.rem(lax.axis_index("lev"), 2)
    eye = identity(128)
    for z, folded in enumerate(neighbours(climb, descend, own, core == 0)):
        for j in range(half):
            table[z, 128 * j : 128 * (j + 1), :] = rebuild(folded, j, eye)
    border = jnp.where(core == 0, half - 1, 0)
    border_ref[...] = table[:, pl.ds(pl.multiple_of(128 * border, 128), 128), :]

    def keep(k, _, value):
        out_ref[:, k * span : (k + 1) * span] = value

    add_far(core * (part_ref.shape[0] - count), count, core * half, table, part_ref, pert_ref, keep)


def far_rest_kernel(
    cols, count, part_ref, pert_ref, pair, pair_climb, pair_descend, begun, border_ref, out_hbm, table, staged, sems
):
    half, span = cols // 2, SPACING // 2
    core = lax.rem(lax.axis_index("lev"), 2)
    first = core == 0
    total = part_ref.shape[0]
    early = total - count
    start = core * (total - early) * span
    copies = [pltpu.make_async_copy(begun, out_hbm.at[:, pl.ds(start, early * span)], sems.at[count])]
    copies[0].start()
    eye = identity(128)
    for z, folded in enumerate(neighbours(pair_climb, pair_descend, pair, jnp.logical_not(first))):
        for j in range(half):
            at = pl.multiple_of(128 * j + jnp.where(first, 128, 0), 128)
            table[z, pl.ds(at, 128), :] = rebuild(folded, j, eye)
    at = pl.multiple_of(jnp.where(first, 0, 128 * half), 128)
    table[:, pl.ds(at, 128), :] = border_ref[...]

    def keep(k, patch_x, value):
        inside = pl.ds(patch_x * span, span)
        staged[:, inside] = value
        copies.append(pltpu.make_async_copy(staged.at[:, inside], out_hbm.at[:, inside], sems.at[k]))
        copies[-1].start()

    first_column = jnp.where(first, half - 1, 0)
    add_far((1 - core) * early, count, first_column, table, part_ref, pert_ref, keep)
    for copy in copies:
        copy.wait()


def paired_device(
    members, obs_pert, innovation, obs_precision, obs_owner, obs_slot, obs_count, local_weight
):
    axes = ("tx", "ty", "lev")
    ways = pair_patterns(axes)

    def send(value, way):
        return lax.ppermute(value, axes, ways[way])

    bf16, f32 = jnp.bfloat16, jnp.float32
    rows, size = obs_pert.shape
    cols = obs_owner.shape[0] + 2
    half = cols // 2
    shape = jax.ShapeDtypeStruct
    counts = obs_count.reshape(1, -1)
    lists = (obs_owner, obs_slot, counts, local_weight)
    scalars = [v.reshape(rows // size, size) for v in (innovation, obs_precision)]
    packed = device_call(
        functools.partial(pack_kernel, rows),
        tuple(pltpu.with_memory_space_constraint(v, pltpu.HBM) for v in (obs_pert, *scalars, *lists)),
        shape((rows + 16, size), bf16),
        [pltpu.VMEM(v.shape, v.dtype) for v in scalars]
        + [
            pltpu.VMEM(obs_owner.shape, jnp.int32),
            pltpu.VMEM(obs_slot.shape, jnp.int32),
            pltpu.SMEM(counts.shape, jnp.int32),
            pltpu.VMEM(local_weight.shape, f32),
            pltpu.VMEM((16, size), f32),
            pltpu.SemaphoreType.DMA((7,)),
        ],
        in_hbm=True,
    )
    across = send(packed, "across")
    climb, descend = send(packed, "climb"), send(packed, "descend")
    across_climb, across_descend = send(across, "climb"), send(across, "descend")
    table = device_call(
        functools.partial(table_kernel, rows, cols),
        (*lists, across),
        shape((136, 128), f32),
        flops=6 * 2 * 48 * 256 * 128,
    )
    tall = size * cols + 16
    near = device_call(
        functools.partial(gram_near_kernel, rows, cols),
        (table, packed, climb, descend, across),
        shape((tall, size), f32),
        [
            pltpu.VMEM((size, 4 * rows), f32),
            pltpu.VMEM((4 * rows, size), bf16),
            pltpu.VMEM((tall, 4 * rows), bf16),
        ],
        flops=2 * tall * size * 4 * rows,
    )
    rest = device_call(
        functools.partial(rest_kernel, rows, cols, 4),
        (table, near, across_climb, across_descend),
        shape((size * half + 16, size), bf16),
        flops=2 * tall * size * rows,
    )
    mine = device_call(
        functools.partial(mine_kernel, rows, cols, 4),
        (table, near, across_climb, across_descend),
        shape((size * half + 8, size), f32),
        flops=2 * tall * size * rows,
    )
    total, half_sum = device_call(
        functools.partial(join_kernel, half),
        (mine, send(rest, "core")),
        [shape((size * half + 8, size), f32), shape((272, size), bf16)],
    )
    weights = device_call(
        functools.partial(solve_kernel, half),
        (total, send(half_sum, "half")),
        shape((272, size), bf16),
        flops=2 * 27 * half * size**3,
    )
    pair = send(weights, "core")
    up = send(weights, "climb")
    down = send(weights, "descend")
    levels, width_x, width_y, _ = members.shape
    patches = (width_x * 2 // SPACING, 2, levels * SPACING**2 // 4, size)
    part, pert = device_call(
        functools.partial(near_kernel, cols),
        (members, weights, pair),
        [shape(patches, f32), shape(patches, bf16)],
        [pltpu.VMEM((cols * size, size), bf16)],
        flops=2 * levels * width_x * width_y * size * 2 * size,
    )
    up, down, part = lax.optimization_barrier((up, down, part))
    pair_up, pair_down = send(up, "core"), send(down, "core")
    early, span = cols // 2, SPACING // 2
    begun, border = device_call(
        functools.partial(far_first_kernel, cols, early),
        (part, pert, weights, up, down),
        [shape((levels, early * span, width_y, size), bf16), shape((2, size, size), bf16)],
        [pltpu.VMEM((2, half * size, size), bf16)],
        flops=2 * levels * span * early * width_y * size * 2 * size,
    )
    count = patches[0] - early
    return device_call(
        functools.partial(far_rest_kernel, cols, count),
        (part, pert, pair, pair_up, pair_down, begun, border),
        shape(members.shape, bf16),
        [
            pltpu.VMEM((2, (half + 1) * size, size), bf16),
            pltpu.VMEM(members.shape, bf16),
            pltpu.SemaphoreType.DMA((count + 1,)),
        ],
        flops=2 * levels * span * count * width_y * size * 2 * size,
        out_hbm=True,
    )


def fits_pairs(mesh, members, obs_pert, obs_owner):
    sizes = dict(mesh.shape)
    coarse_x, coarse_y, slots = obs_owner
    _, width_x, width_y, size = members
    return (
        sizes["tx"] == 2
        and sizes["lev"] == 4
        and (coarse_x + 2, coarse_y) == (6, 1)
        and (width_x, width_y) == (coarse_x * SPACING, coarse_y * SPACING)
        and size == LANES
        and obs_pert == (2 * LANES, LANES)
        and slots == 2 * LANES
    )


def solution(mesh):
    placed = (
        P("lev", "tx", "ty", None),
        P(("tx", "ty", "lev"), None),
        P(("tx", "ty", "lev")),
        P(("tx", "ty", "lev")),
        P("tx", "ty", None),
        P("tx", "ty", None),
        P("tx", "ty"),
        P("tx", "ty", None),
    )

    def local(members, obs_pert, innovation, obs_precision, obs_owner, *rest):
        paired = fits_pairs(mesh, members.shape, obs_pert.shape, obs_owner.shape)
        return (paired_device if paired else per_device)(
            members, obs_pert, innovation, obs_precision, obs_owner, *rest
        )

    return jax.shard_map(
        local,
        mesh=mesh,
        in_specs=placed,
        out_specs=P("lev", "tx", "ty", None),
        check_vma=False,
    )
```
